32 devices in a mesh: dp: 8 (over z, x), ctx: 4 (over y, core).
Axes of the slice: x: 2, y: 2, z: 4, core: 2. Of those that a mesh axis runs over, the one named last changes fastest.
Arguments:
- hidden_in: bfloat16 [8, 1024, 8192], P('dp', 'ctx'), may hold values from -6 to 6
- queries: bfloat16 [8, 1024, 4096], P('dp', 'ctx'), may hold values from -128 to 128
- key_projection_weight: bfloat16 [8192, 512], P('dp'), may hold values from -0.0625 to 0.0625
- value_projection_weight: bfloat16 [8192, 512], P('dp'), may hold values from -0.0625 to 0.0625
- key_projection_bias: float32 [512], replicated, may hold values from -2.5 to 2.5
- value_projection_bias: float32 [512], replicated, may hold values from -3 to 3
- block_segments: int32 [8, 8], P('dp'), may hold values from 0 to 4, never falling along the last dimension, each value on 1 to 3 neighbouring positions
Outputs:
- attended: bfloat16 [8, 1024, 4096], P('dp', 'ctx')
The draws below stay inside these ranges and needn't reach their ends.
Inputs may be any that keep to these rules, and one draw needn't show every extreme that they name: `block_segments`: each row starts with segment 0 and never falls; every one of the 5 segments spans 1 to 3 blocks.
All inputs are finite; a program needn't handle non-finite values.
Results may differ from the reference program's by a relative error of at most 0.0079.
Values may be sent and summed in bfloat16 or wider, within the bound.
No kernel may reach another device: no remote copies, remote signals or barrier semaphores. Data moves between devices by JAX's collectives and lax.ppermute only.
A program may use at most 128 MiB of HBM per device.

```python
import math
import jax
import jax.numpy as jnp
import numpy as np
from jax import lax

MODEL_WIDTH = 8192
HEAD_SIZE = 128
QUERY_HEADS = 32
KEY_VALUE_HEADS = 4
BLK = 128
SEGS = 5
PACK_LENGTH = 1024
NBLK = 8
MOST = 3
PACKS = 8


def key_bias_entries(key):
    random_subkey = jax.random.fold_in(key, 17)
    unscaled_sample = jax.random.normal(random_subkey, (KEY_VALUE_HEADS * HEAD_SIZE,), jnp.float32)
    return 0.5 * jnp.clip(unscaled_sample, -3.0, 3.0)


def draw_key_projection_bias(key, part):
    return key_bias_entries(key)


def draw_queries(key, part):
    base_key = jax.random.fold_in(key, 23)
    shape_all = (PACKS, PACK_LENGTH, QUERY_HEADS * HEAD_SIZE)
    return jnp.clip(jax.random.normal(base_key, shape_all, jnp.float32), -6.0, 6.0).astype(jnp.bfloat16)


def shard_levels(own_key, shape, split, least, high):
    level, own = 1.0, jax.random.fold_in(own_key, 6)
    for axis_at, shards_of in split:
        heights = jnp.exp(jax.random.uniform(jax.random.fold_in(own, axis_at), (shards_of,), jnp.float32, least / len(split), high / len(split)))
        level = level * jnp.repeat(heights, shape[axis_at] // shards_of).reshape([-1 if axis == axis_at else 1 for axis in range(len(shape))])
    return level


def profile(number_of, total, bound, slope):
    weights = [(1 << 20) // math.isqrt(rank ** slope) + 1 for rank in range(2, number_of + 1)]
    rest, holding = total - bound - (number_of - 1), [1] * (number_of - 1)
    while rest > 0:
        free = [i for i in range(number_of - 1) if holding[i] < bound]
        mass, left = sum([weights[i] for i in free]), rest
        for i in free:
            more = min(bound - holding[i], max(1, left * weights[i] // mass), rest)
            holding[i] = holding[i] + more
            rest = rest - more
    return np.array([bound] + holding)


def uneven_parts(stream_key, number_of, total, limit, skew):
    if number_of == 2:
        one = jax.random.randint(stream_key, (), max(1, total - limit), min(limit, total - 1) + 1)
        return jnp.stack([one, total - one])
    tallies = jnp.asarray(profile(number_of, total, limit, skew), jnp.int32)
    pairs = (number_of - 1) // 2
    source_of, receiver = tallies[1:1 + 2 * pairs:2], tallies[2:2 + 2 * pairs:2]
    margin = jnp.minimum(source_of - 1, limit - receiver)
    moved = jax.random.randint(jax.random.fold_in(stream_key, 1), (pairs,), 0, 1 << 20) % (margin + 1)
    tallies = tallies.at[1:1 + 2 * pairs:2].set(source_of - moved).at[2:2 + 2 * pairs:2].set(receiver + moved)
    return tallies[jax.random.permutation(jax.random.fold_in(stream_key, 2), number_of)]


def bell_draw(rng, extent, scale, limit, split=(), held_as=jnp.bfloat16):
    drawn = scale * jax.random.normal(rng, extent, jnp.float32)
    if split:
        drawn = drawn * shard_levels(rng, extent, split, -0.22, 0.18)
    return jnp.clip(drawn, -limit, limit).astype(held_as)


def setup_inputs(seed: int = 0) -> dict:
    splits = jax.random.split(jax.random.key(seed), 8)
    hidden_in = bell_draw(splits[0], (PACKS, PACK_LENGTH, MODEL_WIDTH), 1.0, 6.0, ((0, 8), (1, 4)))
    queries = draw_queries(jax.random.fold_in(splits[7], 71), 0)
    key_projection_weight = bell_draw(splits[2], (MODEL_WIDTH, KEY_VALUE_HEADS * HEAD_SIZE), MODEL_WIDTH ** -0.5, 0.0625, ((0, 8),))
    value_projection_weight = bell_draw(splits[3], (MODEL_WIDTH, KEY_VALUE_HEADS * HEAD_SIZE), MODEL_WIDTH ** -0.5, 0.0625, ((0, 8),))
    key_projection_bias = draw_key_projection_bias(jax.random.fold_in(splits[7], 71), 0)
    value_projection_bias = bell_draw(splits[5], (KEY_VALUE_HEADS * HEAD_SIZE,), 0.5, 3.0, (), jnp.float32)
    block_segments = jax.vmap(lambda own: jnp.searchsorted(jnp.cumsum(uneven_parts(own, SEGS, NBLK, MOST, 0)), jnp.arange(NBLK), side="right"))(jax.random.split(splits[6], PACKS)).reshape((PACKS, NBLK)).astype(jnp.int32)
    return dict(hidden_in=hidden_in, queries=queries, key_projection_weight=key_projection_weight, value_projection_weight=value_projection_weight, key_projection_bias=key_projection_bias, value_projection_bias=value_projection_bias, block_segments=block_segments)


rope_base = 1000000.0

def rotary_rotate(head_vecs, token_positions):
    half_dim = head_vecs.shape[-1] // 2
    frequency = rope_base ** (-(jnp.arange(half_dim, dtype=jnp.float32) * 2.0 / head_vecs.shape[-1]))
    angles = token_positions.astype(jnp.float32)[:, None] * frequency[None, :]
    cos_part = jnp.cos(angles)[:, None, :]
    sine_part = jnp.sin(angles)[:, None, :]
    first_half = head_vecs[..., :half_dim]
    second_half = head_vecs[..., half_dim:]
    return jnp.concatenate([first_half * cos_part - second_half * sine_part, second_half * cos_part + first_half * sine_part], axis=-1)

def reference(hidden_in, queries, key_projection_weight, value_projection_weight, key_projection_bias, value_projection_bias, block_segments):
    group_width = QUERY_HEADS // KEY_VALUE_HEADS
    rows_per_block = math.gcd(PACK_LENGTH, 512)
    block_count = PACK_LENGTH // rows_per_block
    token_positions = jnp.arange(PACK_LENGTH, dtype=jnp.int32)
    score_scale = 1.0 / math.sqrt(HEAD_SIZE)

    def one_pack(packed):
        pack_tokens, packed_query_rows, pack_segs = packed
        key_projected_rows = jnp.dot(pack_tokens, key_projection_weight, preferred_element_type=jnp.float32) + key_projection_bias
        key_row_values = rotary_rotate(key_projected_rows.reshape(PACK_LENGTH, KEY_VALUE_HEADS, HEAD_SIZE), token_positions)
        key_row_values = lax.optimization_barrier(key_row_values.astype(jnp.bfloat16)).astype(jnp.float32)
        value_proj = jnp.dot(pack_tokens, value_projection_weight, preferred_element_type=jnp.float32) + value_projection_bias
        value_row_values = lax.optimization_barrier(value_proj.astype(jnp.bfloat16)).astype(jnp.float32)
        value_row_values = value_row_values.reshape(PACK_LENGTH, KEY_VALUE_HEADS, HEAD_SIZE)
        segment_tokens = jnp.repeat(pack_segs, BLK)

        def single_block(blocked):
            block_queries, block_pos, block_seg = blocked
            scores = jnp.einsum('tkgd,skd->tkgs', block_queries.astype(jnp.float32), key_row_values) * score_scale
            allowed = (token_positions[None, :] <= block_pos[:, None]) & ((segment_tokens[None, :] == block_seg[:, None]) | (segment_tokens[None, :] == 0))
            scores = jnp.where(allowed[:, None, None, :], scores, -jnp.inf)
            row_peak = lax.optimization_barrier(jnp.max(scores, axis=-1, keepdims=True))
            probs = jnp.exp(scores - row_peak)
            row_total = lax.optimization_barrier(jnp.sum(probs, axis=-1))
            rounded = lax.optimization_barrier(probs.astype(jnp.bfloat16)).astype(jnp.float32)
            mixed = jnp.einsum('tkgs,skd->tkgd', rounded, value_row_values) / row_total[..., None]
            return mixed.astype(jnp.bfloat16).reshape(rows_per_block, QUERY_HEADS * HEAD_SIZE)
        output_rows = lax.map(single_block, (packed_query_rows.reshape(block_count, rows_per_block, KEY_VALUE_HEADS, group_width, HEAD_SIZE), token_positions.reshape(block_count, rows_per_block), segment_tokens.reshape(block_count, rows_per_block)))
        return output_rows.reshape(PACK_LENGTH, QUERY_HEADS * HEAD_SIZE)
    return lax.map(one_pack, (hidden_in, queries, block_segments))
```

```python
import functools
import math

import jax
import jax.numpy as jnp
from jax import lax
from jax.experimental import pallas as pl
from jax.experimental.pallas import tpu as pltpu
from jax.sharding import PartitionSpec as P

HEAD_SIZE = 128
KEY_VALUE_HEADS = 4
BLK = 128
MASKED = -1e30
CORES = 2

rope_base = 1000000.0


def ring_order(count):
    return list(range(0, count, 2)) + list(range(count - 1, 0, -2))


def rope_tables(token_positions):
    half_dim = HEAD_SIZE // 2
    frequency = rope_base ** (
        -(jnp.arange(half_dim, dtype=jnp.float32) * 2.0 / HEAD_SIZE)
    )
    angles = token_positions.astype(jnp.float32)[:, None] * frequency[None, :]
    return jnp.cos(angles)[:, None, :], jnp.sin(angles)[:, None, :]


def rotary_rotate(head_vecs, tables):
    cos_part, sine_part = tables
    half_dim = HEAD_SIZE // 2
    first_half = head_vecs[..., :half_dim]
    second_half = head_vecs[..., half_dim:]
    return jnp.concatenate(
        [
            first_half * cos_part - second_half * sine_part,
            second_half * cos_part + first_half * sine_part,
        ],
        axis=-1,
    )


def attention_kernel(hops, row_blocks, group, facts, *refs):
    q_ref = refs[0]
    k_refs = refs[1 : 1 + hops]
    v_refs = refs[1 + hops : 1 + 2 * hops]
    out_ref, score_ref, peak_ref, total_ref, acc_ref = refs[-5:]
    chip_blocks = CORES * row_blocks
    row_block = pl.program_id(1)
    source_core, ctx_index = facts[1], facts[2]
    chip = ctx_index // CORES
    here = ctx_index * row_blocks + row_block
    segment = facts[3 + here]
    factor = math.log2(math.e) / math.sqrt(HEAD_SIZE)
    rows = group * BLK

    def place(local):
        core = local // row_blocks
        slot = jnp.where(core == source_core, 0, row_blocks) + local % row_blocks
        return pl.ds(pl.multiple_of(slot * BLK, BLK), BLK)

    def queries():
        return jnp.concatenate(
            [q_ref[:, h * HEAD_SIZE : (h + 1) * HEAD_SIZE] for h in range(group)], axis=0
        )

    def scores(k_ref, local):
        return lax.dot_general(
            queries(),
            k_ref[place(local), :],
            (((1,), (1,)), ((), ())),
            preferred_element_type=jnp.float32,
        )

    def over_blocks(visit):
        for hop in range(hops):

            @pl.loop(0, chip_blocks)
            def _(local):
                block = (chip - hop) * chip_blocks + local
                seen = facts[3 + jnp.maximum(block, 0)]

                @pl.when(
                    (block >= 0) & (block < here) & ((seen == 0) | (seen == segment))
                )
                def _():
                    visit(hop, local)

    diagonal = lax.rem(here, chip_blocks)
    later = lax.broadcasted_iota(jnp.int32, (rows, BLK), 1) > (
        lax.broadcasted_iota(jnp.int32, (rows, BLK), 0) % BLK
    )
    own = jnp.where(later, MASKED, scores(k_refs[0], diagonal))
    score_ref[diagonal] = own
    peak_ref[...] = own

    def first(hop, local):
        found = scores(k_refs[hop], local)
        score_ref[hop * chip_blocks + local] = found
        peak_ref[...] = jnp.maximum(peak_ref[...], found)

    over_blocks(first)
    peak = jnp.max(peak_ref[...], axis=1, keepdims=True)
    peak_ref[...] = jnp.broadcast_to(peak, (rows, BLK))

    def weigh(hop, local):
        probs = jnp.exp2((score_ref[hop * chip_blocks + local] - peak_ref[...]) * factor)
        return probs, jnp.dot(
            probs.astype(jnp.bfloat16),
            v_refs[hop][place(local), :],
            preferred_element_type=jnp.float32,
        )

    total_ref[...], acc_ref[...] = weigh(0, diagonal)

    def second(hop, local):
        probs, mixed = weigh(hop, local)
        total_ref[...] += probs
        acc_ref[...] += mixed

    over_blocks(second)
    total = jnp.sum(total_ref[...], axis=1, keepdims=True)
    mixed = (acc_ref[...] / total).astype(out_ref.dtype)
    for h in range(group):
        out_ref[:, h * HEAD_SIZE : (h + 1) * HEAD_SIZE] = mixed[h * BLK : (h + 1) * BLK]


def attend(facts, queries, keys, values, before):
    hops = len(keys)
    number_of_rows, query_width = queries.shape
    group = query_width // HEAD_SIZE // KEY_VALUE_HEADS
    heads = KEY_VALUE_HEADS // CORES
    row_blocks = number_of_rows // BLK
    width = group * HEAD_SIZE
    rows = group * BLK
    q_spec = pl.BlockSpec((BLK, width), lambda l, r, f: (r, f[0] * heads + l))
    kv_spec = pl.BlockSpec((keys[0].shape[0], HEAD_SIZE), lambda l, r, f: (0, l))
    operands = [facts, queries, *keys, *values]
    in_specs = [q_spec] + [kv_spec] * (2 * hops)
    aliases = {}
    if before is not None:
        aliases = {len(operands): 0}
        operands.append(before)
        in_specs.append(pl.BlockSpec(memory_space=pl.ANY))
    total_blocks = hops * CORES * row_blocks
    pairs = heads * row_blocks * rows * total_blocks * BLK // 2
    return pl.pallas_call(
        functools.partial(attention_kernel, hops, row_blocks, group),
        out_shape=jax.ShapeDtypeStruct(queries.shape, queries.dtype),
        grid_spec=pltpu.PrefetchScalarGridSpec(
            num_scalar_prefetch=1,
            grid=(heads, row_blocks),
            in_specs=in_specs,
            out_specs=q_spec,
            scratch_shapes=[
                pltpu.VMEM((total_blocks, rows, BLK), jnp.float32),
                pltpu.VMEM((rows, BLK), jnp.float32),
                pltpu.VMEM((rows, BLK), jnp.float32),
                pltpu.VMEM((rows, HEAD_SIZE), jnp.float32),
            ],
        ),
        input_output_aliases=aliases,
        cost_estimate=pl.CostEstimate(
            flops=4 * pairs * HEAD_SIZE,
            bytes_accessed=2 * number_of_rows * query_width * 2,
            transcendentals=pairs,
        ),
        name="attend",
    )(*operands)


def body(
    hidden_in,
    queries,
    key_projection_weight,
    value_projection_weight,
    key_projection_bias,
    value_projection_bias,
    block_segments,
):
    own_tokens = hidden_in[0]
    number_of_rows = own_tokens.shape[0]
    depth, kv_width = key_projection_weight.shape
    dp_size, ctx_size = lax.axis_size("dp"), lax.axis_size("ctx")
    chips = ctx_size // CORES
    my_index = lax.axis_index("ctx")
    core, chip = my_index % CORES, my_index // CORES
    plane = chip % 2
    half_width = kv_width // CORES
    ring = ring_order(dp_size)
    dp_index = lax.axis_index("dp")
    spots = [0] * dp_size
    for spot, index in enumerate(ring):
        spots[index] = spot
    my_spot = jnp.asarray(spots, jnp.int32)[dp_index]
    ring_array = jnp.asarray(ring, jnp.int32)

    def to_sibling(x):
        return lax.ppermute(x, "ctx", [(i, i ^ 1) for i in range(ctx_size)])

    def to_plane(x):
        return lax.ppermute(x, "ctx", [(i, i ^ CORES) for i in range(ctx_size)])

    def to_next_chip(x):
        return lax.ppermute(x, "ctx", [(i, i + CORES) for i in range(ctx_size - CORES)])

    def along_ring(x, step):
        return lax.ppermute(
            x, "dp", [(ring[i], ring[(i + step) % dp_size]) for i in range(dp_size)]
        )

    key_weight = lax.dynamic_slice_in_dim(key_projection_weight, core * half_width, half_width, 1)
    value_weight = lax.dynamic_slice_in_dim(
        value_projection_weight, core * half_width, half_width, 1
    )
    strip = depth // 2
    key_strip = lax.dynamic_slice_in_dim(key_weight, plane * strip, strip, 0)

    tokens = jnp.concatenate([own_tokens, to_sibling(own_tokens)], axis=0)

    def product(piece, source, start):
        columns = lax.dynamic_slice_in_dim(tokens, source * depth + start, piece.shape[0], 1)
        return jnp.dot(columns, piece, preferred_element_type=jnp.float32)

    def source_at(distance):
        return ring_array[(my_spot + distance + dp_size) % dp_size]

    key_proj = product(key_weight, dp_index, 0)
    value_proj = product(value_weight, dp_index, 0)

    half_ring = dp_size // 2
    travelling = {1: key_strip, -1: key_strip}
    for hop in range(1, half_ring + 1):
        for step in (1, -1):
            piece, start, size = travelling[step], 0, strip
            if hop == half_ring:
                size = strip // 2
                start = 0 if step == 1 else size
                piece = piece[start : start + size]
            piece = along_ring(piece, step)
            travelling[step] = piece
            other = to_plane(piece)
            source = source_at(-step * hop)
            key_proj += product(piece, source, plane * strip + start)
            key_proj += product(other, source, (1 - plane) * strip + start)

    travelling = {1: value_weight, -1: value_weight}
    for hop in range(1, half_ring + 1):
        for step in (1, -1):
            piece, start = travelling[step], 0
            if hop == half_ring:
                start = 0 if step == 1 else strip
                piece = piece[start : start + strip]
            piece = along_ring(piece, step)
            travelling[step] = piece
            value_proj += product(piece, source_at(-step * hop), start)

    arange = jnp.arange(number_of_rows, dtype=jnp.int32)
    positions = jnp.concatenate(
        [my_index * number_of_rows + arange, (my_index ^ 1) * number_of_rows + arange]
    )
    heads = KEY_VALUE_HEADS // CORES
    chip_rows = CORES * number_of_rows
    key_bias = lax.dynamic_slice_in_dim(key_projection_bias, core * half_width, half_width, 0)
    value_bias = lax.dynamic_slice_in_dim(value_projection_bias, core * half_width, half_width, 0)
    key_rows = rotary_rotate(
        (key_proj + key_bias).reshape(chip_rows, heads, HEAD_SIZE), rope_tables(positions)
    )
    key_rows = key_rows.astype(jnp.bfloat16).reshape(chip_rows, half_width)
    value_rows = (value_proj + value_bias).astype(jnp.bfloat16)

    keys, values = [key_rows], [value_rows]
    for _ in range(chips - 1):
        keys.append(to_next_chip(keys[-1]))
        values.append(to_next_chip(values[-1]))
    sibling_keys = [to_sibling(x) for x in keys]
    sibling_values = [to_sibling(x) for x in values]

    def facts(half):
        return jnp.concatenate([jnp.stack([half, half, my_index]), block_segments[0]])

    own_queries = queries[0]
    attended = attend(facts(core), own_queries, keys, values, None)
    attended = attend(facts(1 - core), own_queries, sibling_keys, sibling_values, attended)
    return attended[None]


def solution(mesh):
    placed = (
        P("dp", "ctx", None),
        P("dp", "ctx", None),
        P("dp", None),
        P("dp", None),
        P(),
        P(),
        P("dp", None),
    )
    return jax.shard_map(
        body, mesh=mesh, in_specs=placed, out_specs=P("dp", "ctx", None), check_vma=False
    )
```

```python
import functools
import math

import jax
import jax.numpy as jnp
from jax import lax
from jax.experimental import pallas as pl
from jax.experimental.pallas import tpu as pltpu
from jax.sharding import PartitionSpec as P

HEAD_SIZE = 128
KEY_VALUE_HEADS = 4
BLK = 128
MASKED = -1e30
CORES = 2

rope_base = 1000000.0


def ring_order(count):
    return list(range(0, count, 2)) + list(range(count - 1, 0, -2))


def rope_tables(token_positions):
    half_dim = HEAD_SIZE // 2
    frequency = rope_base ** (
        -(jnp.arange(half_dim, dtype=jnp.float32) * 2.0 / HEAD_SIZE)
    )
    angles = token_positions.astype(jnp.float32)[:, None] * frequency[None, :]
    cos_part, sine_part = jnp.cos(angles), jnp.sin(angles)
    return (
        jnp.concatenate([cos_part, cos_part], axis=1),
        jnp.concatenate([-sine_part, sine_part], axis=1),
    )


def project_kernel(plan, finish, block_index, *refs):
    operands = 1 + max(part[0] for parts in plan for part in parts)
    own_ref, sibling_ref = refs[:2]
    piece_refs = refs[2 : 2 + operands]
    extra_refs = refs[2 + operands : -4]
    out_ref, weight_ref, acc_ref, sems = refs[-4:]
    step = pl.program_id(0)
    number_of_rows = own_ref.shape[0]
    part_rows = weight_ref.shape[1] // 2

    def part_copy(operand, first_row, at, part):
        return pltpu.make_async_copy(
            piece_refs[operand].at[pl.ds(first_row, part_rows), :],
            weight_ref.at[at, pl.ds(part * part_rows, part_rows), :],
            sems.at[at, part],
        )

    @pl.when(step == 0)
    def _():
        for at, parts in enumerate(plan):
            for part, (operand, first_row) in enumerate(parts):
                part_copy(operand, first_row, at, part).start()
        if finish == "add_value":
            acc_ref[...] = extra_refs[0][...]
        else:
            acc_ref[...] = jnp.zeros_like(acc_ref)

    for part in range(2):
        part_copy(0, 0, step, part).wait()
    for half, tokens_ref in enumerate((own_ref, sibling_ref)):
        acc_ref[half * number_of_rows : (half + 1) * number_of_rows, :] += jnp.dot(
            tokens_ref[...], weight_ref[step], preferred_element_type=jnp.float32
        )

    @pl.when(step == len(plan) - 1)
    def _():
        if finish == "sum":
            out_ref[...] = acc_ref[...]
        elif finish == "add_value":
            out_ref[...] = (acc_ref[...] + extra_refs[1][...]).astype(out_ref.dtype)
        else:
            bias_ref, cos_ref, sine_ref = extra_refs
            for first in range(0, acc_ref.shape[1], HEAD_SIZE):
                lanes = slice(first, first + HEAD_SIZE)
                head = acc_ref[:, lanes] + bias_ref[:, lanes]
                turned = head * cos_ref[...] + pltpu.roll(head, HEAD_SIZE // 2, 1) * sine_ref[...]
                out_ref[:, lanes] = turned.astype(out_ref.dtype)


def project(finish, own_tokens, sibling_tokens, pieces, plan, block_index, extras):
    number_of_rows = own_tokens.shape[0]
    width = pieces[0].shape[1]
    strip = own_tokens.shape[1] // block_index[1]
    token_spec = pl.BlockSpec((number_of_rows, strip), lambda p, b: (0, b[p]))
    whole = [pl.BlockSpec(x.shape, lambda p, b: (0, 0)) for x in extras]
    out = jax.ShapeDtypeStruct(
        (CORES * number_of_rows, width), jnp.float32 if finish == "sum" else jnp.bfloat16
    )
    return pl.pallas_call(
        functools.partial(project_kernel, plan, finish),
        out_shape=out,
        grid_spec=pltpu.PrefetchScalarGridSpec(
            num_scalar_prefetch=1,
            grid=(len(plan),),
            in_specs=[token_spec, token_spec]
            + [pl.BlockSpec(memory_space=pl.ANY)] * len(pieces)
            + whole,
            out_specs=pl.BlockSpec(out.shape, lambda p, b: (0, 0)),
            scratch_shapes=[
                pltpu.VMEM((len(plan), strip, width), jnp.bfloat16),
                pltpu.VMEM((CORES * number_of_rows, width), jnp.float32),
                pltpu.SemaphoreType.DMA((len(plan), 2)),
            ],
        ),
        cost_estimate=pl.CostEstimate(
            flops=2 * len(plan) * strip * CORES * number_of_rows * width,
            bytes_accessed=2 * len(plan) * strip * (CORES * number_of_rows + width),
            transcendentals=0,
        ),
        name="project_" + finish,
    )(block_index[0], own_tokens, sibling_tokens, *pieces, *extras)


def attention_kernel(hops, row_blocks, group, facts, *refs):
    q_ref = refs[0]
    k_refs = refs[1 : 1 + hops]
    v_refs = refs[1 + hops : 1 + 2 * hops]
    out_ref, score_ref, peak_ref, total_ref, acc_ref = refs[-5:]
    chip_blocks = CORES * row_blocks
    row_block = pl.program_id(1)
    source_core, ctx_index = facts[1], facts[2]
    chip = ctx_index // CORES
    here = ctx_index * row_blocks + row_block
    segment = facts[3 + here]
    factor = math.log2(math.e) / math.sqrt(HEAD_SIZE)
    rows = group * BLK

    def place(local):
        core = local // row_blocks
        slot = jnp.where(core == source_core, 0, row_blocks) + local % row_blocks
        return pl.ds(pl.multiple_of(slot * BLK, BLK), BLK)

    def queries():
        return jnp.concatenate(
            [q_ref[:, h * HEAD_SIZE : (h + 1) * HEAD_SIZE] for h in range(group)], axis=0
        )

    def scores(k_ref, local):
        return lax.dot_general(
            queries(),
            k_ref[place(local), :],
            (((1,), (1,)), ((), ())),
            preferred_element_type=jnp.float32,
        )

    def over_blocks(visit):
        for hop in range(hops):

            @pl.loop(0, chip_blocks)
            def _(local):
                block = (chip - hop) * chip_blocks + local
                seen = facts[3 + jnp.maximum(block, 0)]

                @pl.when(
                    (block >= 0) & (block < here) & ((seen == 0) | (seen == segment))
                )
                def _():
                    visit(hop, local)

    diagonal = lax.rem(here, chip_blocks)
    later = lax.broadcasted_iota(jnp.int32, (rows, BLK), 1) > (
        lax.broadcasted_iota(jnp.int32, (rows, BLK), 0) % BLK
    )
    own = jnp.where(later, MASKED, scores(k_refs[0], diagonal))
    score_ref[diagonal] = own
    peak_ref[...] = own

    def first(hop, local):
        found = scores(k_refs[hop], local)
        score_ref[hop * chip_blocks + local] = found
        peak_ref[...] = jnp.maximum(peak_ref[...], found)

    over_blocks(first)
    peak = jnp.max(peak_ref[...], axis=1, keepdims=True)
    peak_ref[...] = jnp.broadcast_to(peak, (rows, BLK))

    def weigh(hop, local):
        probs = jnp.exp2((score_ref[hop * chip_blocks + local] - peak_ref[...]) * factor)
        return probs, jnp.dot(
            probs.astype(jnp.bfloat16),
            v_refs[hop][place(local), :],
            preferred_element_type=jnp.float32,
        )

    total_ref[...], acc_ref[...] = weigh(0, diagonal)

    def second(hop, local):
        probs, mixed = weigh(hop, local)
        total_ref[...] += probs
        acc_ref[...] += mixed

    over_blocks(second)
    total = jnp.sum(total_ref[...], axis=1, keepdims=True)
    mixed = (acc_ref[...] / total).astype(out_ref.dtype)
    for h in range(group):
        out_ref[:, h * HEAD_SIZE : (h + 1) * HEAD_SIZE] = mixed[h * BLK : (h + 1) * BLK]


def attend(facts, queries, keys, values, before):
    hops = len(keys)
    number_of_rows, query_width = queries.shape
    group = query_width // HEAD_SIZE // KEY_VALUE_HEADS
    heads = KEY_VALUE_HEADS // CORES
    row_blocks = number_of_rows // BLK
    width = group * HEAD_SIZE
    rows = group * BLK
    q_spec = pl.BlockSpec((BLK, width), lambda l, r, f: (r, f[0] * heads + l))
    kv_spec = pl.BlockSpec((keys[0].shape[0], HEAD_SIZE), lambda l, r, f: (0, l))
    operands = [facts, queries, *keys, *values]
    in_specs = [q_spec] + [kv_spec] * (2 * hops)
    aliases = {}
    if before is not None:
        aliases = {len(operands): 0}
        operands.append(before)
        in_specs.append(pl.BlockSpec(memory_space=pl.ANY))
    total_blocks = hops * CORES * row_blocks
    pairs = heads * row_blocks * rows * total_blocks * BLK // 2
    return pl.pallas_call(
        functools.partial(attention_kernel, hops, row_blocks, group),
        out_shape=jax.ShapeDtypeStruct(queries.shape, queries.dtype),
        grid_spec=pltpu.PrefetchScalarGridSpec(
            num_scalar_prefetch=1,
            grid=(heads, row_blocks),
            in_specs=in_specs,
            out_specs=q_spec,
            scratch_shapes=[
                pltpu.VMEM((total_blocks, rows, BLK), jnp.float32),
                pltpu.VMEM((rows, BLK), jnp.float32),
                pltpu.VMEM((rows, BLK), jnp.float32),
                pltpu.VMEM((rows, HEAD_SIZE), jnp.float32),
            ],
        ),
        input_output_aliases=aliases,
        cost_estimate=pl.CostEstimate(
            flops=4 * pairs * HEAD_SIZE,
            bytes_accessed=2 * number_of_rows * query_width * 2,
            transcendentals=pairs,
        ),
        name="attend",
    )(*operands)


def body(
    hidden_in,
    queries,
    key_projection_weight,
    value_projection_weight,
    key_projection_bias,
    value_projection_bias,
    block_segments,
):
    own_tokens = hidden_in[0]
    number_of_rows = own_tokens.shape[0]
    depth, kv_width = key_projection_weight.shape
    dp_size, ctx_size = lax.axis_size("dp"), lax.axis_size("ctx")
    chips = ctx_size // CORES
    my_index = lax.axis_index("ctx")
    core, chip = my_index % CORES, my_index // CORES
    plane = chip % 2
    half_width = kv_width // CORES
    ring = ring_order(dp_size)
    dp_index = lax.axis_index("dp")
    spots = [0] * dp_size
    for spot, index in enumerate(ring):
        spots[index] = spot
    my_spot = jnp.asarray(spots, jnp.int32)[dp_index]
    ring_array = jnp.asarray(ring, jnp.int32)

    def to_sibling(x):
        return lax.ppermute(x, "ctx", [(i, i ^ 1) for i in range(ctx_size)])

    def to_plane(x):
        return lax.ppermute(x, "ctx", [(i, i ^ CORES) for i in range(ctx_size)])

    def to_next_chip(x):
        return lax.ppermute(x, "ctx", [(i, i + CORES) for i in range(ctx_size - CORES)])

    def along_ring(x, step):
        return lax.ppermute(
            x, "dp", [(ring[i], ring[(i + step) % dp_size]) for i in range(dp_size)]
        )

    key_weight = lax.dynamic_slice_in_dim(key_projection_weight, core * half_width, half_width, 1)
    value_weight = lax.dynamic_slice_in_dim(
        value_projection_weight, core * half_width, half_width, 1
    )
    strip = depth // 2
    part = strip // 2
    key_strip = lax.dynamic_slice_in_dim(key_weight, plane * strip, strip, 0)
    sibling_tokens = to_sibling(own_tokens)

    def source_at(distance):
        return ring_array[(my_spot + distance + dp_size) % dp_size]

    half_ring = dp_size // 2
    strips_in_all = dp_size * 2

    key_pieces, key_plan, key_blocks = [key_weight], [], []
    for side in range(2):
        key_plan.append(((0, side * strip), (0, side * strip + part)))
        key_blocks.append(dp_index * 2 + side)
    travelling = {1: key_strip, -1: key_strip}
    last = []
    for hop in range(1, half_ring + 1):
        for step in (1, -1):
            piece = travelling[step]
            if hop == half_ring:
                first_row = 0 if step == 1 else part
                piece = piece[first_row : first_row + part]
            piece = along_ring(piece, step)
            travelling[step] = piece
            last.append((len(key_pieces), len(key_pieces) + 1))
            key_pieces += [piece, to_plane(piece)]
            if hop < half_ring:
                for side, at in enumerate(last[-1]):
                    key_plan.append(((at, 0), (at, part)))
                    key_blocks.append(
                        source_at(-step * hop) * 2 + (plane if side == 0 else 1 - plane)
                    )
    for side in range(2):
        key_plan.append(((last[-2][side], 0), (last[-1][side], 0)))
        key_blocks.append(source_at(half_ring) * 2 + (plane if side == 0 else 1 - plane))

    value_pieces, value_plan, value_blocks = [value_weight], [], []
    for side in range(2):
        value_plan.append(((0, side * strip), (0, side * strip + part)))
        value_blocks.append(dp_index * 2 + side)
    travelling = {1: value_weight, -1: value_weight}
    for hop in range(1, half_ring):
        for step in (1, -1):
            piece = along_ring(travelling[step], step)
            travelling[step] = piece
            at = len(value_pieces)
            value_pieces.append(piece)
            for side in range(2):
                value_plan.append(((at, side * strip), (at, side * strip + part)))
                value_blocks.append(source_at(-step * hop) * 2 + side)
    end_pieces = [
        along_ring(travelling[1][:strip], 1),
        along_ring(travelling[-1][strip:], -1),
    ]
    end_plan = [((side, 0), (side, part)) for side in range(2)]
    end_blocks = [source_at(half_ring) * 2 + side for side in range(2)]

    arange = jnp.arange(number_of_rows, dtype=jnp.int32)
    positions = jnp.concatenate(
        [my_index * number_of_rows + arange, (my_index ^ 1) * number_of_rows + arange]
    )
    key_bias = lax.dynamic_slice_in_dim(key_projection_bias, core * half_width, half_width, 0)
    value_bias = lax.dynamic_slice_in_dim(value_projection_bias, core * half_width, half_width, 0)

    def projected(finish, pieces, plan, blocks, extras):
        return project(
            finish,
            own_tokens,
            sibling_tokens,
            pieces,
            tuple(plan),
            (jnp.stack(blocks).astype(jnp.int32), strips_in_all),
            extras,
        )

    key_rows = projected(
        "key", key_pieces, key_plan, key_blocks, [key_bias[None], *rope_tables(positions)]
    )
    value_sum = projected("sum", value_pieces, value_plan, value_blocks, [])
    value_rows = projected(
        "add_value", end_pieces, end_plan, end_blocks, [value_sum, value_bias[None]]
    )

    keys, values = [key_rows], [value_rows]
    for _ in range(chips - 1):
        keys.append(to_next_chip(keys[-1]))
        values.append(to_next_chip(values[-1]))
    sibling_keys = [to_sibling(x) for x in keys]
    sibling_values = [to_sibling(x) for x in values]

    def facts(half):
        return jnp.concatenate([jnp.stack([half, half, my_index]), block_segments[0]])

    own_queries = queries[0]
    attended = attend(facts(core), own_queries, keys, values, None)
    attended = attend(facts(1 - core), own_queries, sibling_keys, sibling_values, attended)
    return attended[None]


def solution(mesh):
    placed = (
        P("dp", "ctx", None),
        P("dp", "ctx", None),
        P("dp", None),
        P("dp", None),
        P(),
        P(),
        P("dp", None),
    )
    return jax.shard_map(
        body, mesh=mesh, in_specs=placed, out_specs=P("dp", "ctx", None), check_vma=False
    )
```

```python
import functools
import math

import jax
import jax.numpy as jnp
from jax import lax
from jax.experimental import pallas as pl
from jax.experimental.pallas import tpu as pltpu
from jax.sharding import PartitionSpec as P


HEAD_SIZE = 128
KEY_VALUE_HEADS = 4
BLK = 128
MASKED = -1e30
CORES = 2

rope_base = 1000000.0


def ring_order(count):
    return list(range(0, count, 2)) + list(range(count - 1, 0, -2))


def rope_tables(token_positions):
    half_dim = HEAD_SIZE // 2
    frequency = rope_base ** (
        -(jnp.arange(half_dim, dtype=jnp.float32) * 2.0 / HEAD_SIZE)
    )
    angles = token_positions.astype(jnp.float32)[:, None] * frequency[None, :]
    cos_part, sine_part = jnp.cos(angles), jnp.sin(angles)
    return (
        jnp.concatenate([cos_part, cos_part], axis=1),
        jnp.concatenate([-sine_part, sine_part], axis=1),
    )


def project_kernel(plan, finish, columns, own_ref, sibling_ref, *refs):
    operands = 1 + max(part[0] for parts in plan for part in parts)
    piece_refs = refs[:operands]
    extra_refs = refs[operands:-6]
    out_ref, token_ref, weight_ref, acc_ref, token_sems, weight_sems = refs[-6:]
    number_of_rows, strip = own_ref.shape[0], weight_ref.shape[1]
    part_rows = strip // 2

    def token_copy(at, half):
        tokens_ref = (own_ref, sibling_ref)[half]
        return pltpu.make_async_copy(
            tokens_ref.at[:, pl.ds(pl.multiple_of(columns[at] * strip, strip), strip)],
            token_ref.at[at, pl.ds(half * number_of_rows, number_of_rows), :],
            token_sems.at[at, half],
        )

    def part_copy(operand, first_row, at, part):
        return pltpu.make_async_copy(
            piece_refs[operand].at[pl.ds(first_row, part_rows), :],
            weight_ref.at[at, pl.ds(part * part_rows, part_rows), :],
            weight_sems.at[at, part],
        )

    for at, parts in enumerate(plan):
        for part, (operand, first_row) in enumerate(parts):
            part_copy(operand, first_row, at, part).start()
        for half in range(2):
            token_copy(at, half).start()
    if finish == "add":
        acc_ref[...] = extra_refs[0][...]
    else:
        acc_ref[...] = jnp.zeros_like(acc_ref)

    @pl.loop(0, len(plan) // 2)
    def _(pair):
        for at in (2 * pair, 2 * pair + 1):
            for half in range(2):
                part_copy(0, 0, at, half).wait()
                token_copy(at, half).wait()
        acc_ref[...] += jnp.dot(
            token_ref[2 * pair], weight_ref[2 * pair], preferred_element_type=jnp.float32
        ) + jnp.dot(
            token_ref[2 * pair + 1], weight_ref[2 * pair + 1], preferred_element_type=jnp.float32
        )

    if finish == "key":
        bias_ref, cos_ref, sine_ref = extra_refs
        for first in range(0, acc_ref.shape[1], HEAD_SIZE):
            lanes = slice(first, first + HEAD_SIZE)
            head = acc_ref[:, lanes] + bias_ref[:, lanes]
            turned = head * cos_ref[...] + pltpu.roll(head, HEAD_SIZE // 2, 1) * sine_ref[...]
            out_ref[:, lanes] = turned.astype(out_ref.dtype)
    elif finish == "sum":
        out_ref[...] = acc_ref[...] + extra_refs[0][...]
    else:
        out_ref[...] = acc_ref[...].astype(out_ref.dtype)


def project(finish, strip, own_tokens, sibling_tokens, pieces, plan, columns, extras):
    number_of_rows = own_tokens.shape[0]
    width = pieces[0].shape[1]
    anywhere = pl.BlockSpec(memory_space=pl.ANY)
    chip_rows = CORES * number_of_rows
    out = jax.ShapeDtypeStruct(
        (chip_rows, width), jnp.float32 if finish == "sum" else jnp.bfloat16
    )
    return pl.pallas_call(
        functools.partial(project_kernel, plan, finish),
        out_shape=out,
        grid_spec=pltpu.PrefetchScalarGridSpec(
            num_scalar_prefetch=1,
            grid=(1,),
            in_specs=[anywhere] * (2 + len(pieces))
            + [pl.BlockSpec(x.shape, lambda p, b: (0, 0)) for x in extras],
            out_specs=pl.BlockSpec(out.shape, lambda p, b: (0, 0)),
            scratch_shapes=[
                pltpu.VMEM((len(plan), chip_rows, strip), jnp.bfloat16),
                pltpu.VMEM((len(plan), strip, width), jnp.bfloat16),
                pltpu.VMEM((chip_rows, width), jnp.float32),
                pltpu.SemaphoreType.DMA((len(plan), 2)),
                pltpu.SemaphoreType.DMA((len(plan), 2)),
            ],
        ),
        cost_estimate=pl.CostEstimate(
            flops=2 * len(plan) * strip * chip_rows * width,
            bytes_accessed=2 * len(plan) * strip * (chip_rows + width),
            transcendentals=0,
        ),
    )(columns, own_tokens, sibling_tokens, *pieces, *extras)


def attention_kernel(hops, row_blocks, group, facts, *refs):
    q_ref = refs[0]
    k_refs = refs[1 : 1 + hops]
    v_refs = refs[1 + hops : 1 + 2 * hops]
    out_ref, score_ref, peak_ref, total_ref, acc_ref = refs[-5:]
    chip_blocks = CORES * row_blocks
    row_block = pl.program_id(1)
    source_core, ctx_index = facts[1], facts[2]
    chip = ctx_index // CORES
    here = ctx_index * row_blocks + row_block
    segment = facts[3 + here]
    factor = math.log2(math.e) / math.sqrt(HEAD_SIZE)
    rows = group * BLK

    def place(local):
        core = local // row_blocks
        slot = jnp.where(core == source_core, 0, row_blocks) + local % row_blocks
        return pl.ds(pl.multiple_of(slot * BLK, BLK), BLK)

    def queries():
        return jnp.concatenate(
            [q_ref[:, h * HEAD_SIZE : (h + 1) * HEAD_SIZE] for h in range(group)], axis=0
        )

    def scores(k_ref, local):
        return lax.dot_general(
            queries(),
            k_ref[place(local), :],
            (((1,), (1,)), ((), ())),
            preferred_element_type=jnp.float32,
        )

    def over_blocks(visit):
        for hop in range(hops):

            @pl.loop(0, chip_blocks)
            def _(local):
                block = (chip - hop) * chip_blocks + local
                seen = facts[3 + jnp.maximum(block, 0)]

                @pl.when(
                    (block >= 0) & (block < here) & ((seen == 0) | (seen == segment))
                )
                def _():
                    visit(hop, local)

    diagonal = lax.rem(here, chip_blocks)
    later = lax.broadcasted_iota(jnp.int32, (rows, BLK), 1) > (
        lax.broadcasted_iota(jnp.int32, (rows, BLK), 0) % BLK
    )
    own = jnp.where(later, MASKED, scores(k_refs[0], diagonal))
    score_ref[diagonal] = own
    peak_ref[...] = own

    def first(hop, local):
        found = scores(k_refs[hop], local)
        score_ref[hop * chip_blocks + local] = found
        peak_ref[...] = jnp.maximum(peak_ref[...], found)

    over_blocks(first)
    peak = jnp.max(peak_ref[...], axis=1, keepdims=True)
    peak_ref[...] = jnp.broadcast_to(peak, (rows, BLK))

    def weigh(hop, local):
        probs = jnp.exp2((score_ref[hop * chip_blocks + local] - peak_ref[...]) * factor)
        return probs, jnp.dot(
            probs.astype(jnp.bfloat16),
            v_refs[hop][place(local), :],
            preferred_element_type=jnp.float32,
        )

    total_ref[...], acc_ref[...] = weigh(0, diagonal)

    def second(hop, local):
        probs, mixed = weigh(hop, local)
        total_ref[...] += probs
        acc_ref[...] += mixed

    over_blocks(second)
    total = jnp.sum(total_ref[...], axis=1, keepdims=True)
    mixed = (acc_ref[...] / total).astype(out_ref.dtype)
    for h in range(group):
        out_ref[:, h * HEAD_SIZE : (h + 1) * HEAD_SIZE] = mixed[h * BLK : (h + 1) * BLK]


def attend(facts, queries, keys, values, before):
    hops = len(keys)
    number_of_rows, query_width = queries.shape
    group = query_width // HEAD_SIZE // KEY_VALUE_HEADS
    heads = KEY_VALUE_HEADS // CORES
    row_blocks = number_of_rows // BLK
    width = group * HEAD_SIZE
    rows = group * BLK
    q_spec = pl.BlockSpec((BLK, width), lambda l, r, f: (r, f[0] * heads + l))
    kv_spec = pl.BlockSpec((keys[0].shape[0], HEAD_SIZE), lambda l, r, f: (0, l))
    operands = [facts, queries, *keys, *values]
    in_specs = [q_spec] + [kv_spec] * (2 * hops)
    aliases = {}
    if before is not None:
        aliases = {len(operands): 0}
        operands.append(before)
        in_specs.append(pl.BlockSpec(memory_space=pl.ANY))
    total_blocks = hops * CORES * row_blocks
    pairs = heads * row_blocks * rows * total_blocks * BLK // 2
    return pl.pallas_call(
        functools.partial(attention_kernel, hops, row_blocks, group),
        out_shape=jax.ShapeDtypeStruct(queries.shape, queries.dtype),
        grid_spec=pltpu.PrefetchScalarGridSpec(
            num_scalar_prefetch=1,
            grid=(heads, row_blocks),
            in_specs=in_specs,
            out_specs=q_spec,
            scratch_shapes=[
                pltpu.VMEM((total_blocks, rows, BLK), jnp.float32),
                pltpu.VMEM((rows, BLK), jnp.float32),
                pltpu.VMEM((rows, BLK), jnp.float32),
                pltpu.VMEM((rows, HEAD_SIZE), jnp.float32),
            ],
        ),
        input_output_aliases=aliases,
        cost_estimate=pl.CostEstimate(
            flops=4 * pairs * HEAD_SIZE,
            bytes_accessed=2 * number_of_rows * query_width * 2,
            transcendentals=pairs,
        ),
        name="attend",
    )(*operands)


def layer(
    hidden_in,
    queries,
    key_projection_weight,
    value_projection_weight,
    key_projection_bias,
    value_projection_bias,
    block_segments,
):
    own_tokens = hidden_in[0]
    number_of_rows = own_tokens.shape[0]
    depth, kv_width = key_projection_weight.shape
    dp_size, ctx_size = lax.axis_size("dp"), lax.axis_size("ctx")
    chips = ctx_size // CORES
    my_index = lax.axis_index("ctx")
    core, chip = my_index % CORES, my_index // CORES
    plane = chip % 2
    half_width = kv_width // CORES
    ring = ring_order(dp_size)
    dp_index = lax.axis_index("dp")
    spots = [0] * dp_size
    for spot, index in enumerate(ring):
        spots[index] = spot
    my_spot = jnp.asarray(spots, jnp.int32)[dp_index]
    ring_array = jnp.asarray(ring, jnp.int32)

    def to_sibling(x):
        return lax.ppermute(x, "ctx", [(i, i ^ 1) for i in range(ctx_size)])

    def to_plane(x):
        return lax.ppermute(x, "ctx", [(i, i ^ CORES) for i in range(ctx_size)])

    def to_next_chip(x):
        return lax.ppermute(x, "ctx", [(i, i + CORES) for i in range(ctx_size - CORES)])

    def along_ring(x, step):
        return lax.ppermute(
            x, "dp", [(ring[i], ring[(i + step) % dp_size]) for i in range(dp_size)]
        )

    key_weight = lax.dynamic_slice_in_dim(key_projection_weight, core * half_width, half_width, 1)
    value_weight = lax.dynamic_slice_in_dim(
        value_projection_weight, core * half_width, half_width, 1
    )
    strip = depth // 2
    part = strip // 2
    key_strip = lax.dynamic_slice_in_dim(key_weight, plane * strip, strip, 0)
    sibling_tokens = to_sibling(own_tokens)

    def source_at(distance):
        return ring_array[(my_spot + distance + dp_size) % dp_size]

    half_ring = dp_size // 2

    key_pieces, key_plan, key_blocks = [key_weight], [], []
    for side in range(2):
        key_plan.append(((0, side * strip), (0, side * strip + part)))
        key_blocks.append(dp_index * 2 + side)
    travelling = {1: key_strip, -1: key_strip}
    last = []
    for hop in range(1, half_ring + 1):
        for step in (1, -1):
            piece = travelling[step]
            if hop == half_ring:
                first_row = 0 if step == 1 else part
                piece = piece[first_row : first_row + part]
            piece = along_ring(piece, step)
            travelling[step] = piece
            last.append((len(key_pieces), len(key_pieces) + 1))
            key_pieces += [piece, to_plane(piece)]
            if hop < half_ring:
                for side, at in enumerate(last[-1]):
                    key_plan.append(((at, 0), (at, part)))
                    key_blocks.append(
                        source_at(-step * hop) * 2 + (plane if side == 0 else 1 - plane)
                    )
    for side in range(2):
        key_plan.append(((last[-2][side], 0), (last[-1][side], 0)))
        key_blocks.append(source_at(half_ring) * 2 + (plane if side == 0 else 1 - plane))

    value_pieces, value_plan, value_blocks = [value_weight], [], []
    for side in range(2):
        value_plan.append(((0, side * strip), (0, side * strip + part)))
        value_blocks.append(dp_index * 2 + side)
    travelling = {1: value_weight, -1: value_weight}
    for hop in range(1, half_ring):
        for step in (1, -1):
            piece = along_ring(travelling[step], step)
            travelling[step] = piece
            at = len(value_pieces)
            value_pieces.append(piece)
            for side in range(2):
                value_plan.append(((at, side * strip), (at, side * strip + part)))
                value_blocks.append(source_at(-step * hop) * 2 + side)
    end_pieces = [
        along_ring(travelling[1][:strip], 1),
        along_ring(travelling[-1][strip:], -1),
    ]
    end_plan = [((side, 0), (side, part)) for side in range(2)]
    end_blocks = [source_at(half_ring) * 2 + side for side in range(2)]

    arange = jnp.arange(number_of_rows, dtype=jnp.int32)
    positions = jnp.concatenate(
        [my_index * number_of_rows + arange, (my_index ^ 1) * number_of_rows + arange]
    )
    key_bias = lax.dynamic_slice_in_dim(key_projection_bias, core * half_width, half_width, 0)
    value_bias = lax.dynamic_slice_in_dim(value_projection_bias, core * half_width, half_width, 0)

    def projected(finish, pieces, plan, blocks, extras):
        return project(
            finish,
            strip,
            own_tokens,
            sibling_tokens,
            pieces,
            tuple(plan),
            jnp.stack(blocks).astype(jnp.int32),
            extras,
        )

    key_rows = projected(
        "key", key_pieces, key_plan, key_blocks, [key_bias[None], *rope_tables(positions)]
    )
    value_sum = projected("sum", value_pieces, value_plan, value_blocks, [value_bias[None]])
    value_rows = projected("add", end_pieces, end_plan, end_blocks, [value_sum])

    keys, values = [key_rows], [value_rows]
    for _ in range(chips - 1):
        keys.append(to_next_chip(keys[-1]))
        values.append(to_next_chip(values[-1]))
    sibling_keys = [to_sibling(x) for x in keys]
    sibling_values = [to_sibling(x) for x in values]

    def facts(half):
        return jnp.concatenate([jnp.stack([half, half, my_index]), block_segments[0]])

    own_queries = queries[0]
    attended = attend(facts(core), own_queries, keys, values, None)
    attended = attend(facts(1 - core), own_queries, sibling_keys, sibling_values, attended)
    return attended[None]


def solution(mesh):
    placed = (
        P("dp", "ctx", None),
        P("dp", "ctx", None),
        P("dp", None),
        P("dp", None),
        P(),
        P(),
        P("dp", None),
    )
    return jax.shard_map(
        layer, mesh=mesh, in_specs=placed, out_specs=P("dp", "ctx", None), check_vma=False
    )
```

```python
import functools
import math

import jax
import jax.numpy as jnp
from jax import lax
from jax.experimental import pallas as pl
from jax.experimental.pallas import tpu as pltpu
from jax.sharding import PartitionSpec as P


HEAD_SIZE = 128
KEY_VALUE_HEADS = 4
BLK = 128
MASKED = -1e30
CORES = 2
SPARE_VMEM = 4 << 20

rope_base = 1000000.0


def ring_order(count):
    return list(range(0, count, 2)) + list(range(count - 1, 0, -2))


def rope_tables(token_positions):
    half_dim = HEAD_SIZE // 2
    frequency = rope_base ** (
        -(jnp.arange(half_dim, dtype=jnp.float32) * 2.0 / HEAD_SIZE)
    )
    angles = token_positions.astype(jnp.float32)[:, None] * frequency[None, :]
    cos_part, sine_part = jnp.cos(angles), jnp.sin(angles)
    return (
        jnp.concatenate([cos_part, cos_part], axis=1),
        jnp.concatenate([-sine_part, sine_part], axis=1),
    )


def project_kernel(plan, finish, added, columns, own_ref, sibling_ref, *refs):
    operands = 1 + max(part[0] for parts in plan for part in parts)
    piece_refs = refs[:operands]
    extra_refs = refs[operands:-6]
    out_ref, token_ref, weight_ref, acc_ref, token_sems, weight_sems = refs[-6:]
    number_of_rows, strip = own_ref.shape[0], weight_ref.shape[1]
    part_rows = strip // 2

    def token_copy(at, half):
        tokens_ref = (own_ref, sibling_ref)[half]
        return pltpu.make_async_copy(
            tokens_ref.at[:, pl.ds(pl.multiple_of(columns[at] * strip, strip), strip)],
            token_ref.at[at, pl.ds(half * number_of_rows, number_of_rows), :],
            token_sems.at[at, half],
        )

    def part_copy(operand, first_row, at, part):
        return pltpu.make_async_copy(
            piece_refs[operand].at[pl.ds(first_row, part_rows), :],
            weight_ref.at[at, pl.ds(part * part_rows, part_rows), :],
            weight_sems.at[at, part],
        )

    for at, parts in enumerate(plan):
        for part, (operand, first_row) in enumerate(parts):
            part_copy(operand, first_row, at, part).start()
        for half in range(2):
            token_copy(at, half).start()
    if added:
        acc_ref[...] = extra_refs[0][...]
        extra_refs = extra_refs[1:]
    else:
        acc_ref[...] = jnp.zeros_like(acc_ref)

    @pl.loop(0, len(plan) // 2)
    def _(pair):
        for at in (2 * pair, 2 * pair + 1):
            for half in range(2):
                part_copy(0, 0, at, half).wait()
                token_copy(at, half).wait()
        acc_ref[...] += jnp.dot(
            token_ref[2 * pair], weight_ref[2 * pair], preferred_element_type=jnp.float32
        ) + jnp.dot(
            token_ref[2 * pair + 1], weight_ref[2 * pair + 1], preferred_element_type=jnp.float32
        )

    if finish == "key":
        bias_ref, cos_ref, sine_ref = extra_refs
        for first in range(0, acc_ref.shape[1], HEAD_SIZE):
            lanes = slice(first, first + HEAD_SIZE)
            head = acc_ref[:, lanes] + bias_ref[:, lanes]
            turned = head * cos_ref[...] + pltpu.roll(head, HEAD_SIZE // 2, 1) * sine_ref[...]
            out_ref[:, lanes] = turned.astype(out_ref.dtype)
    elif finish == "value":
        out_ref[...] = (acc_ref[...] + extra_refs[0][...]).astype(out_ref.dtype)
    else:
        out_ref[...] = acc_ref[...].astype(out_ref.dtype)


def project(
    finish, strip, own_tokens, sibling_tokens, pieces, plan, columns, before, extras
):
    number_of_rows = own_tokens.shape[0]
    width = pieces[0].shape[1]
    anywhere = pl.BlockSpec(memory_space=pl.ANY)
    chip_rows = CORES * number_of_rows
    out = jax.ShapeDtypeStruct(
        (chip_rows, width), jnp.float32 if finish == "sum" else jnp.bfloat16
    )
    added = before is not None
    if added:
        extras = [before, *extras]
    grant = len(plan) * strip * (chip_rows + width) * 2
    grant += chip_rows * width * (4 + 8 * len(extras) + 8) + SPARE_VMEM
    return pl.pallas_call(
        functools.partial(project_kernel, plan, finish, added),
        out_shape=out,
        grid_spec=pltpu.PrefetchScalarGridSpec(
            num_scalar_prefetch=1,
            grid=(1,),
            in_specs=[anywhere] * (2 + len(pieces))
            + [pl.BlockSpec(x.shape, lambda p, b: (0, 0)) for x in extras],
            out_specs=pl.BlockSpec(out.shape, lambda p, b: (0, 0)),
            scratch_shapes=[
                pltpu.VMEM((len(plan), chip_rows, strip), jnp.bfloat16),
                pltpu.VMEM((len(plan), strip, width), jnp.bfloat16),
                pltpu.VMEM((chip_rows, width), jnp.float32),
                pltpu.SemaphoreType.DMA((len(plan), 2)),
                pltpu.SemaphoreType.DMA((len(plan), 2)),
            ],
        ),
        cost_estimate=pl.CostEstimate(
            flops=2 * len(plan) * strip * chip_rows * width,
            bytes_accessed=2 * len(plan) * strip * (chip_rows + width),
            transcendentals=0,
        ),
        compiler_params=pltpu.CompilerParams(vmem_limit_bytes=grant),
    )(columns, own_tokens, sibling_tokens, *pieces, *extras)


def attention_kernel(hops, row_blocks, group, facts, *refs):
    q_ref = refs[0]
    k_refs = refs[1 : 1 + hops]
    v_refs = refs[1 + hops : 1 + 2 * hops]
    out_ref, score_ref, peak_ref, total_ref, acc_ref = refs[-5:]
    chip_blocks = CORES * row_blocks
    row_block = pl.program_id(1)
    source_core, ctx_index = facts[1], facts[2]
    chip = ctx_index // CORES
    here = ctx_index * row_blocks + row_block
    segment = facts[3 + here]
    factor = math.log2(math.e) / math.sqrt(HEAD_SIZE)
    rows = group * BLK

    def place(local):
        core = local // row_blocks
        slot = jnp.where(core == source_core, 0, row_blocks) + local % row_blocks
        return pl.ds(pl.multiple_of(slot * BLK, BLK), BLK)

    def queries():
        return jnp.concatenate(
            [q_ref[:, h * HEAD_SIZE : (h + 1) * HEAD_SIZE] for h in range(group)], axis=0
        )

    def scores(k_ref, local):
        return lax.dot_general(
            queries(),
            k_ref[place(local), :],
            (((1,), (1,)), ((), ())),
            preferred_element_type=jnp.float32,
        )

    def over_blocks(visit):
        for hop in range(hops):

            @pl.loop(0, chip_blocks)
            def _(local):
                block = (chip - hop) * chip_blocks + local
                seen = facts[3 + jnp.maximum(block, 0)]

                @pl.when(
                    (block >= 0) & (block < here) & ((seen == 0) | (seen == segment))
                )
                def _():
                    visit(hop, local)

    diagonal = lax.rem(here, chip_blocks)
    later = lax.broadcasted_iota(jnp.int32, (rows, BLK), 1) > (
        lax.broadcasted_iota(jnp.int32, (rows, BLK), 0) % BLK
    )
    own = jnp.where(later, MASKED, scores(k_refs[0], diagonal))
    score_ref[diagonal] = own
    peak_ref[...] = own

    def first(hop, local):
        found = scores(k_refs[hop], local)
        score_ref[hop * chip_blocks + local] = found
        peak_ref[...] = jnp.maximum(peak_ref[...], found)

    over_blocks(first)
    peak = jnp.max(peak_ref[...], axis=1, keepdims=True)
    peak_ref[...] = jnp.broadcast_to(peak, (rows, BLK))

    def weigh(hop, local):
        probs = jnp.exp2((score_ref[hop * chip_blocks + local] - peak_ref[...]) * factor)
        return probs, jnp.dot(
            probs.astype(jnp.bfloat16),
            v_refs[hop][place(local), :],
            preferred_element_type=jnp.float32,
        )

    total_ref[...], acc_ref[...] = weigh(0, diagonal)

    def second(hop, local):
        probs, mixed = weigh(hop, local)
        total_ref[...] += probs
        acc_ref[...] += mixed

    over_blocks(second)
    total = jnp.sum(total_ref[...], axis=1, keepdims=True)
    mixed = (acc_ref[...] / total).astype(out_ref.dtype)
    for h in range(group):
        out_ref[:, h * HEAD_SIZE : (h + 1) * HEAD_SIZE] = mixed[h * BLK : (h + 1) * BLK]


def attend(facts, queries, keys, values, before):
    hops = len(keys)
    number_of_rows, query_width = queries.shape
    group = query_width // HEAD_SIZE // KEY_VALUE_HEADS
    heads = KEY_VALUE_HEADS // CORES
    row_blocks = number_of_rows // BLK
    width = group * HEAD_SIZE
    rows = group * BLK
    q_spec = pl.BlockSpec((BLK, width), lambda l, r, f: (r, f[0] * heads + l))
    kv_spec = pl.BlockSpec((keys[0].shape[0], HEAD_SIZE), lambda l, r, f: (0, l))
    operands = [facts, queries, *keys, *values]
    in_specs = [q_spec] + [kv_spec] * (2 * hops)
    aliases = {}
    if before is not None:
        aliases = {len(operands): 0}
        operands.append(before)
        in_specs.append(pl.BlockSpec(memory_space=pl.ANY))
    total_blocks = hops * CORES * row_blocks
    pairs = heads * row_blocks * rows * total_blocks * BLK // 2
    return pl.pallas_call(
        functools.partial(attention_kernel, hops, row_blocks, group),
        out_shape=jax.ShapeDtypeStruct(queries.shape, queries.dtype),
        grid_spec=pltpu.PrefetchScalarGridSpec(
            num_scalar_prefetch=1,
            grid=(heads, row_blocks),
            in_specs=in_specs,
            out_specs=q_spec,
            scratch_shapes=[
                pltpu.VMEM((total_blocks, rows, BLK), jnp.float32),
                pltpu.VMEM((rows, BLK), jnp.float32),
                pltpu.VMEM((rows, BLK), jnp.float32),
                pltpu.VMEM((rows, HEAD_SIZE), jnp.float32),
            ],
        ),
        input_output_aliases=aliases,
        compiler_params=pltpu.CompilerParams(
            vmem_limit_bytes=rows * BLK * 4 * (total_blocks + 6)
            + (BLK * width + hops * keys[0].size) * 8
            + SPARE_VMEM
        ),
        cost_estimate=pl.CostEstimate(
            flops=4 * pairs * HEAD_SIZE,
            bytes_accessed=2 * number_of_rows * query_width * 2,
            transcendentals=pairs,
        ),
        name="attend",
    )(*operands)


def layer(
    hidden_in,
    queries,
    key_projection_weight,
    value_projection_weight,
    key_projection_bias,
    value_projection_bias,
    block_segments,
):
    own_tokens = hidden_in[0]
    number_of_rows = own_tokens.shape[0]
    depth, kv_width = key_projection_weight.shape
    dp_size, ctx_size = lax.axis_size("dp"), lax.axis_size("ctx")
    chips = ctx_size // CORES
    my_index = lax.axis_index("ctx")
    core, chip = my_index % CORES, my_index // CORES
    plane = chip % 2
    half_width = kv_width // CORES
    ring = ring_order(dp_size)
    dp_index = lax.axis_index("dp")
    spots = [0] * dp_size
    for spot, index in enumerate(ring):
        spots[index] = spot
    my_spot = jnp.asarray(spots, jnp.int32)[dp_index]
    ring_array = jnp.asarray(ring, jnp.int32)

    def to_sibling(x):
        return lax.ppermute(x, "ctx", [(i, i ^ 1) for i in range(ctx_size)])

    def to_plane(x):
        return lax.ppermute(x, "ctx", [(i, i ^ CORES) for i in range(ctx_size)])

    def to_next_chip(x):
        return lax.ppermute(x, "ctx", [(i, i + CORES) for i in range(ctx_size - CORES)])

    def along_ring(x, step):
        return lax.ppermute(
            x, "dp", [(ring[i], ring[(i + step) % dp_size]) for i in range(dp_size)]
        )

    key_weight = lax.dynamic_slice_in_dim(key_projection_weight, core * half_width, half_width, 1)
    value_weight = lax.dynamic_slice_in_dim(
        value_projection_weight, core * half_width, half_width, 1
    )
    strip = depth // 2
    part = strip // 2
    key_strip = lax.dynamic_slice_in_dim(key_weight, plane * strip, strip, 0)
    sibling_tokens = to_sibling(own_tokens)

    def source_at(distance):
        return ring_array[(my_spot + distance + dp_size) % dp_size]

    half_ring = dp_size // 2

    arange = jnp.arange(number_of_rows, dtype=jnp.int32)
    positions = jnp.concatenate(
        [my_index * number_of_rows + arange, (my_index ^ 1) * number_of_rows + arange]
    )
    key_bias = lax.dynamic_slice_in_dim(key_projection_bias, core * half_width, half_width, 0)
    value_bias = lax.dynamic_slice_in_dim(value_projection_bias, core * half_width, half_width, 0)

    def projected(finish, strips, before, extras):
        pieces = []

        def operand(piece):
            for at, known in enumerate(pieces):
                if known is piece:
                    return at
            pieces.append(piece)
            return len(pieces) - 1

        plan = tuple(
            tuple((operand(piece), first_row) for piece, first_row in parts) for parts, _ in strips
        )
        columns = jnp.stack([at for _, at in strips]).astype(jnp.int32)
        return project(
            finish, strip, own_tokens, sibling_tokens, pieces, plan, columns, before, extras
        )

    def whole_strip(piece, first_row, at):
        return (((piece, first_row), (piece, first_row + part)), at)

    own_strips = [
        [whole_strip(weight, side * strip, dp_index * 2 + side) for side in range(2)]
        for weight in (key_weight, value_weight)
    ]
    sides = [plane, 1 - plane]
    key_strips = [own_strips[0]]
    travelling = {1: key_strip, -1: key_strip}
    for hop in range(1, half_ring + 1):
        arrived = {}
        for step in (1, -1):
            piece = travelling[step]
            if hop == half_ring:
                first_row = 0 if step == 1 else part
                piece = piece[first_row : first_row + part]
            piece = along_ring(piece, step)
            other = to_plane(piece)
            travelling[step] = piece
            arrived[step] = (piece, other)
        if hop < half_ring:
            key_strips.append(
                [
                    whole_strip(arrived[step][side], 0, source_at(-step * hop) * 2 + sides[side])
                    for step in (1, -1)
                    for side in range(2)
                ]
            )
        else:
            key_strips.append(
                [
                    (
                        ((arrived[1][side], 0), (arrived[-1][side], 0)),
                        source_at(hop) * 2 + sides[side],
                    )
                    for side in range(2)
                ]
            )

    value_strips = [own_strips[1]]
    travelling = {
        (side, step): value_weight[side * strip : (side + 1) * strip]
        for side in range(2)
        for step in (1, -1)
    }
    for hop in range(1, half_ring + 1):
        arrived = []
        for side in range(2):
            for step in (1, -1):
                if hop == half_ring and step != (1, -1)[side]:
                    continue
                piece = along_ring(travelling[side, step], step)
                travelling[side, step] = piece
                arrived.append(whole_strip(piece, 0, source_at(-step * hop) * 2 + side))
        value_strips.append(arrived)

    def joined(hops):
        return [entry for strips in hops for entry in strips]

    key_sum = projected("sum", joined(key_strips[:-2]), None, [])
    key_rows = projected(
        "key", joined(key_strips[-2:]), key_sum, [key_bias[None], *rope_tables(positions)]
    )
    value_sum = projected("sum", joined(value_strips[:-2]), None, [])
    value_sum = projected("sum", value_strips[-2], value_sum, [])
    value_rows = projected("value", value_strips[-1], value_sum, [value_bias[None]])

    keys, values = [key_rows], [value_rows]
    for _ in range(chips - 1):
        keys.append(to_next_chip(keys[-1]))
        values.append(to_next_chip(values[-1]))
    sibling_keys = [to_sibling(x) for x in keys]
    sibling_values = [to_sibling(x) for x in values]

    def facts(half):
        return jnp.concatenate([jnp.stack([half, half, my_index]), block_segments[0]])

    own_queries = queries[0]
    attended = attend(facts(core), own_queries, keys, values, None)
    attended = attend(facts(1 - core), own_queries, sibling_keys, sibling_values, attended)
    return attended[None]


def solution(mesh):
    placed = (
        P("dp", "ctx", None),
        P("dp", "ctx", None),
        P("dp", None),
        P("dp", None),
        P(),
        P(),
        P("dp", None),
    )
    return jax.shard_map(
        layer, mesh=mesh, in_specs=placed, out_specs=P("dp", "ctx", None), check_vma=False
    )
```

```python
import functools
import math

import jax
import jax.numpy as jnp
from jax import lax
from jax.experimental import pallas as pl
from jax.experimental.pallas import tpu as pltpu
from jax.sharding import PartitionSpec as P


HEAD_SIZE = 128
KEY_VALUE_HEADS = 4
BLK = 128
MASKED = -1e30
CORES = 2
SPARE_VMEM = 4 << 20

rope_base = 1000000.0


def ring_order(count):
    return list(range(0, count, 2)) + list(range(count - 1, 0, -2))


def rope_tables(token_positions):
    half_dim = HEAD_SIZE // 2
    frequency = rope_base ** (
        -(jnp.arange(half_dim, dtype=jnp.float32) * 2.0 / HEAD_SIZE)
    )
    angles = token_positions.astype(jnp.float32)[:, None] * frequency[None, :]
    cos_part, sine_part = jnp.cos(angles), jnp.sin(angles)
    return (
        jnp.concatenate([cos_part, cos_part], axis=1),
        jnp.concatenate([-sine_part, sine_part], axis=1),
    )


def project_kernel(plan, finish, added, columns, own_ref, sibling_ref, *refs):
    operands = 1 + max(part[0] for parts in plan for part in parts)
    piece_refs = refs[:operands]
    extra_refs = refs[operands:-6]
    out_ref, token_ref, weight_ref, acc_ref, token_sems, weight_sems = refs[-6:]
    number_of_rows, strip = own_ref.shape[0], weight_ref.shape[1]
    part_rows = strip // 2

    def token_copy(at, half):
        tokens_ref = (own_ref, sibling_ref)[half]
        return pltpu.make_async_copy(
            tokens_ref.at[:, pl.ds(pl.multiple_of(columns[at] * strip, strip), strip)],
            token_ref.at[at, pl.ds(half * number_of_rows, number_of_rows), :],
            token_sems.at[at, half],
        )

    def part_copy(operand, first_row, at, part):
        return pltpu.make_async_copy(
            piece_refs[operand].at[pl.ds(first_row, part_rows), :],
            weight_ref.at[at, pl.ds(part * part_rows, part_rows), :],
            weight_sems.at[at, part],
        )

    for at, parts in enumerate(plan):
        for part, (operand, first_row) in enumerate(parts):
            part_copy(operand, first_row, at, part).start()
        for half in range(2):
            token_copy(at, half).start()
    if added:
        acc_ref[...] = extra_refs[0][...]
        extra_refs = extra_refs[1:]
    else:
        acc_ref[...] = jnp.zeros_like(acc_ref)

    @pl.loop(0, len(plan) // 2)
    def _(pair):
        for at in (2 * pair, 2 * pair + 1):
            for half in range(2):
                part_copy(0, 0, at, half).wait()
                token_copy(at, half).wait()
        acc_ref[...] += jnp.dot(
            token_ref[2 * pair], weight_ref[2 * pair], preferred_element_type=jnp.float32
        ) + jnp.dot(
            token_ref[2 * pair + 1], weight_ref[2 * pair + 1], preferred_element_type=jnp.float32
        )

    if finish == "key":
        bias_ref, cos_ref, sine_ref = extra_refs
        for first in range(0, acc_ref.shape[1], HEAD_SIZE):
            lanes = slice(first, first + HEAD_SIZE)
            head = acc_ref[:, lanes] + bias_ref[:, lanes]
            turned = head * cos_ref[...] + pltpu.roll(head, HEAD_SIZE // 2, 1) * sine_ref[...]
            out_ref[:, lanes] = turned.astype(out_ref.dtype)
    elif finish == "value":
        out_ref[...] = (acc_ref[...] + extra_refs[0][...]).astype(out_ref.dtype)
    else:
        out_ref[...] = acc_ref[...].astype(out_ref.dtype)


def project(
    finish, strip, own_tokens, sibling_tokens, pieces, plan, columns, before, extras
):
    number_of_rows = own_tokens.shape[0]
    width = pieces[0].shape[1]
    anywhere = pl.BlockSpec(memory_space=pltpu.MemorySpace.HBM)
    chip_rows = CORES * number_of_rows
    out = jax.ShapeDtypeStruct(
        (chip_rows, width), jnp.float32 if finish == "sum" else jnp.bfloat16
    )
    added = before is not None
    if added:
        extras = [before, *extras]
    grant = len(plan) * strip * (chip_rows + width) * 2
    grant += chip_rows * width * (4 + 8 * len(extras) + 8) + SPARE_VMEM
    return pl.pallas_call(
        functools.partial(project_kernel, plan, finish, added),
        out_shape=out,
        grid_spec=pltpu.PrefetchScalarGridSpec(
            num_scalar_prefetch=1,
            grid=(1,),
            in_specs=[anywhere] * (2 + len(pieces))
            + [pl.BlockSpec(x.shape, lambda p, b: (0, 0)) for x in extras],
            out_specs=pl.BlockSpec(out.shape, lambda p, b: (0, 0)),
            scratch_shapes=[
                pltpu.VMEM((len(plan), chip_rows, strip), jnp.bfloat16),
                pltpu.VMEM((len(plan), strip, width), jnp.bfloat16),
                pltpu.VMEM((chip_rows, width), jnp.float32),
                pltpu.SemaphoreType.DMA((len(plan), 2)),
                pltpu.SemaphoreType.DMA((len(plan), 2)),
            ],
        ),
        cost_estimate=pl.CostEstimate(
            flops=2 * len(plan) * strip * chip_rows * width,
            bytes_accessed=2 * len(plan) * strip * (chip_rows + width),
            transcendentals=0,
        ),
        compiler_params=pltpu.CompilerParams(vmem_limit_bytes=grant),
    )(columns, own_tokens, sibling_tokens, *pieces, *extras)


def attention_kernel(hops, row_blocks, group, facts, *refs):
    q_ref = refs[0]
    k_refs = refs[1 : 1 + hops]
    v_refs = refs[1 + hops : 1 + 2 * hops]
    out_ref, score_ref, peak_ref, total_ref, acc_ref = refs[-5:]
    chip_blocks = CORES * row_blocks
    row_block = pl.program_id(1)
    source_core, ctx_index = facts[1], facts[2]
    chip = ctx_index // CORES
    here = ctx_index * row_blocks + row_block
    segment = facts[3 + here]
    factor = math.log2(math.e) / math.sqrt(HEAD_SIZE)
    rows = group * BLK

    def place(local):
        core = local // row_blocks
        slot = jnp.where(core == source_core, 0, row_blocks) + local % row_blocks
        return pl.ds(pl.multiple_of(slot * BLK, BLK), BLK)

    def queries():
        return jnp.concatenate(
            [q_ref[:, h * HEAD_SIZE : (h + 1) * HEAD_SIZE] for h in range(group)], axis=0
        )

    def scores(k_ref, local):
        return lax.dot_general(
            queries(),
            k_ref[place(local), :],
            (((1,), (1,)), ((), ())),
            preferred_element_type=jnp.float32,
        )

    def over_blocks(visit):
        for hop in range(hops):

            @pl.loop(0, chip_blocks)
            def _(local):
                block = (chip - hop) * chip_blocks + local
                seen = facts[3 + jnp.maximum(block, 0)]

                @pl.when(
                    (block >= 0) & (block < here) & ((seen == 0) | (seen == segment))
                )
                def _():
                    visit(hop, local)

    diagonal = lax.rem(here, chip_blocks)
    later = lax.broadcasted_iota(jnp.int32, (rows, BLK), 1) > (
        lax.broadcasted_iota(jnp.int32, (rows, BLK), 0) % BLK
    )
    own = jnp.where(later, MASKED, scores(k_refs[0], diagonal))
    score_ref[diagonal] = own
    peak_ref[...] = own

    def first(hop, local):
        found = scores(k_refs[hop], local)
        score_ref[hop * chip_blocks + local] = found
        peak_ref[...] = jnp.maximum(peak_ref[...], found)

    over_blocks(first)
    peak = jnp.max(peak_ref[...], axis=1, keepdims=True)
    peak_ref[...] = jnp.broadcast_to(peak, (rows, BLK))

    def weigh(hop, local):
        probs = jnp.exp2((score_ref[hop * chip_blocks + local] - peak_ref[...]) * factor)
        return probs, jnp.dot(
            probs.astype(jnp.bfloat16),
            v_refs[hop][place(local), :],
            preferred_element_type=jnp.float32,
        )

    total_ref[...], acc_ref[...] = weigh(0, diagonal)

    def second(hop, local):
        probs, mixed = weigh(hop, local)
        total_ref[...] += probs
        acc_ref[...] += mixed

    over_blocks(second)
    total = jnp.sum(total_ref[...], axis=1, keepdims=True)
    mixed = (acc_ref[...] / total).astype(out_ref.dtype)
    for h in range(group):
        out_ref[:, h * HEAD_SIZE : (h + 1) * HEAD_SIZE] = mixed[h * BLK : (h + 1) * BLK]


def attend(facts, queries, keys, values, before):
    hops = len(keys)
    number_of_rows, query_width = queries.shape
    group = query_width // HEAD_SIZE // KEY_VALUE_HEADS
    heads = KEY_VALUE_HEADS // CORES
    row_blocks = number_of_rows // BLK
    width = group * HEAD_SIZE
    rows = group * BLK
    q_spec = pl.BlockSpec((BLK, width), lambda l, r, f: (r, f[0] * heads + l))
    kv_spec = pl.BlockSpec((keys[0].shape[0], HEAD_SIZE), lambda l, r, f: (0, l))
    operands = [facts, queries, *keys, *values]
    in_specs = [q_spec] + [kv_spec] * (2 * hops)
    aliases = {}
    if before is not None:
        aliases = {len(operands): 0}
        operands.append(before)
        in_specs.append(pl.BlockSpec(memory_space=pl.ANY))
    total_blocks = hops * CORES * row_blocks
    pairs = heads * row_blocks * rows * total_blocks * BLK // 2
    return pl.pallas_call(
        functools.partial(attention_kernel, hops, row_blocks, group),
        out_shape=jax.ShapeDtypeStruct(queries.shape, queries.dtype),
        grid_spec=pltpu.PrefetchScalarGridSpec(
            num_scalar_prefetch=1,
            grid=(heads, row_blocks),
            in_specs=in_specs,
            out_specs=q_spec,
            scratch_shapes=[
                pltpu.VMEM((total_blocks, rows, BLK), jnp.float32),
                pltpu.VMEM((rows, BLK), jnp.float32),
                pltpu.VMEM((rows, BLK), jnp.float32),
                pltpu.VMEM((rows, HEAD_SIZE), jnp.float32),
            ],
        ),
        input_output_aliases=aliases,
        compiler_params=pltpu.CompilerParams(
            vmem_limit_bytes=rows * BLK * 4 * (total_blocks + 6)
            + (BLK * width + hops * keys[0].size) * 8
            + SPARE_VMEM
        ),
        cost_estimate=pl.CostEstimate(
            flops=4 * pairs * HEAD_SIZE,
            bytes_accessed=2 * number_of_rows * query_width * 2,
            transcendentals=pairs,
        ),
        name="attend",
    )(*operands)


def layer(
    hidden_in,
    queries,
    key_projection_weight,
    value_projection_weight,
    key_projection_bias,
    value_projection_bias,
    block_segments,
):
    own_tokens = hidden_in[0]
    number_of_rows = own_tokens.shape[0]
    depth, kv_width = key_projection_weight.shape
    dp_size, ctx_size = lax.axis_size("dp"), lax.axis_size("ctx")
    chips = ctx_size // CORES
    my_index = lax.axis_index("ctx")
    core, chip = my_index % CORES, my_index // CORES
    plane = chip % 2
    half_width = kv_width // CORES
    ring = ring_order(dp_size)
    dp_index = lax.axis_index("dp")
    my_spot = jnp.where(dp_index % 2 == 0, dp_index // 2, dp_size - (dp_index + 1) // 2)

    def to_sibling(x):
        return lax.ppermute(x, "ctx", [(i, i ^ 1) for i in range(ctx_size)])

    def to_plane(x):
        return lax.ppermute(x, "ctx", [(i, i ^ CORES) for i in range(ctx_size)])

    def to_next_chip(x):
        return lax.ppermute(x, "ctx", [(i, i + CORES) for i in range(ctx_size - CORES)])

    def along_ring(x, step):
        return lax.ppermute(
            x, "dp", [(ring[i], ring[(i + step) % dp_size]) for i in range(dp_size)]
        )

    key_weight = lax.dynamic_slice_in_dim(key_projection_weight, core * half_width, half_width, 1)
    value_weight = lax.dynamic_slice_in_dim(
        value_projection_weight, core * half_width, half_width, 1
    )
    strip = depth // 2
    part = strip // 2
    key_strip = lax.dynamic_slice_in_dim(key_weight, plane * strip, strip, 0)
    sibling_tokens = to_sibling(own_tokens)

    def source_at(distance):
        spot = (my_spot + distance + dp_size) % dp_size
        return jnp.where(spot < dp_size // 2, 2 * spot, 2 * (dp_size - spot) - 1)

    half_ring = dp_size // 2

    arange = jnp.arange(number_of_rows, dtype=jnp.int32)
    positions = jnp.concatenate(
        [my_index * number_of_rows + arange, (my_index ^ 1) * number_of_rows + arange]
    )
    key_bias = lax.dynamic_slice_in_dim(key_projection_bias, core * half_width, half_width, 0)
    value_bias = lax.dynamic_slice_in_dim(value_projection_bias, core * half_width, half_width, 0)

    def projected(finish, strips, before, extras):
        pieces = []

        def operand(piece):
            for at, known in enumerate(pieces):
                if known is piece:
                    return at
            pieces.append(piece)
            return len(pieces) - 1

        plan = tuple(
            tuple((operand(piece), first_row) for piece, first_row in parts) for parts, _ in strips
        )
        columns = jnp.stack([at for _, at in strips]).astype(jnp.int32)
        return project(
            finish, strip, own_tokens, sibling_tokens, pieces, plan, columns, before, extras
        )

    def whole_strip(piece, first_row, at):
        return (((piece, first_row), (piece, first_row + part)), at)

    own_strips = [
        [whole_strip(weight, side * strip, dp_index * 2 + side) for side in range(2)]
        for weight in (key_weight, value_weight)
    ]
    sides = [plane, 1 - plane]
    key_strips = [own_strips[0]]
    travelling = {1: key_strip, -1: key_strip}
    for hop in range(1, half_ring + 1):
        arrived = {}
        for step in (1, -1):
            piece = travelling[step]
            if hop == half_ring:
                first_row = 0 if step == 1 else part
                piece = piece[first_row : first_row + part]
            piece = along_ring(piece, step)
            other = to_plane(piece)
            travelling[step] = piece
            arrived[step] = (piece, other)
        if hop < half_ring:
            key_strips.append(
                [
                    whole_strip(arrived[step][side], 0, source_at(-step * hop) * 2 + sides[side])
                    for step in (1, -1)
                    for side in range(2)
                ]
            )
        else:
            key_strips.append(
                [
                    (
                        ((arrived[1][side], 0), (arrived[-1][side], 0)),
                        source_at(hop) * 2 + sides[side],
                    )
                    for side in range(2)
                ]
            )

    value_strips = [own_strips[1]]
    travelling = {
        (side, step): value_weight[side * strip : (side + 1) * strip]
        for side in range(2)
        for step in (1, -1)
    }
    for hop in range(1, half_ring + 1):
        arrived = []
        for side in range(2):
            for step in (1, -1):
                if hop == half_ring and step != (1, -1)[side]:
                    continue
                piece = along_ring(travelling[side, step], step)
                travelling[side, step] = piece
                arrived.append(whole_strip(piece, 0, source_at(-step * hop) * 2 + side))
        value_strips.append(arrived)

    def joined(hops):
        return [entry for strips in hops for entry in strips]

    key_sum = projected("sum", joined(key_strips[:-2]), None, [])
    key_rows = projected(
        "key", joined(key_strips[-2:]), key_sum, [key_bias[None], *rope_tables(positions)]
    )
    value_sum = projected("sum", joined(value_strips[:-2]), None, [])
    value_sum = projected("sum", value_strips[-2], value_sum, [])
    value_rows = projected("value", value_strips[-1], value_sum, [value_bias[None]])

    keys, values = [key_rows], [value_rows]
    for _ in range(chips - 1):
        keys.append(to_next_chip(keys[-1]))
        values.append(to_next_chip(values[-1]))
    sibling_keys = [to_sibling(x) for x in keys]
    sibling_values = [to_sibling(x) for x in values]

    def facts(half):
        return jnp.concatenate([jnp.stack([half, half, my_index]), block_segments[0]])

    own_queries = queries[0]
    attended = attend(facts(core), own_queries, keys, values, None)
    attended = attend(facts(1 - core), own_queries, sibling_keys, sibling_values, attended)
    return attended[None]


def solution(mesh):
    placed = (
        P("dp", "ctx", None),
        P("dp", "ctx", None),
        P("dp", None),
        P("dp", None),
        P(),
        P(),
        P("dp", None),
    )
    return jax.shard_map(
        layer, mesh=mesh, in_specs=placed, out_specs=P("dp", "ctx", None), check_vma=False
    )
```

```python
import functools
import math

import jax
import jax.numpy as jnp
from jax import lax
from jax.experimental import pallas as pl
from jax.experimental.pallas import tpu as pltpu
from jax.sharding import PartitionSpec as P


HEAD_SIZE = 128
KEY_VALUE_HEADS = 4
BLK = 128
MASKED = -1e30
CORES = 2
CHUNK = 2 * BLK
SPARE_VMEM = 4 << 20
MOST_VMEM = 67043328

rope_base = 1000000.0


def ring_order(count):
    return list(range(0, count, 2)) + list(range(count - 1, 0, -2))


def rope_tables(token_positions):
    half_dim = HEAD_SIZE // 2
    frequency = rope_base ** (
        -(jnp.arange(half_dim, dtype=jnp.float32) * 2.0 / HEAD_SIZE)
    )
    angles = token_positions.astype(jnp.float32)[:, None] * frequency[None, :]
    cos_part, sine_part = jnp.cos(angles), jnp.sin(angles)
    return (
        jnp.concatenate([cos_part, cos_part], axis=1),
        jnp.concatenate([-sine_part, sine_part], axis=1),
    )


def project_kernel(plan, finish, added, columns, own_ref, sibling_ref, *refs):
    operands = 1 + max(part[0] for parts in plan for part in parts)
    piece_refs = refs[:operands]
    extra_refs = refs[operands:-6]
    out_ref, token_ref, weight_ref, acc_ref, token_sems, weight_sems = refs[-6:]
    number_of_rows, strip = own_ref.shape[0], weight_ref.shape[1]
    part_rows = strip // 2

    def token_copy(at, half):
        tokens_ref = (own_ref, sibling_ref)[half]
        return pltpu.make_async_copy(
            tokens_ref.at[:, pl.ds(pl.multiple_of(columns[at] * strip, strip), strip)],
            token_ref.at[at, pl.ds(half * number_of_rows, number_of_rows), :],
            token_sems.at[at, half],
        )

    def part_copy(operand, first_row, at, part):
        return pltpu.make_async_copy(
            piece_refs[operand].at[pl.ds(first_row, part_rows), :],
            weight_ref.at[at, pl.ds(part * part_rows, part_rows), :],
            weight_sems.at[at, part],
        )

    for at, parts in enumerate(plan):
        for part, (operand, first_row) in enumerate(parts):
            part_copy(operand, first_row, at, part).start()
        for half in range(2):
            token_copy(at, half).start()
    if added:
        acc_ref[...] = extra_refs[0][...]
        extra_refs = extra_refs[1:]
    else:
        acc_ref[...] = jnp.zeros_like(acc_ref)

    @pl.loop(0, len(plan) // 2)
    def _(pair):
        for at in (2 * pair, 2 * pair + 1):
            for half in range(2):
                part_copy(0, 0, at, half).wait()
                token_copy(at, half).wait()
        acc_ref[...] += jnp.dot(
            token_ref[2 * pair], weight_ref[2 * pair], preferred_element_type=jnp.float32
        ) + jnp.dot(
            token_ref[2 * pair + 1], weight_ref[2 * pair + 1], preferred_element_type=jnp.float32
        )

    if finish == "key":
        bias_ref, cos_ref, sine_ref = extra_refs
        for first in range(0, acc_ref.shape[1], HEAD_SIZE):
            lanes = slice(first, first + HEAD_SIZE)
            head = acc_ref[:, lanes] + bias_ref[:, lanes]
            turned = head * cos_ref[...] + pltpu.roll(head, HEAD_SIZE // 2, 1) * sine_ref[...]
            out_ref[:, lanes] = turned.astype(out_ref.dtype)
    elif finish == "value":
        out_ref[...] = (acc_ref[...] + extra_refs[0][...]).astype(out_ref.dtype)
    else:
        out_ref[...] = acc_ref[...].astype(out_ref.dtype)


def project(
    finish, strip, own_tokens, sibling_tokens, pieces, plan, columns, before, extras
):
    number_of_rows = own_tokens.shape[0]
    width = pieces[0].shape[1]
    anywhere = pl.BlockSpec(memory_space=pltpu.MemorySpace.HBM)
    chip_rows = CORES * number_of_rows
    out = jax.ShapeDtypeStruct(
        (chip_rows, width), jnp.float32 if finish == "sum" else jnp.bfloat16
    )
    added = before is not None
    if added:
        extras = [before, *extras]
    grant = MOST_VMEM - (3 << 19) * (finish == "value" or (added and finish == "sum"))
    return pl.pallas_call(
        functools.partial(project_kernel, plan, finish, added),
        out_shape=out,
        grid_spec=pltpu.PrefetchScalarGridSpec(
            num_scalar_prefetch=1,
            grid=(1,),
            in_specs=[anywhere] * (2 + len(pieces))
            + [pl.BlockSpec(x.shape, lambda p, b: (0, 0)) for x in extras],
            out_specs=pl.BlockSpec(out.shape, lambda p, b: (0, 0)),
            scratch_shapes=[
                pltpu.VMEM((len(plan), chip_rows, strip), jnp.bfloat16),
                pltpu.VMEM((len(plan), strip, width), jnp.bfloat16),
                pltpu.VMEM((chip_rows, width), jnp.float32),
                pltpu.SemaphoreType.DMA((len(plan), 2)),
                pltpu.SemaphoreType.DMA((len(plan), 2)),
            ],
        ),
        cost_estimate=pl.CostEstimate(
            flops=2 * len(plan) * strip * chip_rows * width,
            bytes_accessed=2 * len(plan) * strip * (chip_rows + width),
            transcendentals=0,
        ),
        compiler_params=pltpu.CompilerParams(vmem_limit_bytes=grant),
    )(columns, own_tokens, sibling_tokens, *pieces, *extras)


class Blocks:
    def __init__(self, facts, hops, row_blocks, row_block):
        self.row_blocks, self.source_core = row_blocks, facts[1]
        per_chip = CORES * row_blocks
        chip = facts[2] // CORES
        here = facts[2] * row_blocks + row_block
        segment = facts[3 + here]
        self.diagonal = lax.rem(here, per_chip)
        self.entries, slot = [], jnp.int32(0)
        for hop in range(hops):
            for local in range(per_chip):
                block = (chip - hop) * per_chip + local
                seen = facts[3 + jnp.maximum(block, 0)]
                allowed = (block >= 0) & (block < here) & ((seen == 0) | (seen == segment))
                self.entries.append((hop, local, allowed, slot))
                slot = slot + jnp.where(allowed, 1, 0)
        self.odd = lax.rem(slot, 2) == 1
        self.free_slot = slot
        self.chunks = (slot + 2) // 2

    def place(self, local):
        core = local // self.row_blocks
        slot = jnp.where(core == self.source_core, 0, self.row_blocks)
        slot = slot + lax.rem(local, self.row_blocks)
        return pl.ds(pl.multiple_of(slot * BLK, BLK), BLK)

    def gather(self, refs, chosen_ref):
        def slot_rows(slot):
            return pl.ds(pl.multiple_of(slot * BLK, BLK), BLK)

        for hop, local, allowed, slot in self.entries:

            @pl.when(allowed)
            def _(hop=hop, local=local, slot=slot):
                chosen_ref[slot_rows(slot), :] = refs[hop][self.place(jnp.int32(local)), :]

        @pl.when(jnp.logical_not(self.odd))
        def _():
            chosen_ref[slot_rows(self.free_slot), :] = jnp.zeros((BLK, HEAD_SIZE), jnp.bfloat16)

        chosen_ref[slot_rows(2 * self.chunks - 1), :] = refs[0][self.place(self.diagonal), :]


def chunk_rows(chunk):
    return pl.ds(pl.multiple_of(chunk * CHUNK, CHUNK), CHUNK)


def score_kernel(hops, row_blocks, group, facts, q_ref, *refs):
    k_refs = refs[:hops]
    probs_ref, inverse_ref, chosen_ref, score_ref, peak_ref, total_ref = refs[hops:]
    blocks = Blocks(facts, hops, row_blocks, pl.program_id(1))
    blocks.gather(k_refs, chosen_ref)
    factor = math.log2(math.e) / math.sqrt(HEAD_SIZE)
    rows = group * BLK

    def scores(chunk):
        heads = [q_ref[:, h * HEAD_SIZE : (h + 1) * HEAD_SIZE] for h in range(group)]
        return lax.dot_general(
            jnp.concatenate(heads, axis=0),
            chosen_ref[chunk_rows(chunk), :],
            (((1,), (1,)), ((), ())),
            preferred_element_type=jnp.float32,
        )

    last = blocks.chunks - 1
    column = lax.broadcasted_iota(jnp.int32, (rows, CHUNK), 1)
    row = lax.broadcasted_iota(jnp.int32, (rows, CHUNK), 0) % BLK
    first_column = jnp.where(blocks.odd, 0, BLK)
    found = jnp.where(
        (column >= first_column) & (column - BLK <= row), scores(last), MASKED
    )
    score_ref[last] = found
    peak_ref[...] = jnp.maximum(found[:, :BLK], found[:, BLK:])

    @pl.loop(0, last)
    def _(chunk):
        found = scores(chunk)
        score_ref[chunk] = found
        peak_ref[...] = jnp.maximum(
            peak_ref[...], jnp.maximum(found[:, :BLK], found[:, BLK:])
        )

    peak_ref[...] = jnp.broadcast_to(
        jnp.max(peak_ref[...], axis=1, keepdims=True), (rows, BLK)
    )
    total_ref[...] = jnp.zeros_like(total_ref)

    @pl.loop(0, blocks.chunks)
    def _(chunk):
        peak = peak_ref[...]
        total = total_ref[...]
        for first in range(0, CHUNK, BLK):
            lanes = slice(first, first + BLK)
            probs = jnp.exp2((score_ref[chunk, :, lanes] - peak) * factor)
            probs_ref[0, chunk, :, lanes] = probs.astype(probs_ref.dtype)
            total = total + probs
        total_ref[...] = total

    inverse_ref[0] = jnp.broadcast_to(
        1.0 / jnp.sum(total_ref[...], axis=1, keepdims=True), (rows, BLK)
    )


def mix_kernel(hops, row_blocks, group, facts, probs_ref, inverse_ref, *refs):
    v_refs = refs[:hops]
    out_ref, chosen_ref, held_ref, acc_ref, sems = refs[-5:]
    head, row_block = pl.program_id(0), pl.program_id(1)
    step = head * row_blocks + row_block
    steps = pl.num_programs(0) * row_blocks
    blocks = Blocks(facts, hops, row_blocks, row_block)

    def fetch(at, chunk):
        side = lax.rem(at, 2)
        return pltpu.make_async_copy(
            probs_ref.at[at, chunk], held_ref.at[side, chunk], sems.at[side, chunk]
        )

    @pl.when(step == 0)
    def _():
        @pl.loop(0, blocks.chunks)
        def _(chunk):
            fetch(step, chunk).start()

    @pl.when(step + 1 < steps)
    def _():
        coming = Blocks(facts, hops, row_blocks, lax.rem(row_block + 1, row_blocks))

        @pl.loop(0, coming.chunks)
        def _(chunk):
            fetch(step + 1, chunk).start()

    blocks.gather(v_refs, chosen_ref)
    acc_ref[...] = jnp.zeros_like(acc_ref)

    @pl.loop(0, blocks.chunks)
    def _(chunk):
        fetch(step, chunk).wait()
        acc_ref[...] += jnp.dot(
            held_ref[lax.rem(step, 2), chunk],
            chosen_ref[chunk_rows(chunk), :],
            preferred_element_type=jnp.float32,
        )

    mixed = (acc_ref[...] * inverse_ref[0]).astype(out_ref.dtype)
    for h in range(group):
        out_ref[:, h * HEAD_SIZE : (h + 1) * HEAD_SIZE] = mixed[h * BLK : (h + 1) * BLK]


class Attention:
    def __init__(self, facts, queries, hops):
        self.facts, self.queries, self.hops = facts, queries, hops
        self.rows, query_width = queries.shape
        self.group = query_width // HEAD_SIZE // KEY_VALUE_HEADS
        self.heads = KEY_VALUE_HEADS // CORES
        self.row_blocks = self.rows // BLK
        self.stacked = self.group * BLK
        self.chunks = hops * CORES * self.row_blocks * BLK // CHUNK
        self.q_spec = pl.BlockSpec(
            (BLK, self.group * HEAD_SIZE), lambda l, r, f: (r, f[0] * self.heads + l)
        )
        self.kv_spec = pl.BlockSpec((CORES * self.rows, HEAD_SIZE), lambda l, r, f: (0, l))
        self.inverse_spec = pl.BlockSpec(
            (1, self.stacked, BLK), lambda l, r, f: (l * self.row_blocks + r, 0, 0)
        )
        self.pairs = self.heads * self.row_blocks * self.stacked * self.chunks * CHUNK // 2
        self.block_bytes = self.stacked * BLK * 4

    def scores(self, keys):
        count = self.heads * self.row_blocks
        probs = jax.ShapeDtypeStruct(
            (count, self.chunks, self.stacked, CHUNK), jnp.bfloat16
        )
        return pl.pallas_call(
            functools.partial(score_kernel, self.hops, self.row_blocks, self.group),
            out_shape=(
                probs,
                jax.ShapeDtypeStruct((count, self.stacked, BLK), jnp.float32),
            ),
            grid_spec=pltpu.PrefetchScalarGridSpec(
                num_scalar_prefetch=1,
                grid=(self.heads, self.row_blocks),
                in_specs=[self.q_spec] + [self.kv_spec] * self.hops,
                out_specs=(
                    pl.BlockSpec(
                        (1, *probs.shape[1:]), lambda l, r, f: (l * self.row_blocks + r, 0, 0, 0)
                    ),
                    self.inverse_spec,
                ),
                scratch_shapes=[
                    pltpu.VMEM((self.chunks * CHUNK, HEAD_SIZE), jnp.bfloat16),
                    pltpu.VMEM((self.chunks, self.stacked, CHUNK), jnp.float32),
                    pltpu.VMEM((self.stacked, BLK), jnp.float32),
                    pltpu.VMEM((self.stacked, BLK), jnp.float32),
                ],
            ),
            compiler_params=pltpu.CompilerParams(
                vmem_limit_bytes=self.block_bytes * (4 * self.chunks + 8) + SPARE_VMEM
            ),
            cost_estimate=pl.CostEstimate(
                flops=2 * self.pairs * HEAD_SIZE,
                bytes_accessed=self.queries.size + self.pairs * 4,
                transcendentals=self.pairs,
            ),
            name="score",
        )(self.facts, self.queries, *keys)

    def mix(self, probs, inverse, values, before):
        operands = [self.facts, probs, inverse, *values]
        in_specs = [pl.BlockSpec(memory_space=pl.ANY), self.inverse_spec]
        in_specs += [self.kv_spec] * self.hops
        aliases = {}
        if before is not None:
            aliases = {len(operands): 0}
            operands.append(before)
            in_specs.append(pl.BlockSpec(memory_space=pl.ANY))
        return pl.pallas_call(
            functools.partial(mix_kernel, self.hops, self.row_blocks, self.group),
            out_shape=jax.ShapeDtypeStruct(self.queries.shape, self.queries.dtype),
            grid_spec=pltpu.PrefetchScalarGridSpec(
                num_scalar_prefetch=1,
                grid=(self.heads, self.row_blocks),
                in_specs=in_specs,
                out_specs=self.q_spec,
                scratch_shapes=[
                    pltpu.VMEM((self.chunks * CHUNK, HEAD_SIZE), jnp.bfloat16),
                    pltpu.VMEM((2, *probs.shape[1:]), jnp.bfloat16),
                    pltpu.VMEM((self.stacked, HEAD_SIZE), jnp.float32),
                    pltpu.SemaphoreType.DMA((2, self.chunks)),
                ],
            ),
            input_output_aliases=aliases,
            compiler_params=pltpu.CompilerParams(
                vmem_limit_bytes=self.block_bytes * (2 * self.chunks + 8) + SPARE_VMEM
            ),
            cost_estimate=pl.CostEstimate(
                flops=2 * self.pairs * HEAD_SIZE,
                bytes_accessed=self.queries.size + self.pairs * 4,
                transcendentals=0,
            ),
            name="mix",
        )(*operands)


def layer(
    hidden_in,
    queries,
    key_projection_weight,
    value_projection_weight,
    key_projection_bias,
    value_projection_bias,
    block_segments,
):
    own_tokens = hidden_in[0]
    number_of_rows = own_tokens.shape[0]
    depth, kv_width = key_projection_weight.shape
    dp_size, ctx_size = lax.axis_size("dp"), lax.axis_size("ctx")
    chips = ctx_size // CORES
    my_index = lax.axis_index("ctx")
    core, chip = my_index % CORES, my_index // CORES
    plane = chip % 2
    half_width = kv_width // CORES
    ring = ring_order(dp_size)
    dp_index = lax.axis_index("dp")
    my_spot = jnp.where(dp_index % 2 == 0, dp_index // 2, dp_size - (dp_index + 1) // 2)

    def to_sibling(x):
        return lax.ppermute(x, "ctx", [(i, i ^ 1) for i in range(ctx_size)])

    def to_plane(x):
        return lax.ppermute(x, "ctx", [(i, i ^ CORES) for i in range(ctx_size)])

    def to_next_chip(x):
        return lax.ppermute(x, "ctx", [(i, i + CORES) for i in range(ctx_size - CORES)])

    def along_ring(x, step):
        return lax.ppermute(
            x, "dp", [(ring[i], ring[(i + step) % dp_size]) for i in range(dp_size)]
        )

    key_weight = lax.dynamic_slice_in_dim(key_projection_weight, core * half_width, half_width, 1)
    value_weight = lax.dynamic_slice_in_dim(
        value_projection_weight, core * half_width, half_width, 1
    )
    strip = depth // 2
    part = strip // 2
    key_strip = lax.dynamic_slice_in_dim(key_weight, plane * strip, strip, 0)
    sibling_tokens = to_sibling(own_tokens)

    def source_at(distance):
        spot = (my_spot + distance + dp_size) % dp_size
        return jnp.where(spot < dp_size // 2, 2 * spot, 2 * (dp_size - spot) - 1)

    half_ring = dp_size // 2

    arange = jnp.arange(number_of_rows, dtype=jnp.int32)
    positions = jnp.concatenate(
        [my_index * number_of_rows + arange, (my_index ^ 1) * number_of_rows + arange]
    )
    key_bias = lax.dynamic_slice_in_dim(key_projection_bias, core * half_width, half_width, 0)
    value_bias = lax.dynamic_slice_in_dim(value_projection_bias, core * half_width, half_width, 0)

    def projected(finish, strips, before, extras):
        pieces = []

        def operand(piece):
            for at, known in enumerate(pieces):
                if known is piece:
                    return at
            pieces.append(piece)
            return len(pieces) - 1

        plan = tuple(
            tuple((operand(piece), first_row) for piece, first_row in parts) for parts, _ in strips
        )
        columns = jnp.stack([at for _, at in strips]).astype(jnp.int32)
        return project(
            finish, strip, own_tokens, sibling_tokens, pieces, plan, columns, before, extras
        )

    def whole_strip(piece, first_row, at):
        return (((piece, first_row), (piece, first_row + part)), at)

    own_strips = [
        [whole_strip(weight, side * strip, dp_index * 2 + side) for side in range(2)]
        for weight in (key_weight, value_weight)
    ]
    sides = [plane, 1 - plane]
    key_strips = [own_strips[0]]
    travelling = {1: key_strip, -1: key_strip}
    for hop in range(1, half_ring + 1):
        arrived = {}
        for step in (1, -1):
            piece = travelling[step]
            if hop == half_ring:
                first_row = 0 if step == 1 else part
                piece = piece[first_row : first_row + part]
            piece = along_ring(piece, step)
            other = to_plane(piece)
            travelling[step] = piece
            arrived[step] = (piece, other)
        if hop < half_ring:
            key_strips.append(
                [
                    whole_strip(arrived[step][side], 0, source_at(-step * hop) * 2 + sides[side])
                    for step in (1, -1)
                    for side in range(2)
                ]
            )
        else:
            key_strips.append(
                [
                    (
                        ((arrived[1][side], 0), (arrived[-1][side], 0)),
                        source_at(hop) * 2 + sides[side],
                    )
                    for side in range(2)
                ]
            )

    value_strips = [own_strips[1]]
    travelling = {
        (side, step): value_weight[side * strip : (side + 1) * strip]
        for side in range(2)
        for step in (1, -1)
    }
    for hop in range(1, half_ring + 1):
        arrived = []
        for side in range(2):
            for step in (1, -1):
                if hop == half_ring and step != (1, -1)[side]:
                    continue
                piece = along_ring(travelling[side, step], step)
                travelling[side, step] = piece
                arrived.append(whole_strip(piece, 0, source_at(-step * hop) * 2 + side))
        value_strips.append(arrived)

    def joined(hops):
        return [entry for strips in hops for entry in strips]

    key_sum = projected("sum", joined(key_strips[:-2]), None, [])
    key_rows = projected(
        "key", joined(key_strips[-2:]), key_sum, [key_bias[None], *rope_tables(positions)]
    )
    value_sum = projected("sum", joined(value_strips[:-2]), None, [])
    value_sum = projected("sum", value_strips[-2], value_sum, [])
    value_rows = projected("value", value_strips[-1], value_sum, [value_bias[None]])

    keys, values = [key_rows], [value_rows]
    for _ in range(1, chips):
        keys.append(to_next_chip(keys[-1]))
        values.append(to_next_chip(values[-1]))
    sibling_keys = [to_sibling(x) for x in keys]
    sibling_values = [to_sibling(x) for x in values]

    def attention(half):
        facts = jnp.concatenate([jnp.stack([half, half, my_index]), block_segments[0]])
        return Attention(facts, queries[0], chips)

    near, far = attention(core), attention(1 - core)
    near_weights = near.scores(keys)
    far_weights = far.scores(sibling_keys)
    attended = near.mix(*near_weights, values, None)
    attended = far.mix(*far_weights, sibling_values, attended)
    return attended[None]


def solution(mesh):
    placed = (
        P("dp", "ctx", None),
        P("dp", "ctx", None),
        P("dp", None),
        P("dp", None),
        P(),
        P(),
        P("dp", None),
    )
    return jax.shard_map(
        layer, mesh=mesh, in_specs=placed, out_specs=P("dp", "ctx", None), check_vma=False
    )
```

```python
import functools
import math

import jax
import jax.numpy as jnp
from jax import lax
from jax.experimental import pallas as pl
from jax.experimental.pallas import tpu as pltpu
from jax.sharding import PartitionSpec as P


HEAD_SIZE = 128
KEY_VALUE_HEADS = 4
BLK = 128
MASKED = -1e30
CORES = 2
CHUNK = 2 * BLK
SPARE_VMEM = 4 << 20
MOST_VMEM = 67043328
LEFT_VMEM = 3 << 20

rope_base = 1000000.0


def ring_order(count):
    return list(range(0, count, 2)) + list(range(count - 1, 0, -2))


def rope_tables(token_positions):
    half_dim = HEAD_SIZE // 2
    frequency = rope_base ** (
        -(jnp.arange(half_dim, dtype=jnp.float32) * 2.0 / HEAD_SIZE)
    )
    angles = token_positions.astype(jnp.float32)[:, None] * frequency[None, :]
    cos_part, sine_part = jnp.cos(angles), jnp.sin(angles)
    return (
        jnp.concatenate([cos_part, cos_part], axis=1),
        jnp.concatenate([-sine_part, sine_part], axis=1),
    )


def project_kernel(plan, finish, added, columns, own_ref, sibling_ref, *refs):
    operands = 1 + max(part[0] for parts in plan for part in parts)
    piece_refs = refs[:operands]
    extra_refs = refs[operands:-6]
    out_ref, token_ref, weight_ref, acc_ref, token_sems, weight_sems = refs[-6:]
    number_of_rows, strip = own_ref.shape[0], weight_ref.shape[1]
    part_rows = strip // 2

    def token_copy(at, half):
        tokens_ref = (own_ref, sibling_ref)[half]
        return pltpu.make_async_copy(
            tokens_ref.at[:, pl.ds(pl.multiple_of(columns[at] * strip, strip), strip)],
            token_ref.at[at, pl.ds(half * number_of_rows, number_of_rows), :],
            token_sems.at[at, half],
        )

    def part_copy(operand, first_row, at, part):
        return pltpu.make_async_copy(
            piece_refs[operand].at[pl.ds(first_row, part_rows), :],
            weight_ref.at[at, pl.ds(part * part_rows, part_rows), :],
            weight_sems.at[at, part],
        )

    for at, parts in enumerate(plan):
        for part, (operand, first_row) in enumerate(parts):
            part_copy(operand, first_row, at, part).start()
        for half in range(2):
            token_copy(at, half).start()
    if added:
        acc_ref[...] = extra_refs[0][...]
        extra_refs = extra_refs[1:]
    else:
        acc_ref[...] = jnp.zeros_like(acc_ref)

    @pl.loop(0, len(plan) // 2)
    def _(pair):
        for at in (2 * pair, 2 * pair + 1):
            for half in range(2):
                part_copy(0, 0, at, half).wait()
                token_copy(at, half).wait()
        acc_ref[...] += jnp.dot(
            token_ref[2 * pair], weight_ref[2 * pair], preferred_element_type=jnp.float32
        ) + jnp.dot(
            token_ref[2 * pair + 1], weight_ref[2 * pair + 1], preferred_element_type=jnp.float32
        )

    if finish == "key":
        bias_ref, cos_ref, sine_ref = extra_refs
        for first in range(0, acc_ref.shape[1], HEAD_SIZE):
            lanes = slice(first, first + HEAD_SIZE)
            head = acc_ref[:, lanes] + bias_ref[:, lanes]
            turned = head * cos_ref[...] + pltpu.roll(head, HEAD_SIZE // 2, 1) * sine_ref[...]
            out_ref[:, lanes] = turned.astype(out_ref.dtype)
    elif finish == "value":
        out_ref[...] = (acc_ref[...] + extra_refs[0][...]).astype(out_ref.dtype)
    else:
        out_ref[...] = acc_ref[...].astype(out_ref.dtype)


def project(
    finish, strip, own_tokens, sibling_tokens, pieces, plan, columns, before, extras
):
    number_of_rows = own_tokens.shape[0]
    width = pieces[0].shape[1]
    anywhere = pl.BlockSpec(memory_space=pltpu.MemorySpace.HBM)
    chip_rows = CORES * number_of_rows
    out = jax.ShapeDtypeStruct(
        (chip_rows, width), jnp.float32 if finish == "sum" else jnp.bfloat16
    )
    added = before is not None
    if added:
        extras = [before, *extras]
    grant = MOST_VMEM - LEFT_VMEM
    return pl.pallas_call(
        functools.partial(project_kernel, plan, finish, added),
        out_shape=out,
        grid_spec=pltpu.PrefetchScalarGridSpec(
            num_scalar_prefetch=1,
            grid=(1,),
            in_specs=[anywhere] * (2 + len(pieces))
            + [pl.BlockSpec(x.shape, lambda p, b: (0, 0)) for x in extras],
            out_specs=pl.BlockSpec(out.shape, lambda p, b: (0, 0)),
            scratch_shapes=[
                pltpu.VMEM((len(plan), chip_rows, strip), jnp.bfloat16),
                pltpu.VMEM((len(plan), strip, width), jnp.bfloat16),
                pltpu.VMEM((chip_rows, width), jnp.float32),
                pltpu.SemaphoreType.DMA((len(plan), 2)),
                pltpu.SemaphoreType.DMA((len(plan), 2)),
            ],
        ),
        cost_estimate=pl.CostEstimate(
            flops=2 * len(plan) * strip * chip_rows * width,
            bytes_accessed=2 * len(plan) * strip * (chip_rows + width),
            transcendentals=0,
        ),
        compiler_params=pltpu.CompilerParams(vmem_limit_bytes=grant),
    )(columns, own_tokens, sibling_tokens, *pieces, *extras)


def partial_kernel(copies, shards, facts, own_ref, sibling_ref, *refs):
    piece_refs = refs[:-7]
    key_ref, value_ref, token_ref, weight_ref, acc_ref, token_sems, weight_sems = refs[-7:]
    number_of_rows, depth = own_ref.shape[0], weight_ref.shape[1]
    width = weight_ref.shape[2] // 2
    for operand, shard, first_row, side, lane in copies:
        piece_ref = piece_refs[operand]
        row = first_row
        if side >= 0:
            row = pl.multiple_of((facts[0] if side == 0 else 1 - facts[0]) * (depth // 2), depth // 2)
        pltpu.make_async_copy(
            piece_ref,
            weight_ref.at[shard, pl.ds(row, piece_ref.shape[0]), pl.ds(lane, width)],
            weight_sems.at[shard],
        ).start()
    for shard in range(shards):
        columns = pl.ds(pl.multiple_of(facts[1 + shard] * depth, depth), depth)
        for half, tokens_ref in enumerate((own_ref, sibling_ref)):
            pltpu.make_async_copy(
                tokens_ref.at[:, columns],
                token_ref.at[shard, pl.ds(half * number_of_rows, number_of_rows), :],
                token_sems.at[shard],
            ).start()
    acc_ref[...] = jnp.zeros_like(acc_ref)

    @pl.loop(0, shards)
    def _(shard):
        pltpu.make_async_copy(
            weight_ref.at[shard], weight_ref.at[shard], weight_sems.at[shard]
        ).wait()
        pltpu.make_async_copy(
            token_ref.at[shard], token_ref.at[shard], token_sems.at[shard]
        ).wait()
        acc_ref[...] += jnp.dot(
            token_ref[shard], weight_ref[shard], preferred_element_type=jnp.float32
        )

    key_ref[...] = acc_ref[:, :width]
    value_ref[...] = acc_ref[:, width:]


def project_partial(own_tokens, sibling_tokens, pieces, copies, sources, plane, depth):
    shards = len(sources)
    chip_rows = CORES * own_tokens.shape[0]
    width = pieces[0].shape[1]
    facts = jnp.stack([plane, *sources]).astype(jnp.int32)
    out = jax.ShapeDtypeStruct((chip_rows, width), jnp.float32)
    out_spec = pl.BlockSpec(out.shape, lambda p, b: (0, 0))
    anywhere = pl.BlockSpec(memory_space=pltpu.MemorySpace.HBM)
    return pl.pallas_call(
        functools.partial(partial_kernel, tuple(copies), shards),
        out_shape=(out, out),
        grid_spec=pltpu.PrefetchScalarGridSpec(
            num_scalar_prefetch=1,
            grid=(1,),
            in_specs=[anywhere] * (2 + len(pieces)),
            out_specs=(out_spec, out_spec),
            scratch_shapes=[
                pltpu.VMEM((shards, chip_rows, depth), jnp.bfloat16),
                pltpu.VMEM((shards, depth, 2 * width), jnp.bfloat16),
                pltpu.VMEM((chip_rows, 2 * width), jnp.float32),
                pltpu.SemaphoreType.DMA((shards,)),
                pltpu.SemaphoreType.DMA((shards,)),
            ],
        ),
        compiler_params=pltpu.CompilerParams(vmem_limit_bytes=MOST_VMEM - LEFT_VMEM),
        cost_estimate=pl.CostEstimate(
            flops=4 * shards * depth * chip_rows * width,
            bytes_accessed=2 * shards * depth * (chip_rows + 2 * width),
            transcendentals=0,
        ),
        name="project_partial",
    )(facts, own_tokens, sibling_tokens, *pieces)


class Blocks:
    def __init__(self, facts, hops, row_blocks, row_block):
        self.row_blocks, self.source_core = row_blocks, facts[1]
        per_chip = CORES * row_blocks
        chip = facts[2] // CORES
        here = facts[2] * row_blocks + row_block
        segment = facts[3 + here]
        self.diagonal = lax.rem(here, per_chip)
        self.entries, slot = [], jnp.int32(0)
        for hop in range(hops):
            for local in range(per_chip):
                block = (chip - hop) * per_chip + local
                seen = facts[3 + jnp.maximum(block, 0)]
                allowed = (block >= 0) & (block < here) & ((seen == 0) | (seen == segment))
                self.entries.append((hop, local, allowed, slot))
                slot = slot + jnp.where(allowed, 1, 0)
        self.odd = lax.rem(slot, 2) == 1
        self.free_slot = slot
        self.chunks = (slot + 2) // 2

    def place(self, local):
        core = local // self.row_blocks
        slot = jnp.where(core == self.source_core, 0, self.row_blocks)
        slot = slot + lax.rem(local, self.row_blocks)
        return pl.ds(pl.multiple_of(slot * BLK, BLK), BLK)

    def gather(self, refs, chosen_ref):
        def slot_rows(slot):
            return pl.ds(pl.multiple_of(slot * BLK, BLK), BLK)

        for hop, local, allowed, slot in self.entries:

            @pl.when(allowed)
            def _(hop=hop, local=local, slot=slot):
                chosen_ref[slot_rows(slot), :] = refs[hop][self.place(jnp.int32(local)), :]

        @pl.when(jnp.logical_not(self.odd))
        def _():
            chosen_ref[slot_rows(self.free_slot), :] = jnp.zeros((BLK, HEAD_SIZE), jnp.bfloat16)

        chosen_ref[slot_rows(2 * self.chunks - 1), :] = refs[0][self.place(self.diagonal), :]


def chunk_rows(chunk):
    return pl.ds(pl.multiple_of(chunk * CHUNK, CHUNK), CHUNK)


def find_scores(blocks, group, q_ref, key_ref, score_ref, peak_ref):
    rows = group * BLK

    def scores(chunk):
        heads = [q_ref[:, h * HEAD_SIZE : (h + 1) * HEAD_SIZE] for h in range(group)]
        return lax.dot_general(
            jnp.concatenate(heads, axis=0),
            key_ref[chunk_rows(chunk), :],
            (((1,), (1,)), ((), ())),
            preferred_element_type=jnp.float32,
        )

    last = blocks.chunks - 1
    column = lax.broadcasted_iota(jnp.int32, (rows, CHUNK), 1)
    row = lax.broadcasted_iota(jnp.int32, (rows, CHUNK), 0) % BLK
    first_column = jnp.where(blocks.odd, 0, BLK)
    found = jnp.where(
        (column >= first_column) & (column - BLK <= row), scores(last), MASKED
    )
    score_ref[last] = found
    peak_ref[...] = jnp.maximum(found[:, :BLK], found[:, BLK:])

    @pl.loop(0, last)
    def _(chunk):
        found = scores(chunk)
        score_ref[chunk] = found
        peak_ref[...] = jnp.maximum(
            peak_ref[...], jnp.maximum(found[:, :BLK], found[:, BLK:])
        )

    peak_ref[...] = jnp.broadcast_to(
        jnp.max(peak_ref[...], axis=1, keepdims=True), (rows, BLK)
    )


def weights_of(chunk, score_ref, peak_ref, total_ref):
    factor = math.log2(math.e) / math.sqrt(HEAD_SIZE)
    peak, total, halves = peak_ref[...], total_ref[...], []
    for first in range(0, CHUNK, BLK):
        probs = jnp.exp2((score_ref[chunk, :, first : first + BLK] - peak) * factor)
        halves.append(probs.astype(jnp.bfloat16))
        total = total + probs
    total_ref[...] = total
    return halves


def score_kernel(hops, row_blocks, group, facts, q_ref, *refs):
    k_refs = refs[:hops]
    probs_ref, inverse_ref, key_ref, score_ref, peak_ref, total_ref = refs[hops:]
    blocks = Blocks(facts, hops, row_blocks, pl.program_id(1))
    blocks.gather(k_refs, key_ref)
    find_scores(blocks, group, q_ref, key_ref, score_ref, peak_ref)
    total_ref[...] = jnp.zeros_like(total_ref)

    @pl.loop(0, blocks.chunks)
    def _(chunk):
        halves = weights_of(chunk, score_ref, peak_ref, total_ref)
        for at, half in enumerate(halves):
            probs_ref[0, chunk, :, at * BLK : (at + 1) * BLK] = half

    inverse_ref[0] = jnp.broadcast_to(
        1.0 / jnp.sum(total_ref[...], axis=1, keepdims=True), (group * BLK, BLK)
    )


def attend_kernel(hops, row_blocks, group, facts, q_ref, *refs):
    k_refs, v_refs = refs[:hops], refs[hops : 2 * hops]
    out_ref, key_ref, value_ref, score_ref, peak_ref, total_ref, acc_ref = refs[-7:]
    blocks = Blocks(facts, hops, row_blocks, pl.program_id(1))
    blocks.gather(k_refs, key_ref)
    find_scores(blocks, group, q_ref, key_ref, score_ref, peak_ref)
    blocks.gather(v_refs, value_ref)
    total_ref[...] = jnp.zeros_like(total_ref)
    acc_ref[...] = jnp.zeros_like(acc_ref)

    @pl.loop(0, blocks.chunks)
    def _(chunk):
        halves = weights_of(chunk, score_ref, peak_ref, total_ref)
        acc_ref[...] += jnp.dot(
            jnp.concatenate(halves, axis=1),
            value_ref[chunk_rows(chunk), :],
            preferred_element_type=jnp.float32,
        )

    mixed = (acc_ref[...] / jnp.sum(total_ref[...], axis=1, keepdims=True)).astype(out_ref.dtype)
    for h in range(group):
        out_ref[:, h * HEAD_SIZE : (h + 1) * HEAD_SIZE] = mixed[h * BLK : (h + 1) * BLK]


def mix_kernel(hops, row_blocks, group, facts, probs_ref, inverse_ref, *refs):
    v_refs = refs[:hops]
    out_ref, chosen_ref, held_ref, acc_ref, sems = refs[-5:]
    head, row_block = pl.program_id(0), pl.program_id(1)
    step = head * row_blocks + row_block
    steps = pl.num_programs(0) * row_blocks
    blocks = Blocks(facts, hops, row_blocks, row_block)

    def fetch(at, chunk):
        side = lax.rem(at, 2)
        return pltpu.make_async_copy(
            probs_ref.at[at, chunk], held_ref.at[side, chunk], sems.at[side, chunk]
        )

    @pl.when(step == 0)
    def _():
        @pl.loop(0, blocks.chunks)
        def _(chunk):
            fetch(step, chunk).start()

    @pl.when(step + 1 < steps)
    def _():
        coming = Blocks(facts, hops, row_blocks, lax.rem(row_block + 1, row_blocks))

        @pl.loop(0, coming.chunks)
        def _(chunk):
            fetch(step + 1, chunk).start()

    blocks.gather(v_refs, chosen_ref)
    acc_ref[...] = jnp.zeros_like(acc_ref)

    @pl.loop(0, blocks.chunks)
    def _(chunk):
        fetch(step, chunk).wait()
        acc_ref[...] += jnp.dot(
            held_ref[lax.rem(step, 2), chunk],
            chosen_ref[chunk_rows(chunk), :],
            preferred_element_type=jnp.float32,
        )

    mixed = (acc_ref[...] * inverse_ref[0]).astype(out_ref.dtype)
    for h in range(group):
        out_ref[:, h * HEAD_SIZE : (h + 1) * HEAD_SIZE] = mixed[h * BLK : (h + 1) * BLK]


class Attention:
    def __init__(self, facts, queries, hops):
        self.facts, self.queries, self.hops = facts, queries, hops
        self.rows, query_width = queries.shape
        self.group = query_width // HEAD_SIZE // KEY_VALUE_HEADS
        self.heads = KEY_VALUE_HEADS // CORES
        self.row_blocks = self.rows // BLK
        self.stacked = self.group * BLK
        self.chunks = hops * CORES * self.row_blocks * BLK // CHUNK
        self.q_spec = pl.BlockSpec(
            (BLK, self.group * HEAD_SIZE), lambda l, r, f: (r, f[0] * self.heads + l)
        )
        self.kv_spec = pl.BlockSpec((CORES * self.rows, HEAD_SIZE), lambda l, r, f: (0, l))
        self.inverse_spec = pl.BlockSpec(
            (1, self.stacked, BLK), lambda l, r, f: (l * self.row_blocks + r, 0, 0)
        )
        self.pairs = self.heads * self.row_blocks * self.stacked * self.chunks * CHUNK // 2
        count = self.heads * self.row_blocks
        block_bytes = self.stacked * BLK * 4
        kept = block_bytes * count * (self.chunks + 1) + (2 << 20)
        self.grant = max(MOST_VMEM - kept, block_bytes * (4 * self.chunks + 8) + SPARE_VMEM)

    def scores(self, keys):
        count = self.heads * self.row_blocks
        probs = jax.ShapeDtypeStruct(
            (count, self.chunks, self.stacked, CHUNK), jnp.bfloat16
        )
        return pl.pallas_call(
            functools.partial(score_kernel, self.hops, self.row_blocks, self.group),
            out_shape=(
                probs,
                jax.ShapeDtypeStruct((count, self.stacked, BLK), jnp.float32),
            ),
            grid_spec=pltpu.PrefetchScalarGridSpec(
                num_scalar_prefetch=1,
                grid=(self.heads, self.row_blocks),
                in_specs=[self.q_spec] + [self.kv_spec] * self.hops,
                out_specs=(
                    pl.BlockSpec(
                        (1, *probs.shape[1:]), lambda l, r, f: (l * self.row_blocks + r, 0, 0, 0)
                    ),
                    self.inverse_spec,
                ),
                scratch_shapes=[
                    pltpu.VMEM((self.chunks * CHUNK, HEAD_SIZE), jnp.bfloat16),
                    pltpu.VMEM((self.chunks, self.stacked, CHUNK), jnp.float32),
                    pltpu.VMEM((self.stacked, BLK), jnp.float32),
                    pltpu.VMEM((self.stacked, BLK), jnp.float32),
                ],
            ),
            compiler_params=pltpu.CompilerParams(
                vmem_limit_bytes=self.grant
            ),
            cost_estimate=pl.CostEstimate(
                flops=2 * self.pairs * HEAD_SIZE,
                bytes_accessed=self.queries.size + self.pairs * 4,
                transcendentals=self.pairs,
            ),
            name="score",
        )(self.facts, self.queries, *keys)

    def attend(self, keys, values, before):
        operands = [self.facts, self.queries, *keys, *values]
        in_specs = [self.q_spec] + [self.kv_spec] * (2 * self.hops)
        aliases = {}
        if before is not None:
            aliases = {len(operands): 0}
            operands.append(before)
            in_specs.append(pl.BlockSpec(memory_space=pl.ANY))
        chosen = pltpu.VMEM((self.chunks * CHUNK, HEAD_SIZE), jnp.bfloat16)
        tall = pltpu.VMEM((self.stacked, BLK), jnp.float32)
        return pl.pallas_call(
            functools.partial(attend_kernel, self.hops, self.row_blocks, self.group),
            out_shape=jax.ShapeDtypeStruct(self.queries.shape, self.queries.dtype),
            grid_spec=pltpu.PrefetchScalarGridSpec(
                num_scalar_prefetch=1,
                grid=(self.heads, self.row_blocks),
                in_specs=in_specs,
                out_specs=self.q_spec,
                scratch_shapes=[
                    chosen,
                    chosen,
                    pltpu.VMEM((self.chunks, self.stacked, CHUNK), jnp.float32),
                    tall,
                    tall,
                    tall,
                ],
            ),
            input_output_aliases=aliases,
            compiler_params=pltpu.CompilerParams(
                vmem_limit_bytes=MOST_VMEM - LEFT_VMEM
            ),
            cost_estimate=pl.CostEstimate(
                flops=4 * self.pairs * HEAD_SIZE,
                bytes_accessed=2 * self.queries.size,
                transcendentals=self.pairs,
            ),
            name="attend",
        )(*operands)

    def mix(self, probs, inverse, values, before):
        operands = [self.facts, probs, inverse, *values]
        in_specs = [pl.BlockSpec(memory_space=pl.ANY), self.inverse_spec]
        in_specs += [self.kv_spec] * self.hops
        aliases = {}
        if before is not None:
            aliases = {len(operands): 0}
            operands.append(before)
            in_specs.append(pl.BlockSpec(memory_space=pl.ANY))
        return pl.pallas_call(
            functools.partial(mix_kernel, self.hops, self.row_blocks, self.group),
            out_shape=jax.ShapeDtypeStruct(self.queries.shape, self.queries.dtype),
            grid_spec=pltpu.PrefetchScalarGridSpec(
                num_scalar_prefetch=1,
                grid=(self.heads, self.row_blocks),
                in_specs=in_specs,
                out_specs=self.q_spec,
                scratch_shapes=[
                    pltpu.VMEM((self.chunks * CHUNK, HEAD_SIZE), jnp.bfloat16),
                    pltpu.VMEM((2, *probs.shape[1:]), jnp.bfloat16),
                    pltpu.VMEM((self.stacked, HEAD_SIZE), jnp.float32),
                    pltpu.SemaphoreType.DMA((2, self.chunks)),
                ],
            ),
            input_output_aliases=aliases,
            compiler_params=pltpu.CompilerParams(
                vmem_limit_bytes=self.grant
            ),
            cost_estimate=pl.CostEstimate(
                flops=2 * self.pairs * HEAD_SIZE,
                bytes_accessed=self.queries.size + self.pairs * 4,
                transcendentals=0,
            ),
            name="mix",
        )(*operands)


def layer(
    hidden_in,
    queries,
    key_projection_weight,
    value_projection_weight,
    key_projection_bias,
    value_projection_bias,
    block_segments,
):
    own_tokens = hidden_in[0]
    number_of_rows = own_tokens.shape[0]
    depth, kv_width = key_projection_weight.shape
    dp_size, ctx_size = lax.axis_size("dp"), lax.axis_size("ctx")
    chips = ctx_size // CORES
    my_index = lax.axis_index("ctx")
    core, chip = my_index % CORES, my_index // CORES
    plane = chip % 2
    half_width = kv_width // CORES
    ring = ring_order(dp_size)
    dp_index = lax.axis_index("dp")
    my_spot = jnp.where(dp_index % 2 == 0, dp_index // 2, dp_size - (dp_index + 1) // 2)

    def to_sibling(x):
        return lax.ppermute(x, "ctx", [(i, i ^ 1) for i in range(ctx_size)])

    def to_plane(x):
        return lax.ppermute(x, "ctx", [(i, i ^ CORES) for i in range(ctx_size)])

    def to_next_chip(x):
        return lax.ppermute(x, "ctx", [(i, i + CORES) for i in range(ctx_size - CORES)])

    def along_ring(x, step):
        return lax.ppermute(
            x, "dp", [(ring[i], ring[(i + step) % dp_size]) for i in range(dp_size)]
        )

    key_weight = lax.dynamic_slice_in_dim(key_projection_weight, core * half_width, half_width, 1)
    value_weight = lax.dynamic_slice_in_dim(
        value_projection_weight, core * half_width, half_width, 1
    )
    strip = depth // 2
    part = strip // 2
    key_strip = lax.dynamic_slice_in_dim(key_weight, plane * strip, strip, 0)
    sibling_tokens = to_sibling(own_tokens)

    def source_at(distance):
        spot = (my_spot + distance + dp_size) % dp_size
        return jnp.where(spot < dp_size // 2, 2 * spot, 2 * (dp_size - spot) - 1)

    half_ring = dp_size // 2

    arange = jnp.arange(number_of_rows, dtype=jnp.int32)
    positions = jnp.concatenate(
        [my_index * number_of_rows + arange, (my_index ^ 1) * number_of_rows + arange]
    )
    key_bias = lax.dynamic_slice_in_dim(key_projection_bias, core * half_width, half_width, 0)
    value_bias = lax.dynamic_slice_in_dim(value_projection_bias, core * half_width, half_width, 0)

    def projected(finish, strips, before, extras):
        pieces = []

        def operand(piece):
            for at, known in enumerate(pieces):
                if known is piece:
                    return at
            pieces.append(piece)
            return len(pieces) - 1

        plan = tuple(
            tuple((operand(piece), first_row) for piece, first_row in parts) for parts, _ in strips
        )
        columns = jnp.stack([at for _, at in strips]).astype(jnp.int32)
        return project(
            finish, strip, own_tokens, sibling_tokens, pieces, plan, columns, before, extras
        )

    def whole_strip(piece, first_row, at):
        return (((piece, first_row), (piece, first_row + part)), at)

    own_strips = [
        [whole_strip(weight, side * strip, dp_index * 2 + side) for side in range(2)]
        for weight in (key_weight, value_weight)
    ]
    sides = [plane, 1 - plane]
    key_arrived, value_arrived = {}, {}
    key_strips = [own_strips[0]]
    travelling = {1: key_strip, -1: key_strip}
    for hop in range(1, half_ring + 1):
        arrived = {}
        for step in (1, -1):
            piece = travelling[step]
            if hop == half_ring:
                first_row = 0 if step == 1 else part
                piece = piece[first_row : first_row + part]
            piece = along_ring(piece, step)
            other = to_plane(piece)
            travelling[step] = piece
            arrived[step] = (piece, other)
            key_arrived[hop, step] = (piece, other)
        if hop < half_ring:
            key_strips.append(
                [
                    whole_strip(arrived[step][side], 0, source_at(-step * hop) * 2 + sides[side])
                    for step in (1, -1)
                    for side in range(2)
                ]
            )
        else:
            key_strips.append(
                [
                    (
                        ((arrived[1][side], 0), (arrived[-1][side], 0)),
                        source_at(hop) * 2 + sides[side],
                    )
                    for side in range(2)
                ]
            )

    value_strips = [own_strips[1]]
    travelling = {
        (side, step): value_weight[side * strip : (side + 1) * strip]
        for side in range(2)
        for step in (1, -1)
    }
    for hop in range(1, half_ring + 1):
        arrived = []
        for side in range(2):
            for step in (1, -1):
                if hop == half_ring and step != (1, -1)[side]:
                    continue
                piece = along_ring(travelling[side, step], step)
                travelling[side, step] = piece
                value_arrived[hop, step, side] = piece
                arrived.append(whole_strip(piece, 0, source_at(-step * hop) * 2 + side))
        value_strips.append(arrived)

    def joined(hops):
        return [entry for strips in hops for entry in strips]

    early = half_ring - 2
    sources = [source_at(distance) for distance in range(-early, early + 1)]
    pieces, copies = [key_weight, value_weight], [(0, early, 0, -1, 0), (1, early, 0, -1, half_width)]
    for hop in range(1, early + 1):
        for step in (1, -1):
            shard = early - step * hop
            for side, piece in enumerate(key_arrived[hop, step]):
                copies.append((len(pieces), shard, 0, side, 0))
                pieces.append(piece)
            for side in range(2):
                copies.append((len(pieces), shard, side * strip, -1, half_width))
                pieces.append(value_arrived[hop, step, side])
    key_sum, value_sum = project_partial(
        own_tokens, sibling_tokens, pieces, copies, sources, plane, depth
    )
    key_rows = projected(
        "key", joined(key_strips[-2:]), key_sum, [key_bias[None], *rope_tables(positions)]
    )
    value_sum = projected("sum", value_strips[-2], value_sum, [])
    value_rows = projected("value", value_strips[-1], value_sum, [value_bias[None]])

    keys, values = [key_rows], [value_rows]
    for _ in range(1, chips):
        keys.append(to_next_chip(keys[-1]))
        values.append(to_next_chip(values[-1]))
    sibling_keys = [to_sibling(x) for x in keys]
    sibling_values = [to_sibling(x) for x in values]

    def attention(half):
        facts = jnp.concatenate([jnp.stack([half, half, my_index]), block_segments[0]])
        return Attention(facts, queries[0], chips)

    near, far = attention(core), attention(1 - core)
    near_weights = near.scores(keys)
    attended = near.mix(*near_weights, values, None)
    attended = far.attend(sibling_keys, sibling_values, attended)
    return attended[None]


def solution(mesh):
    placed = (
        P("dp", "ctx", None),
        P("dp", "ctx", None),
        P("dp", None),
        P("dp", None),
        P(),
        P(),
        P("dp", None),
    )
    return jax.shard_map(
        layer, mesh=mesh, in_specs=placed, out_specs=P("dp", "ctx", None), check_vma=False
    )
```

```python
import functools
import math

import jax
import jax.numpy as jnp
from jax import lax
from jax.experimental import pallas as pl
from jax.experimental.pallas import tpu as pltpu
from jax.sharding import PartitionSpec as P


HEAD_SIZE = 128
KEY_VALUE_HEADS = 4
BLK = 128
MASKED = -1e30
CORES = 2
CHUNK = 2 * BLK
MOST_VMEM = 67043328
LEFT_VMEM = 3 << 20

rope_base = 1000000.0


def ring_order(count):
    return list(range(0, count, 2)) + list(range(count - 1, 0, -2))


def rope_tables(token_positions):
    half_dim = HEAD_SIZE // 2
    frequency = rope_base ** (
        -(jnp.arange(half_dim, dtype=jnp.float32) * 2.0 / HEAD_SIZE)
    )
    angles = token_positions.astype(jnp.float32)[:, None] * frequency[None, :]
    cos_part, sine_part = jnp.cos(angles), jnp.sin(angles)
    return jnp.concatenate([cos_part, cos_part, -sine_part, sine_part], axis=1)


def main_kernel(copies, early, late, facts, own_ref, sibling_ref, bias_hbm, table_hbm, *refs):
    piece_refs = refs[:-10]
    key_ref, value_ref, token_ref, weight_ref, acc_ref = refs[-10:-5]
    bias_ref, table_ref, token_sems, weight_sems, other_sems = refs[-5:]
    number_of_rows, depth = own_ref.shape[0], weight_ref.shape[1]
    width = weight_ref.shape[2] // 2
    strip = depth // 2
    others = [
        pltpu.make_async_copy(bias_hbm, bias_ref, other_sems.at[0]),
        pltpu.make_async_copy(table_hbm, table_ref, other_sems.at[1]),
    ]
    for shard in range(early + late):
        for operand, at, side, offset, lane in copies:
            if at != shard:
                continue
            row = offset
            if side >= 0:
                plane = facts[0] if side == 0 else 1 - facts[0]
                row = pl.multiple_of(plane * strip + offset, strip // 2)
            pltpu.make_async_copy(
                piece_refs[operand],
                weight_ref.at[
                    shard, pl.ds(row, piece_refs[operand].shape[0]), pl.ds(lane, width)
                ],
                weight_sems.at[shard],
            ).start()
        columns = pl.ds(pl.multiple_of(facts[1 + shard] * depth, depth), depth)
        for half, tokens_ref in enumerate((own_ref, sibling_ref)):
            pltpu.make_async_copy(
                tokens_ref.at[:, columns],
                token_ref.at[shard, pl.ds(half * number_of_rows, number_of_rows), :],
                token_sems.at[shard],
            ).start()
    for copy in others:
        copy.start()
    acc_ref[...] = jnp.zeros_like(acc_ref)

    def add_shard(shard, lanes):
        strips = weight_ref.at[shard, :, pl.ds(0, lanes)]
        pltpu.make_async_copy(strips, strips, weight_sems.at[shard]).wait()
        pltpu.make_async_copy(
            token_ref.at[shard], token_ref.at[shard], token_sems.at[shard]
        ).wait()
        acc_ref[:, :lanes] += jnp.dot(
            token_ref[shard], weight_ref[shard, :, :lanes], preferred_element_type=jnp.float32
        )

    @pl.loop(0, early)
    def _(shard):
        add_shard(shard, 2 * width)

    for copy in others:
        copy.wait()
    value_ref[...] = acc_ref[:, width:] + bias_ref[:, width:]

    @pl.loop(early, early + late)
    def _(shard):
        add_shard(shard, width)

    for first in range(0, width, HEAD_SIZE):
        lanes = slice(first, first + HEAD_SIZE)
        head = acc_ref[:, lanes] + bias_ref[:, lanes]
        turned = head * table_ref[:, :HEAD_SIZE]
        turned += pltpu.roll(head, HEAD_SIZE // 2, 1) * table_ref[:, HEAD_SIZE:]
        key_ref[:, lanes] = turned.astype(key_ref.dtype)


def project_main(own_tokens, sibling_tokens, bias, table, pieces, copies, sources, early, plane):
    shards = len(sources)
    depth = own_tokens.shape[1] // shards
    chip_rows = CORES * own_tokens.shape[0]
    width = pieces[0].shape[1]
    facts = jnp.stack([plane, *sources]).astype(jnp.int32)
    out_spec = pl.BlockSpec((chip_rows, width), lambda p, b: (0, 0))
    anywhere = pl.BlockSpec(memory_space=pltpu.MemorySpace.HBM)
    return pl.pallas_call(
        functools.partial(main_kernel, tuple(copies), early, shards - early),
        out_shape=(
            jax.ShapeDtypeStruct((chip_rows, width), jnp.bfloat16),
            jax.ShapeDtypeStruct((chip_rows, width), jnp.float32),
        ),
        grid_spec=pltpu.PrefetchScalarGridSpec(
            num_scalar_prefetch=1,
            grid=(1,),
            in_specs=[anywhere] * (4 + len(pieces)),
            out_specs=(out_spec, out_spec),
            scratch_shapes=[
                pltpu.VMEM((shards, chip_rows, depth), jnp.bfloat16),
                pltpu.VMEM((shards, depth, 2 * width), jnp.bfloat16),
                pltpu.VMEM((chip_rows, 2 * width), jnp.float32),
                pltpu.VMEM(bias.shape, jnp.float32),
                pltpu.VMEM(table.shape, jnp.float32),
                pltpu.SemaphoreType.DMA((shards,)),
                pltpu.SemaphoreType.DMA((shards,)),
                pltpu.SemaphoreType.DMA((2,)),
            ],
        ),
        compiler_params=pltpu.CompilerParams(vmem_limit_bytes=MOST_VMEM - LEFT_VMEM),
        cost_estimate=pl.CostEstimate(
            flops=2 * (shards + early) * depth * chip_rows * width,
            bytes_accessed=2 * shards * depth * (chip_rows + width),
            transcendentals=0,
        ),
        name="project_main",
    )(facts, own_tokens, sibling_tokens, bias, table, *pieces)


class Blocks:
    def __init__(self, facts, hops, row_blocks, row_block):
        self.row_blocks, self.source_core = row_blocks, facts[1]
        per_chip = CORES * row_blocks
        chip = facts[2] // CORES
        here = facts[2] * row_blocks + row_block
        segment = facts[3 + here]
        self.diagonal = lax.rem(here, per_chip)
        self.entries, slot = [], jnp.int32(0)
        for hop in range(hops):
            for local in range(per_chip):
                block = (chip - hop) * per_chip + local
                seen = facts[3 + jnp.maximum(block, 0)]
                allowed = (block >= 0) & (block < here) & ((seen == 0) | (seen == segment))
                self.entries.append((hop, local, allowed, slot))
                slot = slot + jnp.where(allowed, 1, 0)
        self.odd = lax.rem(slot, 2) == 1
        self.free_slot = slot
        self.chunks = (slot + 2) // 2

    def place(self, local):
        core = local // self.row_blocks
        slot = jnp.where(core == self.source_core, 0, self.row_blocks)
        slot = slot + lax.rem(local, self.row_blocks)
        return pl.ds(pl.multiple_of(slot * BLK, BLK), BLK)

    def gather(self, refs, chosen_ref):
        def slot_rows(slot):
            return pl.ds(pl.multiple_of(slot * BLK, BLK), BLK)

        for hop, local, allowed, slot in self.entries:

            @pl.when(allowed)
            def _(hop=hop, local=local, slot=slot):
                chosen_ref[slot_rows(slot), :] = refs[hop][self.place(jnp.int32(local)), :]

        @pl.when(jnp.logical_not(self.odd))
        def _():
            chosen_ref[slot_rows(self.free_slot), :] = jnp.zeros((BLK, HEAD_SIZE), jnp.bfloat16)

        chosen_ref[slot_rows(2 * self.chunks - 1), :] = refs[0][self.place(self.diagonal), :]


def chunk_rows(chunk):
    return pl.ds(pl.multiple_of(chunk * CHUNK, CHUNK), CHUNK)


def find_scores(blocks, group, q_ref, key_ref, score_ref, peak_ref):
    rows = group * BLK

    def scores(chunk):
        heads = [q_ref[:, h * HEAD_SIZE : (h + 1) * HEAD_SIZE] for h in range(group)]
        return lax.dot_general(
            jnp.concatenate(heads, axis=0),
            key_ref[chunk_rows(chunk), :],
            (((1,), (1,)), ((), ())),
            preferred_element_type=jnp.float32,
        )

    last = blocks.chunks - 1
    column = lax.broadcasted_iota(jnp.int32, (rows, CHUNK), 1)
    row = lax.broadcasted_iota(jnp.int32, (rows, CHUNK), 0) % BLK
    first_column = jnp.where(blocks.odd, 0, BLK)
    found = jnp.where(
        (column >= first_column) & (column - BLK <= row), scores(last), MASKED
    )
    score_ref[last] = found
    peak_ref[...] = jnp.maximum(found[:, :BLK], found[:, BLK:])

    @pl.loop(0, last)
    def _(chunk):
        found = scores(chunk)
        score_ref[chunk] = found
        peak_ref[...] = jnp.maximum(
            peak_ref[...], jnp.maximum(found[:, :BLK], found[:, BLK:])
        )

    peak_ref[...] = jnp.broadcast_to(
        jnp.max(peak_ref[...], axis=1, keepdims=True), (rows, BLK)
    )


def weights_of(chunk, score_ref, peak_ref, total_ref):
    factor = math.log2(math.e) / math.sqrt(HEAD_SIZE)
    peak, total, halves = peak_ref[...], total_ref[...], []
    for first in range(0, CHUNK, BLK):
        probs = jnp.exp2((score_ref[chunk, :, first : first + BLK] - peak) * factor)
        halves.append(probs.astype(jnp.bfloat16))
        total = total + probs
    total_ref[...] = total
    return halves


def attend_kernel(hops, row_blocks, group, facts, q_ref, *refs):
    k_refs, v_refs = refs[:hops], refs[hops : 2 * hops]
    out_ref, key_ref, value_ref, score_ref, peak_ref, total_ref, acc_ref = refs[-7:]
    blocks = Blocks(facts, hops, row_blocks, pl.program_id(1))
    blocks.gather(k_refs, key_ref)
    find_scores(blocks, group, q_ref, key_ref, score_ref, peak_ref)
    blocks.gather(v_refs, value_ref)
    total_ref[...] = jnp.zeros_like(total_ref)
    acc_ref[...] = jnp.zeros_like(acc_ref)

    @pl.loop(0, blocks.chunks)
    def _(chunk):
        halves = weights_of(chunk, score_ref, peak_ref, total_ref)
        acc_ref[...] += jnp.dot(
            jnp.concatenate(halves, axis=1),
            value_ref[chunk_rows(chunk), :],
            preferred_element_type=jnp.float32,
        )

    mixed = (acc_ref[...] / jnp.sum(total_ref[...], axis=1, keepdims=True)).astype(out_ref.dtype)
    for h in range(group):
        out_ref[:, h * HEAD_SIZE : (h + 1) * HEAD_SIZE] = mixed[h * BLK : (h + 1) * BLK]


class Attention:
    def __init__(self, facts, queries, hops):
        self.facts, self.queries, self.hops = facts, queries, hops
        self.rows, query_width = queries.shape
        self.group = query_width // HEAD_SIZE // KEY_VALUE_HEADS
        self.heads = KEY_VALUE_HEADS // CORES
        self.row_blocks = self.rows // BLK
        self.stacked = self.group * BLK
        self.chunks = hops * CORES * self.row_blocks * BLK // CHUNK
        self.q_spec = pl.BlockSpec(
            (BLK, self.group * HEAD_SIZE), lambda l, r, f: (r, f[0] * self.heads + l)
        )
        self.kv_spec = pl.BlockSpec((CORES * self.rows, HEAD_SIZE), lambda l, r, f: (0, l))
        self.pairs = self.heads * self.row_blocks * self.stacked * self.chunks * CHUNK // 2

    def attend(self, keys, values, before):
        operands = [self.facts, self.queries, *keys, *values]
        in_specs = [self.q_spec] + [self.kv_spec] * (2 * self.hops)
        aliases = {}
        if before is not None:
            aliases = {len(operands): 0}
            operands.append(before)
            in_specs.append(pl.BlockSpec(memory_space=pl.ANY))
        chosen = pltpu.VMEM((self.chunks * CHUNK, HEAD_SIZE), jnp.bfloat16)
        tall = pltpu.VMEM((self.stacked, BLK), jnp.float32)
        return pl.pallas_call(
            functools.partial(attend_kernel, self.hops, self.row_blocks, self.group),
            out_shape=jax.ShapeDtypeStruct(self.queries.shape, self.queries.dtype),
            grid_spec=pltpu.PrefetchScalarGridSpec(
                num_scalar_prefetch=1,
                grid=(self.heads, self.row_blocks),
                in_specs=in_specs,
                out_specs=self.q_spec,
                scratch_shapes=[
                    chosen,
                    chosen,
                    pltpu.VMEM((self.chunks, self.stacked, CHUNK), jnp.float32),
                    tall,
                    tall,
                    tall,
                ],
            ),
            input_output_aliases=aliases,
            compiler_params=pltpu.CompilerParams(
                vmem_limit_bytes=MOST_VMEM - LEFT_VMEM
            ),
            cost_estimate=pl.CostEstimate(
                flops=4 * self.pairs * HEAD_SIZE,
                bytes_accessed=2 * self.queries.size,
                transcendentals=self.pairs,
            ),
            name="attend",
        )(*operands)


def layer(
    hidden_in,
    queries,
    key_projection_weight,
    value_projection_weight,
    key_projection_bias,
    value_projection_bias,
    block_segments,
):
    own_tokens = hidden_in[0]
    number_of_rows = own_tokens.shape[0]
    depth, kv_width = key_projection_weight.shape
    dp_size, ctx_size = lax.axis_size("dp"), lax.axis_size("ctx")
    chips = ctx_size // CORES
    my_index = lax.axis_index("ctx")
    core, chip = my_index % CORES, my_index // CORES
    plane = chip % 2
    half_width = kv_width // CORES
    ring = ring_order(dp_size)
    dp_index = lax.axis_index("dp")
    my_spot = jnp.where(dp_index % 2 == 0, dp_index // 2, dp_size - (dp_index + 1) // 2)

    def to_sibling(x):
        return lax.ppermute(x, "ctx", [(i, i ^ 1) for i in range(ctx_size)])

    def to_plane(x):
        return lax.ppermute(x, "ctx", [(i, i ^ CORES) for i in range(ctx_size)])

    def to_next_chip(x):
        return lax.ppermute(x, "ctx", [(i, i + CORES) for i in range(ctx_size - CORES)])

    def along_ring(x, step):
        return lax.ppermute(
            x, "dp", [(ring[i], ring[(i + step) % dp_size]) for i in range(dp_size)]
        )

    key_weight = lax.dynamic_slice_in_dim(key_projection_weight, core * half_width, half_width, 1)
    value_weight = lax.dynamic_slice_in_dim(
        value_projection_weight, core * half_width, half_width, 1
    )
    strip = depth // 2
    part = strip // 2
    key_strip = lax.dynamic_slice_in_dim(key_weight, plane * strip, strip, 0)
    sibling_tokens = to_sibling(own_tokens)

    def source_at(distance):
        spot = (my_spot + distance + dp_size) % dp_size
        return jnp.where(spot < dp_size // 2, 2 * spot, 2 * (dp_size - spot) - 1)

    half_ring = dp_size // 2

    arange = jnp.arange(number_of_rows, dtype=jnp.int32)
    positions = jnp.concatenate(
        [my_index * number_of_rows + arange, (my_index ^ 1) * number_of_rows + arange]
    )
    key_bias = lax.dynamic_slice_in_dim(key_projection_bias, core * half_width, half_width, 0)
    value_bias = lax.dynamic_slice_in_dim(value_projection_bias, core * half_width, half_width, 0)

    key_arrived, value_arrived = {}, {}
    travelling = {1: key_strip, -1: key_strip}
    for hop in range(1, half_ring + 1):
        for step in (1, -1):
            piece = travelling[step]
            if hop == half_ring:
                first_row = 0 if step == 1 else part
                piece = piece[first_row : first_row + part]
            piece = along_ring(piece, step)
            other = to_plane(piece)
            travelling[step] = piece
            key_arrived[hop, step] = (piece, other)

    travelling = {
        (side, step): value_weight[side * strip : (side + 1) * strip]
        for side in range(2)
        for step in (1, -1)
    }
    for hop in range(1, half_ring + 1):
        for side in range(2):
            for step in (1, -1):
                if hop == half_ring and step != (1, -1)[side]:
                    continue
                piece = along_ring(travelling[side, step], step)
                travelling[side, step] = piece
                value_arrived[hop, step, side] = piece

    early = half_ring - 2
    distances = list(range(-early, early + 1)) + [-half_ring + 1, half_ring - 1, half_ring]
    pieces = [key_weight, value_weight]
    copies = [(0, early, -1, 0, 0), (1, early, -1, 0, half_width)]
    for hop in range(1, half_ring + 1):
        for step in (1, -1):
            shard = distances.index(half_ring if hop == half_ring else -step * hop)
            offset = part if hop == half_ring and step == -1 else 0
            for side, piece in enumerate(key_arrived[hop, step]):
                copies.append((len(pieces), shard, side, offset, 0))
                pieces.append(piece)
            if hop <= early:
                for side in range(2):
                    copies.append((len(pieces), shard, -1, side * strip, half_width))
                    pieces.append(value_arrived[hop, step, side])
    key_rows, value_proj = project_main(
        own_tokens,
        sibling_tokens,
        jnp.concatenate([key_bias, value_bias])[None],
        rope_tables(positions),
        pieces,
        copies,
        [source_at(distance) for distance in distances],
        2 * early + 1,
        plane,
    )

    def picked(source):
        return jnp.concatenate(
            [
                lax.dynamic_slice_in_dim(tokens, source * depth, depth, 1)
                for tokens in (own_tokens, sibling_tokens)
            ],
            axis=0,
        )

    def late_product(columns, side, piece):
        return jnp.dot(
            columns[:, side * strip : (side + 1) * strip],
            piece,
            preferred_element_type=jnp.float32,
        )

    columns = {hop: picked(source_at(hop)) for hop in distances[-3:]}
    for step in (1, -1):
        for side in range(2):
            hop = half_ring - 1
            value_proj += late_product(columns[-step * hop], side, value_arrived[hop, step, side])
    for side, step in enumerate((1, -1)):
        value_proj += late_product(columns[half_ring], side, value_arrived[half_ring, step, side])
    value_rows = value_proj.astype(jnp.bfloat16)

    keys, values = [key_rows], [value_rows]
    for hop in range(1, chips):
        keys.append(to_next_chip(keys[-1]))
        values.append(to_next_chip(values[-1]))
    sibling_keys = [to_sibling(x) for x in keys]
    sibling_values = [to_sibling(x) for x in values]

    def attention(half):
        facts = jnp.concatenate([jnp.stack([half, half, my_index]), block_segments[0]])
        return Attention(facts, queries[0], chips)

    near, far = attention(core), attention(1 - core)
    attended = near.attend(keys, values, None)
    attended = far.attend(sibling_keys, sibling_values, attended)
    return attended[None]


def solution(mesh):
    placed = (
        P("dp", "ctx", None),
        P("dp", "ctx", None),
        P("dp", None),
        P("dp", None),
        P(),
        P(),
        P("dp", None),
    )
    return jax.shard_map(
        layer, mesh=mesh, in_specs=placed, out_specs=P("dp", "ctx", None), check_vma=False
    )
```

```python
import functools
import math

import jax
import jax.numpy as jnp
from jax import lax
from jax.experimental import pallas as pl
from jax.experimental.pallas import tpu as pltpu
from jax.sharding import PartitionSpec as P


HEAD_SIZE = 128
KEY_VALUE_HEADS = 4
BLK = 128
MASKED = -1e30
CORES = 2
CHUNK = 2 * BLK
MOST_VMEM = 67043328
LEFT_VMEM = (4 << 20) - (1 << 16)

rope_base = 1000000.0


def ring_order(count):
    return list(range(0, count, 2)) + list(range(count - 1, 0, -2))


def rope_tables(token_positions):
    half_dim = HEAD_SIZE // 2
    frequency = rope_base ** (
        -(jnp.arange(half_dim, dtype=jnp.float32) * 2.0 / HEAD_SIZE)
    )
    angles = token_positions.astype(jnp.float32)[:, None] * frequency[None, :]
    cos_part, sine_part = jnp.cos(angles), jnp.sin(angles)
    return jnp.concatenate([cos_part, cos_part, -sine_part, sine_part], axis=1)


def main_kernel(copies, early, late, facts, own_ref, sibling_ref, bias_hbm, table_hbm, *refs):
    piece_refs = refs[:-10]
    key_ref, value_ref, token_ref, weight_ref, acc_ref = refs[-10:-5]
    bias_ref, table_ref, token_sems, weight_sems, other_sems = refs[-5:]
    number_of_rows, depth = own_ref.shape[0], weight_ref.shape[1]
    width = weight_ref.shape[2] // 2
    strip = depth // 2
    others = [
        pltpu.make_async_copy(bias_hbm, bias_ref, other_sems.at[0]),
        pltpu.make_async_copy(table_hbm, table_ref, other_sems.at[1]),
    ]
    for shard in range(early + late):
        for operand, at, side, offset, lane in copies:
            if at != shard:
                continue
            row = offset
            if side >= 0:
                plane = facts[0] if side == 0 else 1 - facts[0]
                row = pl.multiple_of(plane * strip + offset, strip // 2)
            pltpu.make_async_copy(
                piece_refs[operand],
                weight_ref.at[
                    shard, pl.ds(row, piece_refs[operand].shape[0]), pl.ds(lane, width)
                ],
                weight_sems.at[shard],
            ).start()
        columns = pl.ds(pl.multiple_of(facts[1 + shard] * depth, depth), depth)
        for half, tokens_ref in enumerate((own_ref, sibling_ref)):
            pltpu.make_async_copy(
                tokens_ref.at[:, columns],
                token_ref.at[shard, pl.ds(half * number_of_rows, number_of_rows), :],
                token_sems.at[shard],
            ).start()
    for copy in others:
        copy.start()
    acc_ref[...] = jnp.zeros_like(acc_ref)

    def add_shard(shard, lanes):
        strips = weight_ref.at[shard, :, pl.ds(0, lanes)]
        pltpu.make_async_copy(strips, strips, weight_sems.at[shard]).wait()
        pltpu.make_async_copy(
            token_ref.at[shard], token_ref.at[shard], token_sems.at[shard]
        ).wait()
        acc_ref[:, :lanes] += jnp.dot(
            token_ref[shard], weight_ref[shard, :, :lanes], preferred_element_type=jnp.float32
        )

    @pl.loop(0, early)
    def _(shard):
        add_shard(shard, 2 * width)

    for copy in others:
        copy.wait()
    value_ref[...] = acc_ref[:, width:] + bias_ref[:, width:]

    @pl.loop(early, early + late)
    def _(shard):
        add_shard(shard, width)

    for first in range(0, width, HEAD_SIZE):
        lanes = slice(first, first + HEAD_SIZE)
        head = acc_ref[:, lanes] + bias_ref[:, lanes]
        turned = head * table_ref[:, :HEAD_SIZE]
        turned += pltpu.roll(head, HEAD_SIZE // 2, 1) * table_ref[:, HEAD_SIZE:]
        key_ref[:, lanes] = turned.astype(key_ref.dtype)


def project_main(own_tokens, sibling_tokens, bias, table, pieces, copies, sources, early, plane):
    shards = len(sources)
    depth = own_tokens.shape[1] // shards
    chip_rows = CORES * own_tokens.shape[0]
    width = pieces[0].shape[1]
    facts = jnp.stack([plane, *sources]).astype(jnp.int32)
    out_spec = pl.BlockSpec((chip_rows, width), lambda p, b: (0, 0))
    anywhere = pl.BlockSpec(memory_space=pltpu.MemorySpace.HBM)
    return pl.pallas_call(
        functools.partial(main_kernel, tuple(copies), early, shards - early),
        out_shape=(
            jax.ShapeDtypeStruct((chip_rows, width), jnp.bfloat16),
            jax.ShapeDtypeStruct((chip_rows, width), jnp.float32),
        ),
        grid_spec=pltpu.PrefetchScalarGridSpec(
            num_scalar_prefetch=1,
            grid=(1,),
            in_specs=[anywhere] * (4 + len(pieces)),
            out_specs=(out_spec, out_spec),
            scratch_shapes=[
                pltpu.VMEM((shards, chip_rows, depth), jnp.bfloat16),
                pltpu.VMEM((shards, depth, 2 * width), jnp.bfloat16),
                pltpu.VMEM((chip_rows, 2 * width), jnp.float32),
                pltpu.VMEM(bias.shape, jnp.float32),
                pltpu.VMEM(table.shape, jnp.float32),
                pltpu.SemaphoreType.DMA((shards,)),
                pltpu.SemaphoreType.DMA((shards,)),
                pltpu.SemaphoreType.DMA((2,)),
            ],
        ),
        compiler_params=pltpu.CompilerParams(vmem_limit_bytes=MOST_VMEM - LEFT_VMEM),
        cost_estimate=pl.CostEstimate(
            flops=2 * (shards + early) * depth * chip_rows * width,
            bytes_accessed=2 * shards * depth * (chip_rows + width),
            transcendentals=0,
        ),
        name="project_main",
    )(facts, own_tokens, sibling_tokens, bias, table, *pieces)


class Blocks:
    def __init__(self, facts, hops, row_blocks, row_block):
        self.row_blocks, self.source_core = row_blocks, facts[1]
        per_chip = CORES * row_blocks
        chip = facts[2] // CORES
        here = facts[2] * row_blocks + row_block
        segment = facts[3 + here]
        self.diagonal = lax.rem(here, per_chip)
        self.entries, slot = [], jnp.int32(0)
        for hop in range(hops):
            for local in range(per_chip):
                block = (chip - hop) * per_chip + local
                seen = facts[3 + jnp.maximum(block, 0)]
                allowed = (block >= 0) & (block < here) & ((seen == 0) | (seen == segment))
                self.entries.append((hop, local, allowed, slot))
                slot = slot + jnp.where(allowed, 1, 0)
        self.odd = lax.rem(slot, 2) == 1
        self.free_slot = slot
        self.chunks = (slot + 2) // 2

    def place(self, local):
        core = local // self.row_blocks
        slot = jnp.where(core == self.source_core, 0, self.row_blocks)
        slot = slot + lax.rem(local, self.row_blocks)
        return pl.ds(pl.multiple_of(slot * BLK, BLK), BLK)

    def gather(self, refs, chosen_ref):
        def slot_rows(slot):
            return pl.ds(pl.multiple_of(slot * BLK, BLK), BLK)

        for hop, local, allowed, slot in self.entries:

            @pl.when(allowed)
            def _(hop=hop, local=local, slot=slot):
                chosen_ref[slot_rows(slot), :] = refs[hop][self.place(jnp.int32(local)), :]

        @pl.when(jnp.logical_not(self.odd))
        def _():
            chosen_ref[slot_rows(self.free_slot), :] = jnp.zeros(
                (BLK, chosen_ref.shape[1]), chosen_ref.dtype
            )

        chosen_ref[slot_rows(2 * self.chunks - 1), :] = refs[0][self.place(self.diagonal), :]


def chunk_rows(chunk):
    return pl.ds(pl.multiple_of(chunk * CHUNK, CHUNK), CHUNK)


def find_scores(blocks, group, q_ref, key_ref, score_ref, peak_ref):
    rows = group * BLK

    def scores(chunk):
        heads = [q_ref[:, h * HEAD_SIZE : (h + 1) * HEAD_SIZE] for h in range(group)]
        return lax.dot_general(
            jnp.concatenate(heads, axis=0),
            key_ref[chunk_rows(chunk), :],
            (((1,), (1,)), ((), ())),
            preferred_element_type=jnp.float32,
        )

    last = blocks.chunks - 1
    column = lax.broadcasted_iota(jnp.int32, (rows, CHUNK), 1)
    row = lax.broadcasted_iota(jnp.int32, (rows, CHUNK), 0) % BLK
    first_column = jnp.where(blocks.odd, 0, BLK)
    found = jnp.where(
        (column >= first_column) & (column - BLK <= row), scores(last), MASKED
    )
    score_ref[last] = found
    peak_ref[...] = jnp.maximum(found[:, :BLK], found[:, BLK:])

    @pl.loop(0, last)
    def _(chunk):
        found = scores(chunk)
        score_ref[chunk] = found
        peak_ref[...] = jnp.maximum(
            peak_ref[...], jnp.maximum(found[:, :BLK], found[:, BLK:])
        )

    peak_ref[...] = jnp.broadcast_to(
        jnp.max(peak_ref[...], axis=1, keepdims=True), (rows, BLK)
    )


def weights_of(chunk, score_ref, peak_ref, total_ref):
    factor = math.log2(math.e) / math.sqrt(HEAD_SIZE)
    peak, total, halves = peak_ref[...], total_ref[...], []
    for first in range(0, CHUNK, BLK):
        probs = jnp.exp2((score_ref[chunk, :, first : first + BLK] - peak) * factor)
        halves.append(probs.astype(jnp.bfloat16))
        total = total + probs
    total_ref[...] = total
    return halves


def attend_kernel(hops, row_blocks, group, facts, q_ref, *refs):
    k_refs, v_refs = refs[:hops], refs[hops : 2 * hops]
    out_ref, key_ref, value_ref, score_ref, peak_ref, total_ref, acc_ref = refs[-7:]
    blocks = Blocks(facts, hops, row_blocks, pl.program_id(0))
    head = pl.program_id(1)
    lanes = pl.ds(pl.multiple_of(head * HEAD_SIZE, HEAD_SIZE), HEAD_SIZE)

    @pl.when(head == 0)
    def _():
        blocks.gather(k_refs, key_ref)
        blocks.gather(v_refs, value_ref)

    find_scores(blocks, group, q_ref, key_ref.at[:, lanes], score_ref, peak_ref)
    total_ref[...] = jnp.zeros_like(total_ref)
    acc_ref[...] = jnp.zeros_like(acc_ref)

    @pl.loop(0, blocks.chunks)
    def _(chunk):
        halves = weights_of(chunk, score_ref, peak_ref, total_ref)
        acc_ref[...] += jnp.dot(
            jnp.concatenate(halves, axis=1),
            value_ref[chunk_rows(chunk), lanes],
            preferred_element_type=jnp.float32,
        )

    mixed = (acc_ref[...] / jnp.sum(total_ref[...], axis=1, keepdims=True)).astype(out_ref.dtype)
    for h in range(group):
        out_ref[:, h * HEAD_SIZE : (h + 1) * HEAD_SIZE] = mixed[h * BLK : (h + 1) * BLK]


class Attention:
    def __init__(self, facts, queries, hops):
        self.facts, self.queries, self.hops = facts, queries, hops
        self.rows, query_width = queries.shape
        self.group = query_width // HEAD_SIZE // KEY_VALUE_HEADS
        self.heads = KEY_VALUE_HEADS // CORES
        self.row_blocks = self.rows // BLK
        self.stacked = self.group * BLK
        self.chunks = hops * CORES * self.row_blocks * BLK // CHUNK
        self.q_spec = pl.BlockSpec(
            (BLK, self.group * HEAD_SIZE), lambda r, l, f: (r, f[0] * self.heads + l)
        )
        self.kv_spec = pl.BlockSpec(
            (CORES * self.rows, self.heads * HEAD_SIZE), lambda r, l, f: (0, 0)
        )
        self.pairs = self.heads * self.row_blocks * self.stacked * self.chunks * CHUNK // 2

    def attend(self, keys, values, before):
        operands = [self.facts, self.queries, *keys, *values]
        in_specs = [self.q_spec] + [self.kv_spec] * (2 * self.hops)
        aliases = {}
        if before is not None:
            aliases = {len(operands): 0}
            operands.append(before)
            in_specs.append(pl.BlockSpec(memory_space=pl.ANY))
        chosen = pltpu.VMEM((self.chunks * CHUNK, self.heads * HEAD_SIZE), jnp.bfloat16)
        tall = pltpu.VMEM((self.stacked, BLK), jnp.float32)
        return pl.pallas_call(
            functools.partial(attend_kernel, self.hops, self.row_blocks, self.group),
            out_shape=jax.ShapeDtypeStruct(self.queries.shape, self.queries.dtype),
            grid_spec=pltpu.PrefetchScalarGridSpec(
                num_scalar_prefetch=1,
                grid=(self.row_blocks, self.heads),
                in_specs=in_specs,
                out_specs=self.q_spec,
                scratch_shapes=[
                    chosen,
                    chosen,
                    pltpu.VMEM((self.chunks, self.stacked, CHUNK), jnp.float32),
                    tall,
                    tall,
                    tall,
                ],
            ),
            input_output_aliases=aliases,
            compiler_params=pltpu.CompilerParams(
                vmem_limit_bytes=MOST_VMEM - LEFT_VMEM
            ),
            cost_estimate=pl.CostEstimate(
                flops=4 * self.pairs * HEAD_SIZE,
                bytes_accessed=2 * self.queries.size,
                transcendentals=self.pairs,
            ),
            name="attend",
        )(*operands)


def layer(
    hidden_in,
    queries,
    key_projection_weight,
    value_projection_weight,
    key_projection_bias,
    value_projection_bias,
    block_segments,
):
    own_tokens = hidden_in[0]
    number_of_rows = own_tokens.shape[0]
    depth, kv_width = key_projection_weight.shape
    dp_size, ctx_size = lax.axis_size("dp"), lax.axis_size("ctx")
    chips = ctx_size // CORES
    my_index = lax.axis_index("ctx")
    core, chip = my_index % CORES, my_index // CORES
    plane = chip % 2
    half_width = kv_width // CORES
    ring = ring_order(dp_size)
    dp_index = lax.axis_index("dp")
    my_spot = jnp.where(dp_index % 2 == 0, dp_index // 2, dp_size - (dp_index + 1) // 2)

    def to_sibling(x):
        return lax.ppermute(x, "ctx", [(i, i ^ 1) for i in range(ctx_size)])

    def to_plane(x):
        return lax.ppermute(x, "ctx", [(i, i ^ CORES) for i in range(ctx_size)])

    def to_next_chip(x):
        return lax.ppermute(x, "ctx", [(i, i + CORES) for i in range(ctx_size - CORES)])

    def along_ring(x, step):
        return lax.ppermute(
            x, "dp", [(ring[i], ring[(i + step) % dp_size]) for i in range(dp_size)]
        )

    key_weight = lax.dynamic_slice_in_dim(key_projection_weight, core * half_width, half_width, 1)
    value_weight = lax.dynamic_slice_in_dim(
        value_projection_weight, core * half_width, half_width, 1
    )
    strip = depth // 2
    part = strip // 2
    key_strip = lax.dynamic_slice_in_dim(key_weight, plane * strip, strip, 0)
    sibling_tokens = to_sibling(own_tokens)

    def source_at(distance):
        spot = (my_spot + distance + dp_size) % dp_size
        return jnp.where(spot < dp_size // 2, 2 * spot, 2 * (dp_size - spot) - 1)

    half_ring = dp_size // 2

    arange = jnp.arange(number_of_rows, dtype=jnp.int32)
    positions = jnp.concatenate(
        [my_index * number_of_rows + arange, (my_index ^ 1) * number_of_rows + arange]
    )
    key_bias = lax.dynamic_slice_in_dim(key_projection_bias, core * half_width, half_width, 0)
    value_bias = lax.dynamic_slice_in_dim(value_projection_bias, core * half_width, half_width, 0)

    key_arrived, value_arrived = {}, {}
    travelling = {1: key_strip, -1: key_strip}
    for hop in range(1, half_ring + 1):
        for step in (1, -1):
            piece = travelling[step]
            if hop == half_ring:
                first_row = 0 if step == 1 else part
                piece = piece[first_row : first_row + part]
            piece = along_ring(piece, step)
            other = to_plane(piece)
            travelling[step] = piece
            key_arrived[hop, step] = (piece, other)

    travelling = {
        (side, step): value_weight[side * strip : (side + 1) * strip]
        for side in range(2)
        for step in (1, -1)
    }
    for hop in range(1, half_ring + 1):
        for side in range(2):
            for step in (1, -1):
                if hop == half_ring and step != (1, -1)[side]:
                    continue
                piece = along_ring(travelling[side, step], step)
                travelling[side, step] = piece
                value_arrived[hop, step, side] = piece

    early = half_ring - 2
    distances = list(range(-early, early + 1)) + [-half_ring + 1, half_ring - 1, half_ring]
    pieces = [key_weight, value_weight]
    copies = [(0, early, -1, 0, 0), (1, early, -1, 0, half_width)]
    for hop in range(1, half_ring + 1):
        for step in (1, -1):
            shard = distances.index(half_ring if hop == half_ring else -step * hop)
            offset = part if hop == half_ring and step == -1 else 0
            for side, piece in enumerate(key_arrived[hop, step]):
                copies.append((len(pieces), shard, side, offset, 0))
                pieces.append(piece)
            if hop <= early:
                for side in range(2):
                    copies.append((len(pieces), shard, -1, side * strip, half_width))
                    pieces.append(value_arrived[hop, step, side])
    table = rope_tables(positions)
    key_rows, value_proj = project_main(
        own_tokens,
        sibling_tokens,
        jnp.concatenate([key_bias, value_bias])[None],
        table,
        pieces,
        copies,
        [source_at(distance) for distance in distances],
        2 * early + 1,
        plane,
    )

    def picked(source):
        return jnp.concatenate(
            [
                lax.dynamic_slice_in_dim(tokens, source * depth, depth, 1)
                for tokens in (own_tokens, sibling_tokens)
            ],
            axis=0,
        )

    def late_product(columns, side, piece):
        return jnp.dot(
            columns[:, side * strip : (side + 1) * strip],
            piece,
            preferred_element_type=jnp.float32,
        )

    columns = {hop: picked(source_at(hop)) for hop in distances[-3:]}
    for step in (1, -1):
        for side in range(2):
            hop = half_ring - 1
            value_proj += late_product(columns[-step * hop], side, value_arrived[hop, step, side])
    for side, step in enumerate((1, -1)):
        value_proj += late_product(columns[half_ring], side, value_arrived[half_ring, step, side])
    value_rows = value_proj.astype(jnp.bfloat16)

    keys, values = [key_rows], [value_rows]
    for hop in range(1, chips):
        keys.append(to_next_chip(keys[-1]))
        values.append(to_next_chip(values[-1]))
    sibling_keys = [to_sibling(x) for x in keys]
    sibling_values = [to_sibling(x) for x in values]

    def attention(half):
        facts = jnp.concatenate([jnp.stack([half, half, my_index]), block_segments[0]])
        return Attention(facts, queries[0], chips)

    near, far = attention(core), attention(1 - core)
    attended = near.attend(keys, values, None)
    attended = far.attend(sibling_keys, sibling_values, attended)
    return attended[None]


def solution(mesh):
    placed = (
        P("dp", "ctx", None),
        P("dp", "ctx", None),
        P("dp", None),
        P("dp", None),
        P(),
        P(),
        P("dp", None),
    )
    return jax.shard_map(
        layer, mesh=mesh, in_specs=placed, out_specs=P("dp", "ctx", None), check_vma=False
    )
```

```python
import functools
import math

import jax
import jax.numpy as jnp
from jax import lax
from jax.experimental import pallas as pl
from jax.experimental.pallas import tpu as pltpu
from jax.sharding import PartitionSpec as P


HEAD_SIZE = 128
KEY_VALUE_HEADS = 4
BLK = 128
MASKED = -1e30
CORES = 2
CHUNK = 2 * BLK
PART = 2
MOST_VMEM = 67043328
LEFT_VMEM = (4 << 20) - (1 << 16)

rope_base = 1000000.0


def ring_order(count):
    return list(range(0, count, 2)) + list(range(count - 1, 0, -2))


def rope_tables(token_positions):
    half_dim = HEAD_SIZE // 2
    frequency = rope_base ** (
        -(jnp.arange(half_dim, dtype=jnp.float32) * 2.0 / HEAD_SIZE)
    )
    angles = token_positions.astype(jnp.float32)[:, None] * frequency[None, :]
    cos_part, sine_part = jnp.cos(angles), jnp.sin(angles)
    return jnp.concatenate([cos_part, cos_part, -sine_part, sine_part], axis=1)


def main_kernel(copies, early, late, facts, own_ref, sibling_ref, bias_hbm, table_hbm, *refs):
    piece_refs = refs[:-10]
    key_ref, value_ref, token_ref, weight_ref, acc_ref = refs[-10:-5]
    bias_ref, table_ref, token_sems, weight_sems, other_sems = refs[-5:]
    number_of_rows, depth = own_ref.shape[0], weight_ref.shape[1]
    width = weight_ref.shape[2] // 2
    strip = depth // 2
    others = [
        pltpu.make_async_copy(bias_hbm, bias_ref, other_sems.at[0]),
        pltpu.make_async_copy(table_hbm, table_ref, other_sems.at[1]),
    ]
    for shard in range(early + late):
        for operand, at, side, offset, lane in copies:
            if at != shard:
                continue
            row = offset
            if side >= 0:
                plane = facts[0] if side == 0 else 1 - facts[0]
                row = pl.multiple_of(plane * strip + offset, strip // 2)
            pltpu.make_async_copy(
                piece_refs[operand],
                weight_ref.at[
                    shard, pl.ds(row, piece_refs[operand].shape[0]), pl.ds(lane, width)
                ],
                weight_sems.at[shard],
            ).start()
        columns = pl.ds(pl.multiple_of(facts[1 + shard] * depth, depth), depth)
        for half, tokens_ref in enumerate((own_ref, sibling_ref)):
            pltpu.make_async_copy(
                tokens_ref.at[:, columns],
                token_ref.at[shard, pl.ds(half * number_of_rows, number_of_rows), :],
                token_sems.at[shard],
            ).start()
    for copy in others:
        copy.start()
    acc_ref[...] = jnp.zeros_like(acc_ref)

    def add_shard(shard, lanes):
        strips = weight_ref.at[shard, :, pl.ds(0, lanes)]
        pltpu.make_async_copy(strips, strips, weight_sems.at[shard]).wait()
        pltpu.make_async_copy(
            token_ref.at[shard], token_ref.at[shard], token_sems.at[shard]
        ).wait()
        acc_ref[:, :lanes] += jnp.dot(
            token_ref[shard], weight_ref[shard, :, :lanes], preferred_element_type=jnp.float32
        )

    @pl.loop(0, early)
    def _(shard):
        add_shard(shard, 2 * width)

    for copy in others:
        copy.wait()
    value_ref[...] = acc_ref[:, width:] + bias_ref[:, width:]

    @pl.loop(early, early + late)
    def _(shard):
        add_shard(shard, width)

    for first in range(0, width, HEAD_SIZE):
        lanes = slice(first, first + HEAD_SIZE)
        head = acc_ref[:, lanes] + bias_ref[:, lanes]
        turned = head * table_ref[:, :HEAD_SIZE]
        turned += pltpu.roll(head, HEAD_SIZE // 2, 1) * table_ref[:, HEAD_SIZE:]
        key_ref[:, lanes] = turned.astype(key_ref.dtype)


def project_main(own_tokens, sibling_tokens, bias, table, pieces, copies, sources, early, plane):
    shards = len(sources)
    depth = own_tokens.shape[1] // shards
    chip_rows = CORES * own_tokens.shape[0]
    width = pieces[0].shape[1]
    facts = jnp.stack([plane, *sources]).astype(jnp.int32)
    out_spec = pl.BlockSpec((chip_rows, width), lambda p, b: (0, 0))
    anywhere = pl.BlockSpec(memory_space=pltpu.MemorySpace.HBM)
    return pl.pallas_call(
        functools.partial(main_kernel, tuple(copies), early, shards - early),
        out_shape=(
            jax.ShapeDtypeStruct((chip_rows, width), jnp.bfloat16),
            jax.ShapeDtypeStruct((chip_rows, width), jnp.float32),
        ),
        grid_spec=pltpu.PrefetchScalarGridSpec(
            num_scalar_prefetch=1,
            grid=(1,),
            in_specs=[anywhere] * (4 + len(pieces)),
            out_specs=(out_spec, out_spec),
            scratch_shapes=[
                pltpu.VMEM((shards, chip_rows, depth), jnp.bfloat16),
                pltpu.VMEM((shards, depth, 2 * width), jnp.bfloat16),
                pltpu.VMEM((chip_rows, 2 * width), jnp.float32),
                pltpu.VMEM(bias.shape, jnp.float32),
                pltpu.VMEM(table.shape, jnp.float32),
                pltpu.SemaphoreType.DMA((shards,)),
                pltpu.SemaphoreType.DMA((shards,)),
                pltpu.SemaphoreType.DMA((2,)),
            ],
        ),
        compiler_params=pltpu.CompilerParams(vmem_limit_bytes=MOST_VMEM - LEFT_VMEM),
        cost_estimate=pl.CostEstimate(
            flops=2 * (shards + early) * depth * chip_rows * width,
            bytes_accessed=2 * shards * depth * (chip_rows + width),
            transcendentals=0,
        ),
        name="project_main",
    )(facts, own_tokens, sibling_tokens, bias, table, *pieces)


class Blocks:
    def __init__(self, facts, hops, row_blocks, row_block):
        self.row_blocks = row_blocks
        per_chip = CORES * row_blocks
        chip = facts[1] // CORES
        here = facts[1] * row_blocks + row_block
        segment = facts[2 + here]
        self.diagonal = lax.rem(here, per_chip)
        self.entries, slot = [], jnp.int32(0)
        for hop in range(hops):
            for local in range(per_chip):
                block = (chip - hop) * per_chip + local
                seen = facts[2 + jnp.maximum(block, 0)]
                allowed = (block >= 0) & (block < here) & ((seen == 0) | (seen == segment))
                self.entries.append((hop, local, allowed, slot))
                slot = slot + jnp.where(allowed, 1, 0)
        self.odd = lax.rem(slot, 2) == 1
        self.free_slot = slot
        self.chunks = (slot + 2) // 2

    def place(self, local, source_core):
        core = local // self.row_blocks
        slot = jnp.where(core == source_core, 0, self.row_blocks)
        slot = slot + lax.rem(local, self.row_blocks)
        return pl.ds(pl.multiple_of(slot * BLK, BLK), BLK)

    def gather(self, refs, source_core, chosen_ref):
        def slot_rows(slot):
            return pl.ds(pl.multiple_of(slot * BLK, BLK), BLK)

        for hop, local, allowed, slot in self.entries:

            @pl.when(allowed)
            def _(hop=hop, local=local, slot=slot):
                chosen_ref[slot_rows(slot), :] = refs[hop][
                    self.place(jnp.int32(local), source_core), :
                ]

        @pl.when(jnp.logical_not(self.odd))
        def _():
            chosen_ref[slot_rows(self.free_slot), :] = jnp.zeros(
                (BLK, chosen_ref.shape[1]), chosen_ref.dtype
            )

        chosen_ref[slot_rows(2 * self.chunks - 1), :] = refs[0][
            self.place(self.diagonal, source_core), :
        ]


def chunk_rows(chunk):
    return pl.ds(pl.multiple_of(chunk * CHUNK, CHUNK), CHUNK)


def find_scores(blocks, group, q_ref, key_ref, score_ref, peak_ref):
    factor = math.log2(math.e) / math.sqrt(HEAD_SIZE)

    def parts_of(chunk):
        keys = key_ref[chunk_rows(chunk), :]
        for first in range(0, group, PART):
            heads = [
                q_ref[:, h * HEAD_SIZE : (h + 1) * HEAD_SIZE] for h in range(first, first + PART)
            ]
            found = lax.dot_general(
                jnp.concatenate(heads, axis=0),
                keys,
                (((1,), (1,)), ((), ())),
                preferred_element_type=jnp.float32,
            )
            yield slice(first * BLK, (first + PART) * BLK), found * factor

    last = blocks.chunks - 1
    column = lax.broadcasted_iota(jnp.int32, (PART * BLK, CHUNK), 1)
    row = lax.broadcasted_iota(jnp.int32, (PART * BLK, CHUNK), 0) % BLK
    first_column = jnp.where(blocks.odd, 0, BLK)
    for rows, found in parts_of(last):
        found = jnp.where((column >= first_column) & (column - BLK <= row), found, MASKED)
        score_ref[last, rows, :] = found
        peak_ref[rows, :] = jnp.maximum(found[:, :BLK], found[:, BLK:])

    @pl.loop(0, last)
    def _(chunk):
        for rows, found in parts_of(chunk):
            score_ref[chunk, rows, :] = found
            peak_ref[rows, :] = jnp.maximum(
                peak_ref[rows, :], jnp.maximum(found[:, :BLK], found[:, BLK:])
            )

    peak_ref[...] = jnp.broadcast_to(
        jnp.max(peak_ref[...], axis=1, keepdims=True), peak_ref.shape
    )


def score_kernel(hops, row_blocks, group, facts, q_ref, *refs):
    k_refs = refs[:hops]
    probs_ref, inverse_ref, key_ref, score_ref, peak_ref, total_ref = refs[hops:]
    blocks = Blocks(facts, hops, row_blocks, pl.program_id(0))
    head = pl.program_id(1)
    lanes = pl.ds(pl.multiple_of(head * HEAD_SIZE, HEAD_SIZE), HEAD_SIZE)

    @pl.when(head == 0)
    def _():
        blocks.gather(k_refs, facts[0], key_ref)

    find_scores(blocks, group, q_ref, key_ref.at[:, lanes], score_ref, peak_ref)
    total_ref[...] = jnp.zeros_like(total_ref)

    @pl.loop(0, blocks.chunks)
    def _(chunk):
        peak, total = peak_ref[...], total_ref[...]
        for column in range(0, CHUNK, BLK):
            probs = jnp.exp2(score_ref[chunk, :, column : column + BLK] - peak)
            probs_ref[0, chunk, :, column : column + BLK] = probs.astype(jnp.bfloat16)
            total = total + probs
        total_ref[...] = total

    inverse_ref[0] = jnp.broadcast_to(
        1.0 / jnp.sum(total_ref[...], axis=1, keepdims=True), total_ref.shape
    )


def attend_kernel(hops, row_blocks, group, heads, facts, q_ref, probs_hbm, inverse_ref, *refs):
    near_values, far_keys, far_values = (refs[at * hops : (at + 1) * hops] for at in range(3))
    out_ref, key_ref, value_ref, score_ref, peak_ref, total_ref, acc_ref = refs[3 * hops : -2]
    held_ref, sems = refs[-2:]
    row_block, head = pl.program_id(0), pl.program_id(1)
    blocks = Blocks(facts, hops, row_blocks, row_block)
    lanes = pl.ds(pl.multiple_of(lax.rem(head, heads) * HEAD_SIZE, HEAD_SIZE), HEAD_SIZE)

    def fetch(rows_of, at, chunk):
        return pltpu.make_async_copy(
            probs_hbm.at[rows_of * heads + at, chunk], held_ref.at[at, chunk], sems.at[at, chunk]
        )

    def fetch_row_block(rows_of):
        for at in range(heads):

            @pl.loop(0, Blocks(facts, hops, row_blocks, rows_of).chunks)
            def _(chunk):
                fetch(rows_of, at, chunk).start()

    @pl.when((row_block == 0) & (head == 0))
    def _():
        fetch_row_block(row_block)

    @pl.when((row_block + 1 < row_blocks) & (head == heads))
    def _():
        fetch_row_block(lax.rem(row_block + 1, row_blocks))

    @pl.when(head == 0)
    def _():
        blocks.gather(near_values, facts[0], value_ref)

    @pl.when(head == heads)
    def _():
        blocks.gather(far_keys, 1 - facts[0], key_ref)
        blocks.gather(far_values, 1 - facts[0], value_ref)

    def store(mixed):
        mixed = mixed.astype(out_ref.dtype)
        for h in range(group):
            out_ref[:, h * HEAD_SIZE : (h + 1) * HEAD_SIZE] = mixed[h * BLK : (h + 1) * BLK]

    acc_ref[...] = jnp.zeros_like(acc_ref)

    @pl.when(head < heads)
    def _():
        @pl.loop(0, blocks.chunks)
        def _(chunk):
            fetch(row_block, head, chunk).wait()
            acc_ref[...] += jnp.dot(
                held_ref[head, chunk],
                value_ref[chunk_rows(chunk), lanes],
                preferred_element_type=jnp.float32,
            )

        store(acc_ref[...] * inverse_ref[0])

    @pl.when(head >= heads)
    def _():
        find_scores(blocks, group, q_ref, key_ref.at[:, lanes], score_ref, peak_ref)
        total_ref[...] = jnp.zeros_like(total_ref)

        @pl.loop(0, blocks.chunks)
        def _(chunk):
            values = value_ref[chunk_rows(chunk), lanes]
            for first in range(0, group * BLK, PART * BLK):
                rows = slice(first, first + PART * BLK)
                peak, total, halves = peak_ref[rows, :], total_ref[rows, :], []
                for column in range(0, CHUNK, BLK):
                    found = score_ref[chunk, rows, column : column + BLK]
                    probs = jnp.exp2(found - peak)
                    halves.append(probs.astype(jnp.bfloat16))
                    total = total + probs
                total_ref[rows, :] = total
                acc_ref[rows, :] += jnp.dot(
                    jnp.concatenate(halves, axis=1), values, preferred_element_type=jnp.float32
                )

        store(acc_ref[...] / jnp.sum(total_ref[...], axis=1, keepdims=True))


class Attention:
    def __init__(self, facts, queries, hops):
        self.facts, self.queries, self.hops = facts, queries, hops
        number_of_rows, query_width = queries.shape
        self.group = query_width // HEAD_SIZE // KEY_VALUE_HEADS
        self.heads = heads = KEY_VALUE_HEADS // CORES
        self.row_blocks = number_of_rows // BLK
        self.stacked = self.group * BLK
        self.chunks = hops * CORES * self.row_blocks * BLK // CHUNK
        self.q_spec = pl.BlockSpec(
            (BLK, self.group * HEAD_SIZE),
            lambda r, l, f: (r, jnp.where(l < heads, f[0], 1 - f[0]) * heads + lax.rem(l, heads)),
        )
        self.kv_spec = pl.BlockSpec(
            (CORES * number_of_rows, heads * HEAD_SIZE), lambda r, l, f: (0, 0)
        )
        self.chosen = pltpu.VMEM((self.chunks * CHUNK, heads * HEAD_SIZE), jnp.bfloat16)
        self.scores = pltpu.VMEM((self.chunks, self.stacked, CHUNK), jnp.float32)
        self.tall = pltpu.VMEM((self.stacked, BLK), jnp.float32)
        count = heads * self.row_blocks
        self.probs = jax.ShapeDtypeStruct(
            (count, self.chunks, self.stacked, CHUNK), jnp.bfloat16
        )
        self.inverse = jax.ShapeDtypeStruct((count, self.stacked, BLK), jnp.float32)
        self.pairs = count * self.stacked * self.chunks * CHUNK // 2

    def call(self, kernel, heads, out_shape, in_specs, out_specs, scratch, operands):
        return pl.pallas_call(
            kernel,
            out_shape=out_shape,
            grid_spec=pltpu.PrefetchScalarGridSpec(
                num_scalar_prefetch=1,
                grid=(self.row_blocks, heads),
                in_specs=[self.q_spec] + in_specs,
                out_specs=out_specs,
                scratch_shapes=scratch,
            ),
            compiler_params=pltpu.CompilerParams(vmem_limit_bytes=MOST_VMEM - LEFT_VMEM),
            cost_estimate=pl.CostEstimate(
                flops=4 * self.pairs * HEAD_SIZE,
                bytes_accessed=2 * self.queries.size,
                transcendentals=self.pairs,
            ),
        )(self.facts, self.queries, *operands)

    def score(self, keys):
        heads, rows = self.heads, self.row_blocks
        return self.call(
            functools.partial(score_kernel, self.hops, rows, self.group),
            heads,
            (self.probs, self.inverse),
            [self.kv_spec] * self.hops,
            (
                pl.BlockSpec((1, *self.probs.shape[1:]), lambda r, l, f: (r * heads + l, 0, 0, 0)),
                pl.BlockSpec((1, self.stacked, BLK), lambda r, l, f: (r * heads + l, 0, 0)),
            ),
            [self.chosen, self.scores, self.tall, self.tall],
            keys,
        )

    def attend(self, probs, inverse, values, far_keys, far_values):
        heads = self.heads
        return self.call(
            functools.partial(attend_kernel, self.hops, self.row_blocks, self.group, heads),
            KEY_VALUE_HEADS,
            jax.ShapeDtypeStruct(self.queries.shape, self.queries.dtype),
            [
                pl.BlockSpec(memory_space=pltpu.MemorySpace.HBM),
                pl.BlockSpec(
                    (1, self.stacked, BLK),
                    lambda r, l, f: (r * heads + jnp.minimum(l, heads - 1), 0, 0),
                ),
            ]
            + [self.kv_spec] * (3 * self.hops),
            self.q_spec,
            [
                self.chosen,
                self.chosen,
                self.scores,
                self.tall,
                self.tall,
                self.tall,
                pltpu.VMEM((heads, *self.probs.shape[1:]), jnp.bfloat16),
                pltpu.SemaphoreType.DMA((heads, self.chunks)),
            ],
            [probs, inverse, *values, *far_keys, *far_values],
        )


def layer(
    hidden_in,
    queries,
    key_projection_weight,
    value_projection_weight,
    key_projection_bias,
    value_projection_bias,
    block_segments,
):
    own_tokens = hidden_in[0]
    number_of_rows = own_tokens.shape[0]
    depth, kv_width = key_projection_weight.shape
    dp_size, ctx_size = lax.axis_size("dp"), lax.axis_size("ctx")
    chips = ctx_size // CORES
    my_index = lax.axis_index("ctx")
    core, chip = my_index % CORES, my_index // CORES
    plane = chip % 2
    half_width = kv_width // CORES
    ring = ring_order(dp_size)
    dp_index = lax.axis_index("dp")
    my_spot = jnp.where(dp_index % 2 == 0, dp_index // 2, dp_size - (dp_index + 1) // 2)

    def to_sibling(x):
        return lax.ppermute(x, "ctx", [(i, i ^ 1) for i in range(ctx_size)])

    def to_plane(x):
        return lax.ppermute(x, "ctx", [(i, i ^ CORES) for i in range(ctx_size)])

    def to_next_chip(x):
        return lax.ppermute(x, "ctx", [(i, i + CORES) for i in range(ctx_size - CORES)])

    def along_ring(x, step):
        return lax.ppermute(
            x, "dp", [(ring[i], ring[(i + step) % dp_size]) for i in range(dp_size)]
        )

    key_weight = lax.dynamic_slice_in_dim(key_projection_weight, core * half_width, half_width, 1)
    value_weight = lax.dynamic_slice_in_dim(
        value_projection_weight, core * half_width, half_width, 1
    )
    strip = depth // 2
    part = strip // 2
    key_strip = lax.dynamic_slice_in_dim(key_weight, plane * strip, strip, 0)
    sibling_tokens = to_sibling(own_tokens)

    def source_at(distance):
        spot = (my_spot + distance + dp_size) % dp_size
        return jnp.where(spot < dp_size // 2, 2 * spot, 2 * (dp_size - spot) - 1)

    half_ring = dp_size // 2

    arange = jnp.arange(number_of_rows, dtype=jnp.int32)
    positions = jnp.concatenate(
        [my_index * number_of_rows + arange, (my_index ^ 1) * number_of_rows + arange]
    )
    key_bias = lax.dynamic_slice_in_dim(key_projection_bias, core * half_width, half_width, 0)
    value_bias = lax.dynamic_slice_in_dim(value_projection_bias, core * half_width, half_width, 0)

    key_arrived, value_arrived = {}, {}
    travelling = {1: key_strip, -1: key_strip}
    for hop in range(1, half_ring + 1):
        for step in (1, -1):
            piece = travelling[step]
            if hop == half_ring:
                first_row = 0 if step == 1 else part
                piece = piece[first_row : first_row + part]
            piece = along_ring(piece, step)
            other = to_plane(piece)
            travelling[step] = piece
            key_arrived[hop, step] = (piece, other)

    travelling = {
        (side, step): value_weight[side * strip : (side + 1) * strip]
        for side in range(2)
        for step in (1, -1)
    }
    for hop in range(1, half_ring + 1):
        for side in range(2):
            for step in (1, -1):
                if hop == half_ring and step != (1, -1)[side]:
                    continue
                piece = along_ring(travelling[side, step], step)
                travelling[side, step] = piece
                value_arrived[hop, step, side] = piece

    early = half_ring - 2
    distances = list(range(-early, early + 1)) + [-half_ring + 1, half_ring - 1, half_ring]
    pieces = [key_weight, value_weight]
    copies = [(0, early, -1, 0, 0), (1, early, -1, 0, half_width)]
    for hop in range(1, half_ring + 1):
        for step in (1, -1):
            shard = distances.index(half_ring if hop == half_ring else -step * hop)
            offset = part if hop == half_ring and step == -1 else 0
            for side, piece in enumerate(key_arrived[hop, step]):
                copies.append((len(pieces), shard, side, offset, 0))
                pieces.append(piece)
            if hop <= early:
                for side in range(2):
                    copies.append((len(pieces), shard, -1, side * strip, half_width))
                    pieces.append(value_arrived[hop, step, side])
    table = rope_tables(positions)
    key_rows, value_proj = project_main(
        own_tokens,
        sibling_tokens,
        jnp.concatenate([key_bias, value_bias])[None],
        table,
        pieces,
        copies,
        [source_at(distance) for distance in distances],
        2 * early + 1,
        plane,
    )

    def picked(source):
        return jnp.concatenate(
            [
                lax.dynamic_slice_in_dim(tokens, source * depth, depth, 1)
                for tokens in (own_tokens, sibling_tokens)
            ],
            axis=0,
        )

    def late_product(columns, side, piece):
        return jnp.dot(
            columns[:, side * strip : (side + 1) * strip],
            piece,
            preferred_element_type=jnp.float32,
        )

    columns = {hop: picked(source_at(hop)) for hop in distances[-3:]}
    for step in (1, -1):
        for side in range(2):
            hop = half_ring - 1
            value_proj += late_product(columns[-step * hop], side, value_arrived[hop, step, side])
    for side, step in enumerate((1, -1)):
        value_proj += late_product(columns[half_ring], side, value_arrived[half_ring, step, side])
    value_rows = value_proj.astype(jnp.bfloat16)

    keys, values = [key_rows], [value_rows]
    for hop in range(1, chips):
        keys.append(to_next_chip(keys[-1]))
        values.append(to_next_chip(values[-1]))
    sibling_keys = [to_sibling(x) for x in keys]
    sibling_values = [to_sibling(x) for x in values]

    facts = jnp.concatenate([jnp.stack([core, my_index]), block_segments[0]])
    attention = Attention(facts, queries[0], chips)
    probs, inverse = attention.score(keys)
    attended = attention.attend(probs, inverse, values, sibling_keys, sibling_values)
    return attended[None]


def solution(mesh):
    placed = (
        P("dp", "ctx", None),
        P("dp", "ctx", None),
        P("dp", None),
        P("dp", None),
        P(),
        P(),
        P("dp", None),
    )
    return jax.shard_map(
        layer, mesh=mesh, in_specs=placed, out_specs=P("dp", "ctx", None), check_vma=False
    )
```

```python
import functools
import math

import jax
import jax.numpy as jnp
from jax import lax
from jax.experimental import pallas as pl
from jax.experimental.pallas import tpu as pltpu
from jax.sharding import PartitionSpec as P


HEAD_SIZE = 128
KEY_VALUE_HEADS = 4
BLK = 128
MASKED = -1e30
CORES = 2
CHUNK = 2 * BLK
PART = 2
MOST_VMEM = 67043328
LEFT_VMEM = (4 << 20) - (1 << 16)

rope_base = 1000000.0


def ring_order(count):
    return list(range(0, count, 2)) + list(range(count - 1, 0, -2))


def rope_tables(token_positions):
    half_dim = HEAD_SIZE // 2
    frequency = rope_base ** (
        -(jnp.arange(half_dim, dtype=jnp.float32) * 2.0 / HEAD_SIZE)
    )
    angles = token_positions.astype(jnp.float32)[:, None] * frequency[None, :]
    cos_part, sine_part = jnp.cos(angles), jnp.sin(angles)
    return jnp.concatenate([cos_part, cos_part, -sine_part, sine_part], axis=1)


def main_kernel(copies, early, late, facts, own_ref, sibling_ref, bias_hbm, table_hbm, *refs):
    piece_refs = refs[:-10]
    key_ref, value_ref, token_ref, weight_ref, acc_ref = refs[-10:-5]
    bias_ref, table_ref, token_sems, weight_sems, other_sems = refs[-5:]
    number_of_rows, depth = own_ref.shape[0], weight_ref.shape[1]
    width = weight_ref.shape[2] // 2
    strip = depth // 2
    others = [
        pltpu.make_async_copy(bias_hbm, bias_ref, other_sems.at[0]),
        pltpu.make_async_copy(table_hbm, table_ref, other_sems.at[1]),
    ]
    for shard in range(early + late):
        for operand, at, side, offset, lane in copies:
            if at != shard:
                continue
            row = offset
            if side >= 0:
                plane = facts[0] if side == 0 else 1 - facts[0]
                row = pl.multiple_of(plane * strip + offset, strip // 2)
            pltpu.make_async_copy(
                piece_refs[operand],
                weight_ref.at[
                    shard, pl.ds(row, piece_refs[operand].shape[0]), pl.ds(lane, width)
                ],
                weight_sems.at[shard],
            ).start()
        columns = pl.ds(pl.multiple_of(facts[1 + shard] * depth, depth), depth)
        for half, tokens_ref in enumerate((own_ref, sibling_ref)):
            pltpu.make_async_copy(
                tokens_ref.at[:, columns],
                token_ref.at[shard, pl.ds(half * number_of_rows, number_of_rows), :],
                token_sems.at[shard],
            ).start()
    for copy in others:
        copy.start()
    acc_ref[...] = jnp.zeros_like(acc_ref)

    def add_shard(shard, lanes):
        strips = weight_ref.at[shard, :, pl.ds(0, lanes)]
        pltpu.make_async_copy(strips, strips, weight_sems.at[shard]).wait()
        pltpu.make_async_copy(
            token_ref.at[shard], token_ref.at[shard], token_sems.at[shard]
        ).wait()
        acc_ref[:, :lanes] += jnp.dot(
            token_ref[shard], weight_ref[shard, :, :lanes], preferred_element_type=jnp.float32
        )

    @pl.loop(0, early)
    def _(shard):
        add_shard(shard, 2 * width)

    for copy in others:
        copy.wait()
    value_ref[...] = acc_ref[:, width:] + bias_ref[:, width:]

    @pl.loop(early, early + late)
    def _(shard):
        add_shard(shard, width)

    for first in range(0, width, HEAD_SIZE):
        lanes = slice(first, first + HEAD_SIZE)
        head = acc_ref[:, lanes] + bias_ref[:, lanes]
        turned = head * table_ref[:, :HEAD_SIZE]
        turned += pltpu.roll(head, HEAD_SIZE // 2, 1) * table_ref[:, HEAD_SIZE:]
        key_ref[:, lanes] = turned.astype(key_ref.dtype)


def project_main(own_tokens, sibling_tokens, bias, table, pieces, copies, sources, early, plane):
    shards = len(sources)
    depth = own_tokens.shape[1] // shards
    chip_rows = CORES * own_tokens.shape[0]
    width = pieces[0].shape[1]
    facts = jnp.stack([plane, *sources]).astype(jnp.int32)
    out_spec = pl.BlockSpec((chip_rows, width), lambda p, b: (0, 0))
    anywhere = pl.BlockSpec(memory_space=pltpu.MemorySpace.HBM)
    return pl.pallas_call(
        functools.partial(main_kernel, tuple(copies), early, shards - early),
        out_shape=(
            jax.ShapeDtypeStruct((chip_rows, width), jnp.bfloat16),
            jax.ShapeDtypeStruct((chip_rows, width), jnp.float32),
        ),
        grid_spec=pltpu.PrefetchScalarGridSpec(
            num_scalar_prefetch=1,
            grid=(1,),
            in_specs=[anywhere] * (4 + len(pieces)),
            out_specs=(out_spec, out_spec),
            scratch_shapes=[
                pltpu.VMEM((shards, chip_rows, depth), jnp.bfloat16),
                pltpu.VMEM((shards, depth, 2 * width), jnp.bfloat16),
                pltpu.VMEM((chip_rows, 2 * width), jnp.float32),
                pltpu.VMEM(bias.shape, jnp.float32),
                pltpu.VMEM(table.shape, jnp.float32),
                pltpu.SemaphoreType.DMA((shards,)),
                pltpu.SemaphoreType.DMA((shards,)),
                pltpu.SemaphoreType.DMA((2,)),
            ],
        ),
        compiler_params=pltpu.CompilerParams(vmem_limit_bytes=MOST_VMEM - LEFT_VMEM),
        cost_estimate=pl.CostEstimate(
            flops=2 * (shards + early) * depth * chip_rows * width,
            bytes_accessed=2 * shards * depth * (chip_rows + width),
            transcendentals=0,
        ),
        name="project_main",
    )(facts, own_tokens, sibling_tokens, bias, table, *pieces)


class Blocks:
    def __init__(self, facts, hops, row_blocks, row_block):
        self.row_blocks = row_blocks
        per_chip = CORES * row_blocks
        chip = facts[1] // CORES
        here = facts[1] * row_blocks + row_block
        segment = facts[2 + here]
        self.diagonal = lax.rem(here, per_chip)
        self.entries, slot = [], jnp.int32(0)
        for hop in range(hops):
            for local in range(per_chip):
                block = (chip - hop) * per_chip + local
                seen = facts[2 + jnp.maximum(block, 0)]
                allowed = (block >= 0) & (block < here) & ((seen == 0) | (seen == segment))
                self.entries.append((hop, local, allowed, slot))
                slot = slot + jnp.where(allowed, 1, 0)
        self.odd = lax.rem(slot, 2) == 1
        self.free_slot = slot
        self.chunks = (slot + 2) // 2

    def place(self, local, source_core):
        core = local // self.row_blocks
        slot = jnp.where(core == source_core, 0, self.row_blocks)
        slot = slot + lax.rem(local, self.row_blocks)
        return pl.ds(pl.multiple_of(slot * BLK, BLK), BLK)

    def gather(self, refs, source_core, chosen_ref):
        def slot_rows(slot):
            return pl.ds(pl.multiple_of(slot * BLK, BLK), BLK)

        for hop, local, allowed, slot in self.entries:

            @pl.when(allowed)
            def _(hop=hop, local=local, slot=slot):
                chosen_ref[slot_rows(slot), :] = refs[hop][
                    self.place(jnp.int32(local), source_core), :
                ]

        @pl.when(jnp.logical_not(self.odd))
        def _():
            chosen_ref[slot_rows(self.free_slot), :] = jnp.zeros(
                (BLK, chosen_ref.shape[1]), chosen_ref.dtype
            )

        chosen_ref[slot_rows(2 * self.chunks - 1), :] = refs[0][
            self.place(self.diagonal, source_core), :
        ]


def chunk_rows(chunk):
    return pl.ds(pl.multiple_of(chunk * CHUNK, CHUNK), CHUNK)


def find_scores(blocks, group, q_ref, key_ref, score_ref, peak_ref):
    factor = math.log2(math.e) / math.sqrt(HEAD_SIZE)

    def parts_of(chunk):
        keys = key_ref[chunk_rows(chunk), :]
        for first in range(0, group, PART):
            heads = [
                q_ref[:, h * HEAD_SIZE : (h + 1) * HEAD_SIZE] for h in range(first, first + PART)
            ]
            found = lax.dot_general(
                jnp.concatenate(heads, axis=0),
                keys,
                (((1,), (1,)), ((), ())),
                preferred_element_type=jnp.float32,
            )
            yield slice(first * BLK, (first + PART) * BLK), found * factor

    last = blocks.chunks - 1
    column = lax.broadcasted_iota(jnp.int32, (PART * BLK, CHUNK), 1)
    row = lax.broadcasted_iota(jnp.int32, (PART * BLK, CHUNK), 0) % BLK
    first_column = jnp.where(blocks.odd, 0, BLK)
    for rows, found in parts_of(last):
        found = jnp.where((column >= first_column) & (column - BLK <= row), found, MASKED)
        score_ref[last, rows, :] = found
        peak_ref[rows, :] = jnp.maximum(found[:, :BLK], found[:, BLK:])

    @pl.loop(0, last)
    def _(chunk):
        for rows, found in parts_of(chunk):
            score_ref[chunk, rows, :] = found
            peak_ref[rows, :] = jnp.maximum(
                peak_ref[rows, :], jnp.maximum(found[:, :BLK], found[:, BLK:])
            )

    peak_ref[...] = jnp.broadcast_to(
        jnp.max(peak_ref[...], axis=1, keepdims=True), peak_ref.shape
    )


def score_kernel(hops, row_blocks, group, facts, q_ref, *refs):
    k_refs = refs[:hops]
    probs_ref, inverse_ref, key_ref, score_ref, peak_ref, total_ref = refs[hops:]
    blocks = Blocks(facts, hops, row_blocks, pl.program_id(0))
    head = pl.program_id(1)
    lanes = pl.ds(pl.multiple_of(head * HEAD_SIZE, HEAD_SIZE), HEAD_SIZE)

    @pl.when(head == 0)
    def _():
        blocks.gather(k_refs, facts[0], key_ref)

    find_scores(blocks, group, q_ref, key_ref.at[:, lanes], score_ref, peak_ref)
    total_ref[...] = jnp.zeros_like(total_ref)

    @pl.loop(0, blocks.chunks)
    def _(chunk):
        peak, total = peak_ref[...], total_ref[...]
        for column in range(0, CHUNK, BLK):
            probs = jnp.exp2(score_ref[chunk, :, column : column + BLK] - peak)
            probs_ref[0, chunk, :, column : column + BLK] = probs.astype(jnp.bfloat16)
            total = total + probs
        total_ref[...] = total

    inverse_ref[0] = jnp.broadcast_to(
        1.0 / jnp.sum(total_ref[...], axis=1, keepdims=True), total_ref.shape
    )


def attend_kernel(hops, row_blocks, group, heads, facts, q_ref, probs_hbm, inverse_ref, *refs):
    near_values, far_keys, far_values = (refs[at * hops : (at + 1) * hops] for at in range(3))
    out_ref, key_ref, value_ref, score_ref, peak_ref, total_ref, acc_ref = refs[3 * hops : -2]
    held_ref, sems = refs[-2:]
    row_block, head = pl.program_id(0), pl.program_id(1)
    blocks = Blocks(facts, hops, row_blocks, row_block)
    lanes = pl.ds(pl.multiple_of(lax.rem(head, heads) * HEAD_SIZE, HEAD_SIZE), HEAD_SIZE)

    def fetch(rows_of, at, chunk):
        return pltpu.make_async_copy(
            probs_hbm.at[rows_of * heads + at, chunk], held_ref.at[at, chunk], sems.at[at, chunk]
        )

    def fetch_row_block(rows_of):
        for at in range(heads):

            @pl.loop(0, Blocks(facts, hops, row_blocks, rows_of).chunks)
            def _(chunk):
                fetch(rows_of, at, chunk).start()

    @pl.when((row_block == 0) & (head == 0))
    def _():
        fetch_row_block(row_block)

    @pl.when((row_block + 1 < row_blocks) & (head == heads))
    def _():
        fetch_row_block(lax.rem(row_block + 1, row_blocks))

    @pl.when(head == 0)
    def _():
        blocks.gather(near_values, facts[0], value_ref)

    @pl.when(head == heads)
    def _():
        blocks.gather(far_keys, 1 - facts[0], key_ref)
        blocks.gather(far_values, 1 - facts[0], value_ref)

    def store(mixed):
        mixed = mixed.astype(out_ref.dtype)
        for h in range(group):
            out_ref[:, h * HEAD_SIZE : (h + 1) * HEAD_SIZE] = mixed[h * BLK : (h + 1) * BLK]

    acc_ref[...] = jnp.zeros_like(acc_ref)

    @pl.when(head < heads)
    def _():
        @pl.loop(0, blocks.chunks)
        def _(chunk):
            fetch(row_block, head, chunk).wait()
            acc_ref[...] += jnp.dot(
                held_ref[head, chunk],
                value_ref[chunk_rows(chunk), lanes],
                preferred_element_type=jnp.float32,
            )

        store(acc_ref[...] * inverse_ref[0])

    @pl.when(head >= heads)
    def _():
        find_scores(blocks, group, q_ref, key_ref.at[:, lanes], score_ref, peak_ref)
        total_ref[...] = jnp.zeros_like(total_ref)

        @pl.loop(0, blocks.chunks)
        def _(chunk):
            values = value_ref[chunk_rows(chunk), lanes]
            for first in range(0, group * BLK, PART * BLK):
                rows = slice(first, first + PART * BLK)
                peak, total, halves = peak_ref[rows, :], total_ref[rows, :], []
                for column in range(0, CHUNK, BLK):
                    found = score_ref[chunk, rows, column : column + BLK]
                    probs = jnp.exp2(found - peak)
                    halves.append(probs.astype(jnp.bfloat16))
                    total = total + probs
                total_ref[rows, :] = total
                acc_ref[rows, :] += jnp.dot(
                    jnp.concatenate(halves, axis=1), values, preferred_element_type=jnp.float32
                )

        store(acc_ref[...] / jnp.sum(total_ref[...], axis=1, keepdims=True))


class Attention:
    def __init__(self, facts, queries, hops):
        self.facts, self.queries, self.hops = facts, queries, hops
        number_of_rows, query_width = queries.shape
        self.group = query_width // HEAD_SIZE // KEY_VALUE_HEADS
        self.heads = heads = KEY_VALUE_HEADS // CORES
        self.row_blocks = number_of_rows // BLK
        self.stacked = self.group * BLK
        self.chunks = hops * CORES * self.row_blocks * BLK // CHUNK
        self.q_spec = pl.BlockSpec(
            (BLK, self.group * HEAD_SIZE),
            lambda r, l, f: (r, jnp.where(l < heads, f[0], 1 - f[0]) * heads + lax.rem(l, heads)),
        )
        self.kv_spec = pl.BlockSpec(
            (CORES * number_of_rows, heads * HEAD_SIZE), lambda r, l, f: (0, 0)
        )
        self.chosen = pltpu.VMEM((self.chunks * CHUNK, heads * HEAD_SIZE), jnp.bfloat16)
        self.scores = pltpu.VMEM((self.chunks, self.stacked, CHUNK), jnp.float32)
        self.tall = pltpu.VMEM((self.stacked, BLK), jnp.float32)
        count = heads * self.row_blocks
        self.probs = jax.ShapeDtypeStruct(
            (count, self.chunks, self.stacked, CHUNK), jnp.bfloat16
        )
        self.inverse = jax.ShapeDtypeStruct((count, self.stacked, BLK), jnp.float32)
        self.pairs = count * self.stacked * self.chunks * CHUNK // 2

    def call(self, kernel, heads, left, out_shape, in_specs, out_specs, scratch, operands):
        return pl.pallas_call(
            kernel,
            out_shape=out_shape,
            grid_spec=pltpu.PrefetchScalarGridSpec(
                num_scalar_prefetch=1,
                grid=(self.row_blocks, heads),
                in_specs=[self.q_spec] + in_specs,
                out_specs=out_specs,
                scratch_shapes=scratch,
            ),
            compiler_params=pltpu.CompilerParams(vmem_limit_bytes=MOST_VMEM - left),
            cost_estimate=pl.CostEstimate(
                flops=4 * self.pairs * HEAD_SIZE,
                bytes_accessed=2 * self.queries.size,
                transcendentals=self.pairs,
            ),
        )(self.facts, self.queries, *operands)

    def score(self, keys):
        heads, rows = self.heads, self.row_blocks
        return self.call(
            functools.partial(score_kernel, self.hops, rows, self.group),
            heads,
            LEFT_VMEM,
            (self.probs, self.inverse),
            [self.kv_spec] * self.hops,
            (
                pl.BlockSpec((1, *self.probs.shape[1:]), lambda r, l, f: (r * heads + l, 0, 0, 0)),
                pl.BlockSpec((1, self.stacked, BLK), lambda r, l, f: (r * heads + l, 0, 0)),
            ),
            [self.chosen, self.scores, self.tall, self.tall],
            keys,
        )

    def attend(self, probs, inverse, values, far_keys, far_values):
        heads = self.heads
        return self.call(
            functools.partial(attend_kernel, self.hops, self.row_blocks, self.group, heads),
            KEY_VALUE_HEADS,
            21 << 18,
            jax.ShapeDtypeStruct(self.queries.shape, self.queries.dtype),
            [
                pl.BlockSpec(memory_space=pltpu.MemorySpace.HBM),
                pl.BlockSpec(
                    (1, self.stacked, BLK),
                    lambda r, l, f: (r * heads + jnp.minimum(l, heads - 1), 0, 0),
                ),
            ]
            + [self.kv_spec] * (3 * self.hops),
            self.q_spec,
            [
                self.chosen,
                self.chosen,
                self.scores,
                self.tall,
                self.tall,
                self.tall,
                pltpu.VMEM((heads, *self.probs.shape[1:]), jnp.bfloat16),
                pltpu.SemaphoreType.DMA((heads, self.chunks)),
            ],
            [probs, inverse, *values, *far_keys, *far_values],
        )


def layer(
    hidden_in,
    queries,
    key_projection_weight,
    value_projection_weight,
    key_projection_bias,
    value_projection_bias,
    block_segments,
):
    own_tokens = hidden_in[0]
    number_of_rows = own_tokens.shape[0]
    depth, kv_width = key_projection_weight.shape
    dp_size, ctx_size = lax.axis_size("dp"), lax.axis_size("ctx")
    chips = ctx_size // CORES
    my_index = lax.axis_index("ctx")
    core, chip = my_index % CORES, my_index // CORES
    plane = chip % 2
    half_width = kv_width // CORES
    ring = ring_order(dp_size)
    dp_index = lax.axis_index("dp")
    my_spot = jnp.where(dp_index % 2 == 0, dp_index // 2, dp_size - (dp_index + 1) // 2)

    def to_sibling(x):
        return lax.ppermute(x, "ctx", [(i, i ^ 1) for i in range(ctx_size)])

    def to_plane(x):
        return lax.ppermute(x, "ctx", [(i, i ^ CORES) for i in range(ctx_size)])

    def to_next_chip(x):
        return lax.ppermute(x, "ctx", [(i, i + CORES) for i in range(ctx_size - CORES)])

    def along_ring(x, step):
        return lax.ppermute(
            x, "dp", [(ring[i], ring[(i + step) % dp_size]) for i in range(dp_size)]
        )

    key_weight = lax.dynamic_slice_in_dim(key_projection_weight, core * half_width, half_width, 1)
    value_weight = lax.dynamic_slice_in_dim(
        value_projection_weight, core * half_width, half_width, 1
    )
    strip = depth // 2
    part = strip // 2
    key_strip = lax.dynamic_slice_in_dim(key_weight, plane * strip, strip, 0)
    sibling_tokens = to_sibling(own_tokens)

    def source_at(distance):
        spot = (my_spot + distance + dp_size) % dp_size
        return jnp.where(spot < dp_size // 2, 2 * spot, 2 * (dp_size - spot) - 1)

    half_ring = dp_size // 2

    arange = jnp.arange(number_of_rows, dtype=jnp.int32)
    positions = jnp.concatenate(
        [my_index * number_of_rows + arange, (my_index ^ 1) * number_of_rows + arange]
    )
    key_bias = lax.dynamic_slice_in_dim(key_projection_bias, core * half_width, half_width, 0)
    value_bias = lax.dynamic_slice_in_dim(value_projection_bias, core * half_width, half_width, 0)

    key_arrived, value_arrived = {}, {}
    travelling = {1: key_strip, -1: key_strip}
    for hop in range(1, half_ring + 1):
        for step in (1, -1):
            piece = travelling[step]
            if hop == half_ring:
                first_row = 0 if step == 1 else part
                piece = piece[first_row : first_row + part]
            piece = along_ring(piece, step)
            other = to_plane(piece)
            travelling[step] = piece
            key_arrived[hop, step] = (piece, other)

    travelling = {
        (side, step): value_weight[side * strip : (side + 1) * strip]
        for side in range(2)
        for step in (1, -1)
    }
    for hop in range(1, half_ring + 1):
        for side in range(2):
            for step in (1, -1):
                if hop == half_ring and step != (1, -1)[side]:
                    continue
                piece = along_ring(travelling[side, step], step)
                travelling[side, step] = piece
                value_arrived[hop, step, side] = piece

    early = half_ring - 2
    distances = list(range(-early, early + 1)) + [-half_ring + 1, half_ring - 1, half_ring]
    pieces = [key_weight, value_weight]
    copies = [(0, early, -1, 0, 0), (1, early, -1, 0, half_width)]
    for hop in range(1, half_ring + 1):
        for step in (1, -1):
            shard = distances.index(half_ring if hop == half_ring else -step * hop)
            offset = part if hop == half_ring and step == -1 else 0
            for side, piece in enumerate(key_arrived[hop, step]):
                copies.append((len(pieces), shard, side, offset, 0))
                pieces.append(piece)
            if hop <= early:
                for side in range(2):
                    copies.append((len(pieces), shard, -1, side * strip, half_width))
                    pieces.append(value_arrived[hop, step, side])
    table = rope_tables(positions)
    key_rows, value_proj = project_main(
        own_tokens,
        sibling_tokens,
        jnp.concatenate([key_bias, value_bias])[None],
        table,
        pieces,
        copies,
        [source_at(distance) for distance in distances],
        2 * early + 1,
        plane,
    )

    def picked(source):
        return jnp.concatenate(
            [
                lax.dynamic_slice_in_dim(tokens, source * depth, depth, 1)
                for tokens in (own_tokens, sibling_tokens)
            ],
            axis=0,
        )

    def late_product(columns, side, piece):
        return jnp.dot(
            columns[:, side * strip : (side + 1) * strip],
            piece,
            preferred_element_type=jnp.float32,
        )

    columns = {hop: picked(source_at(hop)) for hop in distances[-3:]}
    for step in (1, -1):
        for side in range(2):
            hop = half_ring - 1
            value_proj += late_product(columns[-step * hop], side, value_arrived[hop, step, side])
    for side, step in enumerate((1, -1)):
        value_proj += late_product(columns[half_ring], side, value_arrived[half_ring, step, side])
    value_rows = value_proj.astype(jnp.bfloat16)

    keys, values = [key_rows], [value_rows]
    for hop in range(1, chips):
        keys.append(to_next_chip(keys[-1]))
        values.append(to_next_chip(values[-1]))
    sibling_keys = []
    for hop, rows in enumerate(keys):
        sibling_keys.append(to_sibling(rows))
    sibling_values = [to_sibling(x) for x in values]

    facts = jnp.concatenate([jnp.stack([core, my_index]), block_segments[0]])
    attention = Attention(facts, queries[0], chips)
    probs, inverse = attention.score(keys)
    attended = attention.attend(probs, inverse, values, sibling_keys, sibling_values)
    return attended[None]


def solution(mesh):
    placed = (
        P("dp", "ctx", None),
        P("dp", "ctx", None),
        P("dp", None),
        P("dp", None),
        P(),
        P(),
        P("dp", None),
    )
    return jax.shard_map(
        layer, mesh=mesh, in_specs=placed, out_specs=P("dp", "ctx", None), check_vma=False
    )
```

```python
import functools
import math

import jax
import jax.numpy as jnp
from jax import lax
from jax.experimental import pallas as pl
from jax.experimental.pallas import tpu as pltpu
from jax.sharding import PartitionSpec as P


HEAD_SIZE = 128
KEY_VALUE_HEADS = 4
BLK = 128
MASKED = -1e30
CORES = 2
CHUNK = 2 * BLK
PART = 2
MOST_VMEM = 67043328
LEFT_VMEM = (4 << 20) - (1 << 16)

rope_base = 1000000.0


def ring_order(count):
    return list(range(0, count, 2)) + list(range(count - 1, 0, -2))


def rope_tables(token_positions):
    half_dim = HEAD_SIZE // 2
    frequency = rope_base ** (
        -(jnp.arange(half_dim, dtype=jnp.float32) * 2.0 / HEAD_SIZE)
    )
    angles = token_positions.astype(jnp.float32)[:, None] * frequency[None, :]
    cos_part, sine_part = jnp.cos(angles), jnp.sin(angles)
    return jnp.concatenate([cos_part, cos_part, -sine_part, sine_part], axis=1)


def main_kernel(copies, early, late, facts, own_ref, sibling_ref, bias_hbm, table_hbm, *refs):
    piece_refs = refs[:-10]
    key_ref, value_ref, token_ref, weight_ref, acc_ref = refs[-10:-5]
    bias_ref, table_ref, token_sems, weight_sems, other_sems = refs[-5:]
    number_of_rows, depth = own_ref.shape[0], weight_ref.shape[1]
    width = weight_ref.shape[2] // 2
    strip = depth // 2
    others = [
        pltpu.make_async_copy(bias_hbm, bias_ref, other_sems.at[0]),
        pltpu.make_async_copy(table_hbm, table_ref, other_sems.at[1]),
    ]
    for shard in range(early + late):
        for operand, at, side, offset, lane in copies:
            if at != shard:
                continue
            row = offset
            if side >= 0:
                plane = facts[0] if side == 0 else 1 - facts[0]
                row = pl.multiple_of(plane * strip + offset, strip // 2)
            pltpu.make_async_copy(
                piece_refs[operand],
                weight_ref.at[
                    shard, pl.ds(row, piece_refs[operand].shape[0]), pl.ds(lane, width)
                ],
                weight_sems.at[shard],
            ).start()
        columns = pl.ds(pl.multiple_of(facts[1 + shard] * depth, depth), depth)
        for half, tokens_ref in enumerate((own_ref, sibling_ref)):
            pltpu.make_async_copy(
                tokens_ref.at[:, columns],
                token_ref.at[shard, pl.ds(half * number_of_rows, number_of_rows), :],
                token_sems.at[shard],
            ).start()
    for copy in others:
        copy.start()
    acc_ref[...] = jnp.zeros_like(acc_ref)

    def add_shard(shard, lanes):
        strips = weight_ref.at[shard, :, pl.ds(0, lanes)]
        pltpu.make_async_copy(strips, strips, weight_sems.at[shard]).wait()
        pltpu.make_async_copy(
            token_ref.at[shard], token_ref.at[shard], token_sems.at[shard]
        ).wait()
        acc_ref[:, :lanes] += jnp.dot(
            token_ref[shard], weight_ref[shard, :, :lanes], preferred_element_type=jnp.float32
        )

    @pl.loop(0, early)
    def _(shard):
        add_shard(shard, 2 * width)

    for copy in others:
        copy.wait()
    value_ref[...] = acc_ref[:, width:] + bias_ref[:, width:]

    @pl.loop(early, early + late)
    def _(shard):
        add_shard(shard, width)

    for first in range(0, width, HEAD_SIZE):
        lanes = slice(first, first + HEAD_SIZE)
        head = acc_ref[:, lanes] + bias_ref[:, lanes]
        turned = head * table_ref[:, :HEAD_SIZE]
        turned += pltpu.roll(head, HEAD_SIZE // 2, 1) * table_ref[:, HEAD_SIZE:]
        key_ref[:, lanes] = turned.astype(key_ref.dtype)


def project_main(own_tokens, sibling_tokens, bias, table, pieces, copies, sources, early, plane):
    shards = len(sources)
    depth = own_tokens.shape[1] // shards
    chip_rows = CORES * own_tokens.shape[0]
    width = pieces[0].shape[1]
    facts = jnp.stack([plane, *sources]).astype(jnp.int32)
    out_spec = pl.BlockSpec((chip_rows, width), lambda p, b: (0, 0))
    anywhere = pl.BlockSpec(memory_space=pltpu.MemorySpace.HBM)
    return pl.pallas_call(
        functools.partial(main_kernel, tuple(copies), early, shards - early),
        out_shape=(
            jax.ShapeDtypeStruct((chip_rows, width), jnp.bfloat16),
            jax.ShapeDtypeStruct((chip_rows, width), jnp.float32),
        ),
        grid_spec=pltpu.PrefetchScalarGridSpec(
            num_scalar_prefetch=1,
            grid=(1,),
            in_specs=[anywhere] * (4 + len(pieces)),
            out_specs=(out_spec, out_spec),
            scratch_shapes=[
                pltpu.VMEM((shards, chip_rows, depth), jnp.bfloat16),
                pltpu.VMEM((shards, depth, 2 * width), jnp.bfloat16),
                pltpu.VMEM((chip_rows, 2 * width), jnp.float32),
                pltpu.VMEM(bias.shape, jnp.float32),
                pltpu.VMEM(table.shape, jnp.float32),
                pltpu.SemaphoreType.DMA((shards,)),
                pltpu.SemaphoreType.DMA((shards,)),
                pltpu.SemaphoreType.DMA((2,)),
            ],
        ),
        compiler_params=pltpu.CompilerParams(vmem_limit_bytes=MOST_VMEM - LEFT_VMEM),
        cost_estimate=pl.CostEstimate(
            flops=2 * (shards + early) * depth * chip_rows * width,
            bytes_accessed=2 * shards * depth * (chip_rows + width),
            transcendentals=0,
        ),
        name="project_main",
    )(facts, own_tokens, sibling_tokens, bias, table, *pieces)


class Blocks:
    def __init__(self, facts, hops, row_blocks, row_block):
        self.row_blocks = row_blocks
        per_chip = CORES * row_blocks
        chip = facts[1] // CORES
        here = facts[1] * row_blocks + row_block
        segment = facts[2 + here]
        self.diagonal = lax.rem(here, per_chip)
        self.entries, slot = [], jnp.int32(0)
        for hop in range(hops):
            for local in range(per_chip):
                block = (chip - hop) * per_chip + local
                seen = facts[2 + jnp.maximum(block, 0)]
                allowed = (block >= 0) & (block < here) & ((seen == 0) | (seen == segment))
                self.entries.append((hop, local, allowed, slot))
                slot = slot + jnp.where(allowed, 1, 0)
        self.odd = lax.rem(slot, 2) == 1
        self.free_slot = slot
        self.chunks = (slot + 2) // 2

    def place(self, local, source_core):
        core = local // self.row_blocks
        slot = jnp.where(core == source_core, 0, self.row_blocks)
        slot = slot + lax.rem(local, self.row_blocks)
        return pl.ds(pl.multiple_of(slot * BLK, BLK), BLK)

    def gather(self, refs, source_core, chosen_ref):
        def slot_rows(slot):
            return pl.ds(pl.multiple_of(slot * BLK, BLK), BLK)

        for hop, local, allowed, slot in self.entries:

            @pl.when(allowed)
            def _(hop=hop, local=local, slot=slot):
                chosen_ref[slot_rows(slot), :] = refs[hop][
                    self.place(jnp.int32(local), source_core), :
                ]

        @pl.when(jnp.logical_not(self.odd))
        def _():
            chosen_ref[slot_rows(self.free_slot), :] = jnp.zeros(
                (BLK, chosen_ref.shape[1]), chosen_ref.dtype
            )

        chosen_ref[slot_rows(2 * self.chunks - 1), :] = refs[0][
            self.place(self.diagonal, source_core), :
        ]


def chunk_rows(chunk):
    return pl.ds(pl.multiple_of(chunk * CHUNK, CHUNK), CHUNK)


def find_scores(blocks, group, q_ref, key_ref, score_ref, peak_ref):
    factor = math.log2(math.e) / math.sqrt(HEAD_SIZE)

    def parts_of(chunk):
        keys = key_ref[chunk_rows(chunk), :]
        for first in range(0, group, PART):
            heads = [
                q_ref[:, h * HEAD_SIZE : (h + 1) * HEAD_SIZE] for h in range(first, first + PART)
            ]
            found = lax.dot_general(
                jnp.concatenate(heads, axis=0),
                keys,
                (((1,), (1,)), ((), ())),
                preferred_element_type=jnp.float32,
            )
            yield slice(first * BLK, (first + PART) * BLK), found * factor

    last = blocks.chunks - 1
    column = lax.broadcasted_iota(jnp.int32, (PART * BLK, CHUNK), 1)
    row = lax.broadcasted_iota(jnp.int32, (PART * BLK, CHUNK), 0) % BLK
    first_column = jnp.where(blocks.odd, 0, BLK)
    for rows, found in parts_of(last):
        found = jnp.where((column >= first_column) & (column - BLK <= row), found, MASKED)
        score_ref[last, rows, :] = found
        peak_ref[rows, :] = jnp.maximum(found[:, :BLK], found[:, BLK:])

    @pl.loop(0, last)
    def _(chunk):
        for rows, found in parts_of(chunk):
            score_ref[chunk, rows, :] = found
            peak_ref[rows, :] = jnp.maximum(
                peak_ref[rows, :], jnp.maximum(found[:, :BLK], found[:, BLK:])
            )

    peak_ref[...] = jnp.broadcast_to(
        jnp.max(peak_ref[...], axis=1, keepdims=True), peak_ref.shape
    )


def attend_kernel(hops, row_blocks, group, heads, facts, q_ref, *refs):
    near, far = (refs[side * 2 * hops : (side + 1) * 2 * hops] for side in range(2))
    out_ref, key_ref, value_ref, score_ref, peak_ref, total_ref, acc_ref = refs[4 * hops :]
    blocks = Blocks(facts, hops, row_blocks, pl.program_id(0))
    head = pl.program_id(1)
    lanes = pl.ds(pl.multiple_of(lax.rem(head, heads) * HEAD_SIZE, HEAD_SIZE), HEAD_SIZE)

    for side, (half, core) in enumerate(((near, facts[0]), (far, 1 - facts[0]))):

        @pl.when(head == side * heads)
        def _(half=half, core=core):
            blocks.gather(half[:hops], core, key_ref)
            blocks.gather(half[hops:], core, value_ref)

    find_scores(blocks, group, q_ref, key_ref.at[:, lanes], score_ref, peak_ref)
    total_ref[...] = jnp.zeros_like(total_ref)
    acc_ref[...] = jnp.zeros_like(acc_ref)

    @pl.loop(0, blocks.chunks)
    def _(chunk):
        values = value_ref[chunk_rows(chunk), lanes]
        for first in range(0, group * BLK, PART * BLK):
            rows = slice(first, first + PART * BLK)
            peak, total, halves = peak_ref[rows, :], total_ref[rows, :], []
            for column in range(0, CHUNK, BLK):
                found = score_ref[chunk, rows, column : column + BLK]
                probs = jnp.exp2(found - peak)
                halves.append(probs.astype(jnp.bfloat16))
                total = total + probs
            total_ref[rows, :] = total
            acc_ref[rows, :] += jnp.dot(
                jnp.concatenate(halves, axis=1), values, preferred_element_type=jnp.float32
            )

    mixed = (acc_ref[...] / jnp.sum(total_ref[...], axis=1, keepdims=True)).astype(out_ref.dtype)
    for h in range(group):
        out_ref[:, h * HEAD_SIZE : (h + 1) * HEAD_SIZE] = mixed[h * BLK : (h + 1) * BLK]


def attend(facts, queries, near, far):
    hops = len(near) // 2
    number_of_rows, query_width = queries.shape
    group = query_width // HEAD_SIZE // KEY_VALUE_HEADS
    heads = KEY_VALUE_HEADS // CORES
    row_blocks = number_of_rows // BLK
    stacked = group * BLK
    chunks = hops * CORES * row_blocks * BLK // CHUNK
    q_spec = pl.BlockSpec(
        (BLK, group * HEAD_SIZE),
        lambda r, l, f: (r, jnp.where(l < heads, f[0], 1 - f[0]) * heads + lax.rem(l, heads)),
    )
    kv_spec = pl.BlockSpec((CORES * number_of_rows, heads * HEAD_SIZE), lambda r, l, f: (0, 0))
    chosen = pltpu.VMEM((chunks * CHUNK, heads * HEAD_SIZE), jnp.bfloat16)
    tall = pltpu.VMEM((stacked, BLK), jnp.float32)
    pairs = KEY_VALUE_HEADS * row_blocks * stacked * chunks * CHUNK // 2
    return pl.pallas_call(
        functools.partial(attend_kernel, hops, row_blocks, group, heads),
        out_shape=jax.ShapeDtypeStruct(queries.shape, queries.dtype),
        grid_spec=pltpu.PrefetchScalarGridSpec(
            num_scalar_prefetch=1,
            grid=(row_blocks, KEY_VALUE_HEADS),
            in_specs=[q_spec] + [kv_spec] * (4 * hops),
            out_specs=q_spec,
            scratch_shapes=[
                chosen,
                chosen,
                pltpu.VMEM((chunks, stacked, CHUNK), jnp.float32),
                tall,
                tall,
                tall,
            ],
        ),
        compiler_params=pltpu.CompilerParams(vmem_limit_bytes=MOST_VMEM - LEFT_VMEM),
        cost_estimate=pl.CostEstimate(
            flops=4 * pairs * HEAD_SIZE,
            bytes_accessed=4 * queries.size,
            transcendentals=pairs,
        ),
        name="attend",
    )(facts, queries, *near, *far)


def layer(
    hidden_in,
    queries,
    key_projection_weight,
    value_projection_weight,
    key_projection_bias,
    value_projection_bias,
    block_segments,
):
    own_tokens = hidden_in[0]
    number_of_rows = own_tokens.shape[0]
    depth, kv_width = key_projection_weight.shape
    dp_size, ctx_size = lax.axis_size("dp"), lax.axis_size("ctx")
    chips = ctx_size // CORES
    my_index = lax.axis_index("ctx")
    core, chip = my_index % CORES, my_index // CORES
    plane = chip % 2
    half_width = kv_width // CORES
    ring = ring_order(dp_size)
    dp_index = lax.axis_index("dp")
    my_spot = jnp.where(dp_index % 2 == 0, dp_index // 2, dp_size - (dp_index + 1) // 2)

    def to_sibling(x):
        return lax.ppermute(x, "ctx", [(i, i ^ 1) for i in range(ctx_size)])

    def to_plane(x):
        return lax.ppermute(x, "ctx", [(i, i ^ CORES) for i in range(ctx_size)])

    def to_next_chip(x):
        return lax.ppermute(x, "ctx", [(i, i + CORES) for i in range(ctx_size - CORES)])

    def along_ring(x, step):
        return lax.ppermute(
            x, "dp", [(ring[i], ring[(i + step) % dp_size]) for i in range(dp_size)]
        )

    key_weight = lax.dynamic_slice_in_dim(key_projection_weight, core * half_width, half_width, 1)
    value_weight = lax.dynamic_slice_in_dim(
        value_projection_weight, core * half_width, half_width, 1
    )
    strip = depth // 2
    part = strip // 2
    key_strip = lax.dynamic_slice_in_dim(key_weight, plane * strip, strip, 0)
    sibling_tokens = to_sibling(own_tokens)

    def source_at(distance):
        spot = (my_spot + distance + dp_size) % dp_size
        return jnp.where(spot < dp_size // 2, 2 * spot, 2 * (dp_size - spot) - 1)

    half_ring = dp_size // 2

    arange = jnp.arange(number_of_rows, dtype=jnp.int32)
    positions = jnp.concatenate(
        [my_index * number_of_rows + arange, (my_index ^ 1) * number_of_rows + arange]
    )
    key_bias = lax.dynamic_slice_in_dim(key_projection_bias, core * half_width, half_width, 0)
    value_bias = lax.dynamic_slice_in_dim(value_projection_bias, core * half_width, half_width, 0)

    key_arrived, value_arrived = {}, {}
    travelling = {1: key_strip, -1: key_strip}
    for hop in range(1, half_ring + 1):
        for step in (1, -1):
            piece = travelling[step]
            if hop == half_ring:
                first_row = 0 if step == 1 else part
                piece = piece[first_row : first_row + part]
            piece = along_ring(piece, step)
            other = to_plane(piece)
            travelling[step] = piece
            key_arrived[hop, step] = (piece, other)

    travelling = {
        (side, step): value_weight[side * strip : (side + 1) * strip]
        for side in range(2)
        for step in (1, -1)
    }
    for hop in range(1, half_ring + 1):
        for side in range(2):
            for step in (1, -1):
                if hop == half_ring and step != (1, -1)[side]:
                    continue
                piece = along_ring(travelling[side, step], step)
                travelling[side, step] = piece
                value_arrived[hop, step, side] = piece

    early = half_ring - 2
    distances = list(range(-early, early + 1)) + [-half_ring + 1, half_ring - 1, half_ring]
    pieces = [key_weight, value_weight]
    copies = [(0, early, -1, 0, 0), (1, early, -1, 0, half_width)]
    for hop in range(1, half_ring + 1):
        for step in (1, -1):
            shard = distances.index(half_ring if hop == half_ring else -step * hop)
            offset = part if hop == half_ring and step == -1 else 0
            for side, piece in enumerate(key_arrived[hop, step]):
                copies.append((len(pieces), shard, side, offset, 0))
                pieces.append(piece)
            if hop <= early:
                for side in range(2):
                    copies.append((len(pieces), shard, -1, side * strip, half_width))
                    pieces.append(value_arrived[hop, step, side])
    table = rope_tables(positions)
    key_rows, value_proj = project_main(
        own_tokens,
        sibling_tokens,
        jnp.concatenate([key_bias, value_bias])[None],
        table,
        pieces,
        copies,
        [source_at(distance) for distance in distances],
        2 * early + 1,
        plane,
    )

    def picked(source):
        return jnp.concatenate(
            [
                lax.dynamic_slice_in_dim(tokens, source * depth, depth, 1)
                for tokens in (own_tokens, sibling_tokens)
            ],
            axis=0,
        )

    def late_product(columns, side, piece):
        return jnp.dot(
            columns[:, side * strip : (side + 1) * strip],
            piece,
            preferred_element_type=jnp.float32,
        )

    columns = {hop: picked(source_at(hop)) for hop in distances[-3:]}
    for step in (1, -1):
        for side in range(2):
            hop = half_ring - 1
            value_proj += late_product(columns[-step * hop], side, value_arrived[hop, step, side])
    for side, step in enumerate((1, -1)):
        value_proj += late_product(columns[half_ring], side, value_arrived[half_ring, step, side])
    value_rows = value_proj.astype(jnp.bfloat16)

    keys, values = [key_rows], [value_rows]
    for hop in range(1, chips):
        keys.append(to_next_chip(keys[-1]))
        values.append(to_next_chip(values[-1]))
    sibling_keys = [to_sibling(x) for x in keys]
    sibling_values = [to_sibling(x) for x in values]

    facts = jnp.concatenate([jnp.stack([core, my_index]), block_segments[0]])
    attended = attend(
        facts, queries[0], [*keys, *values], [*sibling_keys, *sibling_values]
    )
    return attended[None]


def solution(mesh):
    placed = (
        P("dp", "ctx", None),
        P("dp", "ctx", None),
        P("dp", None),
        P("dp", None),
        P(),
        P(),
        P("dp", None),
    )
    return jax.shard_map(
        layer, mesh=mesh, in_specs=placed, out_specs=P("dp", "ctx", None), check_vma=False
    )
```
